512 devices in a mesh: panel: 2 (over z_hi), colat: 16 (over z_lo, x), lon: 16 (over y, core).
Axes of the slice: x: 4, y: 8, z: 8 (z_hi: 2, z_lo: 4; z = z_hi * 4 + z_lo), core: 2. Of those that a mesh axis runs over, the one named last changes fastest.
Arguments:
- fields_now: float32 [4, 2, 256, 512, 128], P(None, 'panel', 'colat', 'lon'), may hold values from -6 to 6
- diffusivity: float32 [2, 256, 512, 128], P('panel', 'colat', 'lon'), may hold values from 0.5 to 2
- viscosity: float32 [2, 256, 512, 128], P('panel', 'colat', 'lon'), may hold values from 0.5 to 2
- donor_row: int32 [2, 16, 16, 12], P('panel', 'colat', 'lon'), may hold values from 0 to 16
- donor_column: int32 [2, 16, 16, 12], P('panel', 'colat', 'lon'), may hold values from 0 to 32
- donor_offset: float32 [2, 16, 16, 2, 12], P('panel', 'colat', 'lon'), may hold values from 0 to 1
- rim_angle: float32 [2, 16, 16, 12], P('panel', 'colat', 'lon'), may hold values from -3.140625 to 3.140625
Outputs:
- advanced: float32 [4, 2, 256, 512, 128], P(None, 'panel', 'colat', 'lon')
The draws below stay inside these ranges and needn't reach their ends.
All inputs are finite; a program needn't handle non-finite values.
Results may differ from the reference program's by a relative error of at most 0.00002.
Values sent between devices are 32-bit elements; how exact they have to be, the bound alone decides.
A program may use at most 64 MiB of HBM per device.

```python
import math
import jax
import jax.numpy as jnp
from jax import lax

COLAT_DEV = 16
LON_DEV = 32
RADIAL = 128
COLAT_CELLS = 256
LON_CELLS = 512
ROW_SHARE = 8
SLOTS = 12
N_COLAT = 16
N_LON = 16


def set_ends(drawn, rng, low, top_value):
    place = [jax.random.randint(jax.random.fold_in(rng, axis), (), 0, length) for axis, length in enumerate(drawn.shape)]
    longest = drawn.shape.index(max(drawn.shape))
    next_to = place[:longest] + [(place[longest] + 1) % drawn.shape[longest]] + place[longest + 1:]
    return drawn.at[tuple(place)].set(low).at[tuple(next_to)].set(top_value)


def shard_levels(own_key, extent, cuts, smallest, top_value):
    loudness = 1.0
    for position, shards_of in cuts:
        draws = jax.random.uniform(jax.random.fold_in(jax.random.fold_in(own_key, 6), position), (shards_of,), jnp.float32, smallest / len(cuts), top_value / len(cuts))
        loudness = loudness * jnp.repeat(jnp.exp(draws), extent[position] // shards_of).reshape((-1,) + (1,) * (len(extent) - 1 - position))
    return loudness


def gaussian(rng, extent, scale, limit, pieces=(), kind=jnp.bfloat16):
    level = shard_levels(rng, extent, pieces, -0.22, 0.18) if pieces else 1.0
    values = jax.random.normal(rng, extent, jnp.float32) * scale * level
    return jnp.minimum(jnp.maximum(values, -limit), limit).astype(kind)


def setup_inputs(seed: int = 0) -> dict:
    splits = jax.random.split(jax.random.key(seed), 8)
    fields_now = gaussian(splits[0], (4, 2, COLAT_CELLS, LON_CELLS, RADIAL), 1.0, 6.0, ((1, 2), (2, 16), (3, 16)), jnp.float32)
    diffusivity = jnp.clip(jnp.exp(math.log(2.0) - 1.3862944 * jax.random.uniform(splits[1], (2, COLAT_CELLS, LON_CELLS, RADIAL), jnp.float32) ** shard_levels(splits[1], (2, COLAT_CELLS, LON_CELLS, RADIAL), ((0, 2), (1, 16), (2, 16)), -0.2, 0.2)), 0.5, 2.0)
    viscosity = jnp.clip(jnp.exp(math.log(2.0) - 1.3862944 * jax.random.uniform(splits[2], (2, COLAT_CELLS, LON_CELLS, RADIAL), jnp.float32) ** shard_levels(splits[2], (2, COLAT_CELLS, LON_CELLS, RADIAL), ((0, 2), (1, 16), (2, 16)), -0.2, 0.2)), 0.5, 2.0)
    donor_row = set_ends(jax.random.randint(splits[3], (2, N_COLAT, N_LON, SLOTS), 0, COLAT_DEV + 1), jax.random.fold_in(splits[3], 1), 0, COLAT_DEV).astype(jnp.int32)
    donor_column = set_ends(jax.random.randint(splits[4], (2, N_COLAT, N_LON, SLOTS), 0, LON_DEV + 1), jax.random.fold_in(splits[4], 1), 0, LON_DEV).astype(jnp.int32)
    donor_offset = jnp.clip(1.0 * jax.random.uniform(splits[5], (2, N_COLAT, N_LON, 2, SLOTS), jnp.float32) ** shard_levels(splits[5], (2, N_COLAT, N_LON, 2, SLOTS), ((0, 2), (1, 16), (2, 16)), -0.2, 0.2), 0.0, 1.0)
    rim_angle = jnp.clip(jax.random.uniform(splits[6], (2, N_COLAT, N_LON, SLOTS), jnp.float32, -3.140625, 3.140625), -3.140625, 3.140625)
    return dict(fields_now=fields_now, diffusivity=diffusivity, viscosity=viscosity, donor_row=donor_row, donor_column=donor_column, donor_offset=donor_offset, rim_angle=rim_angle)


TIME_STEP = 0.05
BUOYANCY = 1.0


def gradient(stencil):
    return (8.0 * (stencil[3] - stencil[1]) - (stencil[4] - stencil[0])) / 12.0


def curvature(stencil):
    return (16.0 * (stencil[3] + stencil[1]) - (stencil[4] + stencil[0]) - 30.0 * stencil[2]) / 12.0


def advance(padded, thermal, viscous):
    height = padded.shape[1] - 4
    breadth = padded.shape[2] - 4
    center = padded[:, 2:2 + height, 2:2 + breadth]
    radial_len = center.shape[3]
    radial_pad = jnp.pad(center, ((0, 0), (0, 0), (0, 0), (2, 2)))
    along_lat = [padded[:, offset:offset + height, 2:2 + breadth] for offset in range(5)]
    along_lon = [padded[:, 2:2 + height, offset:offset + breadth] for offset in range(5)]
    along_rad = [radial_pad[..., offset:offset + radial_len] for offset in range(5)]
    laplace = curvature(along_rad) + curvature(along_lat) + curvature(along_lon)
    transport = center[1:2] * gradient(along_rad) + center[2:3] * gradient(along_lat) + center[3:4] * gradient(along_lon)
    diffusion = jnp.stack([thermal, viscous, viscous, viscous])
    change = diffusion * laplace - transport
    change = change.at[1].add(BUOYANCY * center[0])
    return center + TIME_STEP * change


def panel_step(packed):
    fields, thermal, viscous = packed
    padded = jnp.pad(fields, ((0, 0), (2, 2), (2, 2), (0, 0)))
    return advance(padded, thermal, viscous)


def reference(fields_now, diffusivity, viscosity, donor_row, donor_column, donor_offset, rim_angle):
    fresh = lax.map(panel_step, (jnp.moveaxis(fields_now, 1, 0), diffusivity, viscosity))
    width = LON_CELLS + 2
    results = [fresh[0], fresh[1]]
    for donor in range(2):
        receiver = 1 - donor
        extended = jnp.pad(fresh[donor], ((0, 0), (1, 1), (1, 1), (0, 0)))
        flattened = extended.reshape(4, (COLAT_CELLS + 2) * width, RADIAL)
        row_start = (jnp.arange(N_COLAT, dtype=jnp.int32) * COLAT_DEV)[:, None, None]
        col_start = (jnp.arange(N_LON, dtype=jnp.int32) * LON_DEV)[None, :, None]
        anchor = ((row_start + donor_row[donor]) * width + col_start + donor_column[donor]).astype(jnp.int32)

        def corner(offset):
            picked = jnp.take(flattened, (anchor + offset).reshape(-1), axis=1)
            return picked.reshape(4, N_COLAT, N_LON, SLOTS, RADIAL)

        frac_row = donor_offset[donor][:, :, 0][None, :, :, :, None]
        frac_lon = donor_offset[donor][:, :, 1][None, :, :, :, None]
        blended = (1.0 - frac_row) * ((1.0 - frac_lon) * corner(0) + frac_lon * corner(1)) + frac_row * ((1.0 - frac_lon) * corner(width) + frac_lon * corner(width + 1))
        cosine = jnp.cos(rim_angle[donor])[..., None]
        sine_part = jnp.sin(rim_angle[donor])[..., None]
        turned_lat = cosine * blended[2] - sine_part * blended[3]
        turned_lon = sine_part * blended[2] + cosine * blended[3]
        blended = jnp.stack([blended[0], blended[1], turned_lat, turned_lon])
        row_full = jnp.transpose(blended[:, :, :, 0:ROW_SHARE], (0, 2, 1, 3, 4)).reshape(4, N_LON, 4 * LON_DEV, RADIAL)
        col_full = blended[:, :, :, ROW_SHARE:].reshape(4, N_COLAT, 4 * COLAT_DEV, RADIAL)
        target = results[receiver]
        col_blocks = col_full.reshape(4, N_COLAT, 4, COLAT_DEV, RADIAL)
        west_strip = jnp.stack([col_blocks[:, :, 0], col_blocks[:, :, 2]], axis=2)
        west_strip = jnp.transpose(west_strip, (0, 1, 3, 2, 4)).reshape(4, COLAT_CELLS, 2, RADIAL)
        east_strip = jnp.stack([col_blocks[:, :, 3], col_blocks[:, :, 1]], axis=2)
        east_strip = jnp.transpose(east_strip, (0, 1, 3, 2, 4)).reshape(4, COLAT_CELLS, 2, RADIAL)
        target = target.at[:, :, 0:2].set(west_strip)
        target = target.at[:, :, LON_CELLS - 2:].set(east_strip)
        row_blocks = row_full.reshape(4, N_LON, 4, LON_DEV, RADIAL)
        north_strip = jnp.stack([row_blocks[:, :, 0], row_blocks[:, :, 2]], axis=2)
        north_strip = jnp.transpose(north_strip, (0, 2, 1, 3, 4)).reshape(4, 2, LON_CELLS, RADIAL)
        south_strip = jnp.stack([row_blocks[:, :, 3], row_blocks[:, :, 1]], axis=2)
        south_strip = jnp.transpose(south_strip, (0, 2, 1, 3, 4)).reshape(4, 2, LON_CELLS, RADIAL)
        target = target.at[:, 0:2].set(north_strip)
        target = target.at[:, COLAT_CELLS - 2:].set(south_strip)
        results[receiver] = target
    return jnp.stack(results, axis=1)
```

```python
import jax
import jax.numpy as jnp
from jax import lax
from jax.sharding import PartitionSpec as P
from jax.experimental import pallas as pl
from jax.experimental.pallas import tpu as pltpu

MESH = pl.DeviceIdType.MESH

TIME_STEP = 0.05
BUOYANCY = 1.0


def with_halo(x, sides, width):
    for axis, dim in sides:
        count, length = (lax.axis_size(axis), x.shape[dim])
        up = [(i, (i + 1) % count) for i in range(count - 1)]
        down = [(j, i) for i, j in up]
        last = lax.slice_in_dim(x, length - width, length, axis=dim)
        leading = lax.slice_in_dim(x, 0, width, axis=dim)
        before = lax.ppermute(last, axis, up)
        after = lax.ppermute(leading, axis, down)
        x = jnp.concatenate([before, x, after], axis=dim)
    return x


def swapped(block, axis, stride):
    count = lax.axis_size(axis)
    route = []
    for low in range(count):
        high = low | 1 << stride
        if high != low and high < count:
            route += [(low, high), (high, low)]
    return lax.ppermute(block, axis, route)


def rim_kernel(row_ref, col_ref, row_out, col_out, send_sem, row_sem, col_sem):
    panel = lax.axis_index("panel")
    colat = lax.axis_index("colat")
    lon = lax.axis_index("lon")
    colat_count = lax.axis_size("colat")
    lon_count = lax.axis_size("lon")
    row_types = row_out.shape[0] // 2
    col_types = col_out.shape[0] // 2
    other = 1 - panel

    def route(share, per_type, count):
        kind = share // per_type
        edge = (kind % 2) * (count - 1)
        slot = (kind // 2) * per_type + share % per_type
        return edge, slot

    row_edge, row_slot = route(colat, row_types, colat_count)
    col_edge, col_slot = route(lon, col_types, lon_count)
    row_dest = (other, row_edge, lon)
    col_dest = (other, colat, col_edge)
    at_row_edge = jnp.logical_or(colat == 0, colat == colat_count - 1)
    at_col_edge = jnp.logical_or(lon == 0, lon == lon_count - 1)
    parity_row = (colat // (colat_count - 1)).astype(jnp.int32)
    parity_col = (lon // (lon_count - 1)).astype(jnp.int32)

    def row_sender(slot):
        kind = 2 * (slot // row_types) + parity_row
        return (other, kind * row_types + slot % row_types, lon)

    def col_sender(slot):
        kind = 2 * (slot // col_types) + parity_col
        return (other, colat, kind * col_types + slot % col_types)

    barrier = pltpu.get_barrier_semaphore()
    pl.semaphore_signal(barrier, 1, device_id=row_dest, device_id_type=MESH)
    pl.semaphore_signal(barrier, 1, device_id=col_dest, device_id_type=MESH)

    @pl.when(at_row_edge)
    def _():
        for slot in range(2 * row_types):
            pl.semaphore_signal(barrier, 1, device_id=row_sender(slot), device_id_type=MESH)

    @pl.when(at_col_edge)
    def _():
        for slot in range(2 * col_types):
            pl.semaphore_signal(barrier, 1, device_id=col_sender(slot), device_id_type=MESH)

    expected = (
        2
        + at_row_edge.astype(jnp.int32) * (2 * row_types)
        + at_col_edge.astype(jnp.int32) * (2 * col_types)
    )
    pl.semaphore_wait(barrier, expected)

    row_copy = pltpu.make_async_remote_copy(
        row_ref, row_out.at[row_slot], send_sem.at[0], row_sem.at[row_slot],
        device_id=row_dest, device_id_type=MESH,
    )
    col_copy = pltpu.make_async_remote_copy(
        col_ref, col_out.at[col_slot], send_sem.at[1], col_sem.at[col_slot],
        device_id=col_dest, device_id_type=MESH,
    )
    row_copy.start()
    col_copy.start()
    row_copy.wait_send()
    col_copy.wait_send()

    @pl.when(at_row_edge)
    def _():
        for slot in range(2 * row_types):
            pltpu.make_async_remote_copy(
                row_ref, row_out.at[slot], send_sem.at[0], row_sem.at[slot],
                device_id=row_sender(slot), device_id_type=MESH,
            ).wait_recv()

    @pl.when(at_col_edge)
    def _():
        for slot in range(2 * col_types):
            pltpu.make_async_remote_copy(
                col_ref, col_out.at[slot], send_sem.at[1], col_sem.at[slot],
                device_id=col_sender(slot), device_id_type=MESH,
            ).wait_recv()


def rim_exchange(rows, cols):
    colat_count = lax.axis_size("colat")
    lon_count = lax.axis_size("lon")
    row_types = colat_count // 4
    col_types = lon_count // 4
    vmem = pl.BlockSpec(memory_space=pltpu.VMEM)
    return pl.pallas_call(
        rim_kernel,
        out_shape=(
            jax.ShapeDtypeStruct((2 * row_types,) + rows.shape, rows.dtype),
            jax.ShapeDtypeStruct((2 * col_types,) + cols.shape, cols.dtype),
        ),
        in_specs=[vmem, vmem],
        out_specs=(vmem, vmem),
        scratch_shapes=[
            pltpu.SemaphoreType.DMA((2,)),
            pltpu.SemaphoreType.DMA((2 * row_types,)),
            pltpu.SemaphoreType.DMA((2 * col_types,)),
        ],
        compiler_params=pltpu.CompilerParams(collective_id=0, has_side_effects=True),
    )(rows, cols)


def gradient(stencil):
    return (8.0 * (stencil[3] - stencil[1]) - (stencil[4] - stencil[0])) / 12.0


def curvature(stencil):
    return (16.0 * (stencil[3] + stencil[1]) - (stencil[4] + stencil[0]) - 30.0 * stencil[2]) / 12.0


def advance(padded, thermal, viscous):
    height = padded.shape[1] - 4
    breadth = padded.shape[2] - 4
    center = padded[:, 2 : 2 + height, 2 : 2 + breadth]
    radial_len = center.shape[3]
    radial_pad = jnp.pad(center, ((0, 0), (0, 0), (0, 0), (2, 2)))
    along_lat = [padded[:, offset : offset + height, 2 : 2 + breadth] for offset in range(5)]
    along_lon = [padded[:, 2 : 2 + height, offset : offset + breadth] for offset in range(5)]
    along_rad = [radial_pad[..., offset : offset + radial_len] for offset in range(5)]
    laplace = curvature(along_rad) + curvature(along_lat) + curvature(along_lon)
    transport = (
        center[1:2] * gradient(along_rad)
        + center[2:3] * gradient(along_lat)
        + center[3:4] * gradient(along_lon)
    )
    diffusion = jnp.stack([thermal, viscous, viscous, viscous])
    change = diffusion * laplace - transport
    change = change.at[1].add(BUOYANCY * center[0])
    return center + TIME_STEP * change


def local(fields_now, diffusivity, viscosity, donor_row, donor_column, donor_offset, rim_angle):
    fields = fields_now[:, 0]
    thermal = diffusivity[0]
    viscous = viscosity[0]
    height = fields.shape[1]
    breadth = fields.shape[2]
    radial_len = fields.shape[3]
    colat_pos = lax.axis_index("colat")
    lon_pos = lax.axis_index("lon")
    colat_count = lax.axis_size("colat")
    lon_count = lax.axis_size("lon")
    row_share = 4 * breadth // colat_count
    padded = with_halo(fields, (("colat", 1), ("lon", 2)), 2)
    fresh = advance(padded, thermal, viscous)
    extended = with_halo(fresh, (("colat", 1), ("lon", 2)), 1)
    width = breadth + 2
    flattened = extended.reshape(4, (height + 2) * width, radial_len)
    anchor = donor_row.reshape(-1) * width + donor_column.reshape(-1)

    def corner(offset):
        return jnp.take(flattened, anchor + offset, axis=1)

    frac_row = donor_offset[0, 0, 0, 0][None, :, None]
    frac_lon = donor_offset[0, 0, 0, 1][None, :, None]
    blended = (1.0 - frac_row) * (
        (1.0 - frac_lon) * corner(0) + frac_lon * corner(1)
    ) + frac_row * ((1.0 - frac_lon) * corner(width) + frac_lon * corner(width + 1))
    angles = rim_angle.reshape(-1)
    cosine = jnp.cos(angles)[:, None]
    sine_part = jnp.sin(angles)[:, None]
    turned_lat = cosine * blended[2] - sine_part * blended[3]
    turned_lon = sine_part * blended[2] + cosine * blended[3]
    blended = jnp.stack([blended[0], blended[1], turned_lat, turned_lon])
    row_buf, col_buf = rim_exchange(blended[:, 0:row_share], blended[:, row_share:])
    col_share = blended.shape[1] - row_share
    col_strip = col_buf.reshape(2, col_buf.shape[0] // 2, 4, col_share, radial_len)
    col_strip = jnp.transpose(col_strip, (2, 0, 1, 3, 4)).reshape(4, 2, height, radial_len)
    west_strip = jnp.transpose(col_strip, (0, 2, 1, 3))
    east_strip = jnp.stack([col_strip[:, 1], col_strip[:, 0]], axis=2)
    fresh = fresh.at[:, :, 0:2].set(jnp.where(lon_pos == 0, west_strip, fresh[:, :, 0:2]))
    fresh = fresh.at[:, :, breadth - 2 :].set(
        jnp.where(lon_pos == lon_count - 1, east_strip, fresh[:, :, breadth - 2 :])
    )
    row_strip = row_buf.reshape(2, row_buf.shape[0] // 2, 4, row_share, radial_len)
    row_strip = jnp.transpose(row_strip, (2, 0, 1, 3, 4)).reshape(4, 2, breadth, radial_len)
    north_strip = row_strip
    south_strip = jnp.stack([row_strip[:, 1], row_strip[:, 0]], axis=1)
    fresh = fresh.at[:, 0:2].set(jnp.where(colat_pos == 0, north_strip, fresh[:, 0:2]))
    fresh = fresh.at[:, height - 2 :].set(
        jnp.where(colat_pos == colat_count - 1, south_strip, fresh[:, height - 2 :])
    )
    return fresh[:, None]


def solution(mesh):
    placed = (
        P(None, "panel", "colat", "lon", None),
        P("panel", "colat", "lon", None),
        P("panel", "colat", "lon", None),
        P("panel", "colat", "lon", None),
        P("panel", "colat", "lon", None),
        P("panel", "colat", "lon", None, None),
        P("panel", "colat", "lon", None),
    )
    return jax.shard_map(
        local,
        mesh=mesh,
        in_specs=placed,
        out_specs=P(None, "panel", "colat", "lon", None),
        check_vma=False,
    )
```

```python
import jax
import jax.numpy as jnp
from jax import lax
from jax.sharding import PartitionSpec as P
from jax.experimental import pallas as pl
from jax.experimental.pallas import tpu as pltpu

MESH = pl.DeviceIdType.MESH

TIME_STEP = 0.05
BUOYANCY = 1.0


def with_halo(x, sides, width):
    for axis, dim in sides:
        count, length = (lax.axis_size(axis), x.shape[dim])
        up = [(i, (i + 1) % count) for i in range(count - 1)]
        down = [(j, i) for i, j in up]
        last = lax.slice_in_dim(x, length - width, length, axis=dim)
        leading = lax.slice_in_dim(x, 0, width, axis=dim)
        before = lax.ppermute(last, axis, up)
        after = lax.ppermute(leading, axis, down)
        x = jnp.concatenate([before, x, after], axis=dim)
    return x


def swapped(block, axis, stride):
    count = lax.axis_size(axis)
    route = []
    for low in range(count):
        high = low | 1 << stride
        if high != low and high < count:
            route += [(low, high), (high, low)]
    return lax.ppermute(block, axis, route)


def rim_kernel(row_ref, col_ref, row_out, col_out, send_sem, row_sem, col_sem):
    panel = lax.axis_index("panel")
    colat = lax.axis_index("colat")
    lon = lax.axis_index("lon")
    colat_count = lax.axis_size("colat")
    lon_count = lax.axis_size("lon")
    row_types = row_out.shape[0] // 2
    col_types = col_out.shape[0] // 2
    other = 1 - panel

    def route(share, per_type, count):
        kind = share // per_type
        edge = (kind % 2) * (count - 1)
        slot = (kind // 2) * per_type + share % per_type
        return edge, slot

    row_edge, row_slot = route(colat, row_types, colat_count)
    col_edge, col_slot = route(lon, col_types, lon_count)
    row_dest = (other, row_edge, lon)
    col_dest = (other, colat, col_edge)
    at_row_edge = jnp.logical_or(colat == 0, colat == colat_count - 1)
    at_col_edge = jnp.logical_or(lon == 0, lon == lon_count - 1)
    parity_row = (colat // (colat_count - 1)).astype(jnp.int32)
    parity_col = (lon // (lon_count - 1)).astype(jnp.int32)

    def row_sender(slot):
        kind = 2 * (slot // row_types) + parity_row
        return (other, kind * row_types + slot % row_types, lon)

    def col_sender(slot):
        kind = 2 * (slot // col_types) + parity_col
        return (other, colat, kind * col_types + slot % col_types)

    barrier = pltpu.get_barrier_semaphore()
    pl.semaphore_signal(barrier, 1, device_id=row_dest, device_id_type=MESH)
    pl.semaphore_signal(barrier, 1, device_id=col_dest, device_id_type=MESH)

    @pl.when(at_row_edge)
    def _():
        for slot in range(2 * row_types):
            pl.semaphore_signal(barrier, 1, device_id=row_sender(slot), device_id_type=MESH)

    @pl.when(at_col_edge)
    def _():
        for slot in range(2 * col_types):
            pl.semaphore_signal(barrier, 1, device_id=col_sender(slot), device_id_type=MESH)

    expected = (
        2
        + at_row_edge.astype(jnp.int32) * (2 * row_types)
        + at_col_edge.astype(jnp.int32) * (2 * col_types)
    )
    pl.semaphore_wait(barrier, expected)

    row_copy = pltpu.make_async_remote_copy(
        row_ref, row_out.at[row_slot], send_sem.at[0], row_sem.at[row_slot],
        device_id=row_dest, device_id_type=MESH,
    )
    col_copy = pltpu.make_async_remote_copy(
        col_ref, col_out.at[col_slot], send_sem.at[1], col_sem.at[col_slot],
        device_id=col_dest, device_id_type=MESH,
    )
    row_copy.start()
    col_copy.start()
    row_copy.wait_send()
    col_copy.wait_send()

    @pl.when(at_row_edge)
    def _():
        for slot in range(2 * row_types):
            pltpu.make_async_remote_copy(
                row_ref, row_out.at[slot], send_sem.at[0], row_sem.at[slot],
                device_id=row_sender(slot), device_id_type=MESH,
            ).wait_recv()

    @pl.when(at_col_edge)
    def _():
        for slot in range(2 * col_types):
            pltpu.make_async_remote_copy(
                col_ref, col_out.at[slot], send_sem.at[1], col_sem.at[slot],
                device_id=col_sender(slot), device_id_type=MESH,
            ).wait_recv()


def rim_exchange(rows, cols):
    colat_count = lax.axis_size("colat")
    lon_count = lax.axis_size("lon")
    row_types = colat_count // 4
    col_types = lon_count // 4
    vmem = pl.BlockSpec(memory_space=pltpu.VMEM)
    return pl.pallas_call(
        rim_kernel,
        out_shape=(
            jax.ShapeDtypeStruct((2 * row_types,) + rows.shape, rows.dtype),
            jax.ShapeDtypeStruct((2 * col_types,) + cols.shape, cols.dtype),
        ),
        in_specs=[vmem, vmem],
        out_specs=(vmem, vmem),
        scratch_shapes=[
            pltpu.SemaphoreType.DMA((2,)),
            pltpu.SemaphoreType.DMA((2 * row_types,)),
            pltpu.SemaphoreType.DMA((2 * col_types,)),
        ],
        compiler_params=pltpu.CompilerParams(collective_id=0, has_side_effects=True),
    )(rows, cols)


DIRECTIONS = ((-1, -1), (-1, 0), (-1, 1), (0, -1), (0, 1), (1, -1), (1, 0), (1, 1))


def halo_kernel(*refs):
    count = len(DIRECTIONS)
    sends = refs[0 : 2 * count]
    recvs = refs[2 * count : 4 * count]
    send_sem, recv_sem = refs[4 * count :]
    panel = lax.axis_index("panel")
    colat = lax.axis_index("colat")
    lon = lax.axis_index("lon")
    colat_count = lax.axis_size("colat")
    lon_count = lax.axis_size("lon")

    def present(step):
        row = colat + step[0]
        col = lon + step[1]
        inside = jnp.logical_and(row >= 0, row < colat_count)
        return jnp.logical_and(inside, jnp.logical_and(col >= 0, col < lon_count))

    def copies(index, part):
        step = DIRECTIONS[index]
        target = (panel, colat + step[0], lon + step[1])
        back = count - 1 - index
        return pltpu.make_async_remote_copy(
            sends[2 * index + part], recvs[2 * back + part],
            send_sem.at[index, part], recv_sem.at[back, part],
            device_id=target, device_id_type=MESH,
        )

    def arriving(index, part):
        step = DIRECTIONS[index]
        source = (panel, colat + step[0], lon + step[1])
        return pltpu.make_async_remote_copy(
            sends[2 * index + part], recvs[2 * index + part],
            send_sem.at[index, part], recv_sem.at[index, part],
            device_id=source, device_id_type=MESH,
        )

    barrier = pltpu.get_barrier_semaphore()
    expected = jnp.int32(0)
    for index, step in enumerate(DIRECTIONS):
        exists = present(step)
        expected = expected + exists.astype(jnp.int32)

        @pl.when(exists)
        def _():
            pl.semaphore_signal(
                barrier, 1, device_id=(panel, colat + step[0], lon + step[1]),
                device_id_type=MESH,
            )

    pl.semaphore_wait(barrier, expected)
    for index, step in enumerate(DIRECTIONS):

        @pl.when(present(step))
        def _():
            copies(index, 0).start()
            copies(index, 1).start()

    for index, step in enumerate(DIRECTIONS):

        @pl.when(present(step))
        def _():
            copies(index, 0).wait_send()
            copies(index, 1).wait_send()
            arriving(index, 0).wait_recv()
            arriving(index, 1).wait_recv()


def halo_exchange(fields, coefs, width):
    height, breadth = fields.shape[1], fields.shape[2]
    sends = []
    shapes = []
    for step in DIRECTIONS:
        for block, depth in ((fields, width), (coefs, 1)):
            rows = slice(0, depth) if step[0] < 0 else slice(height - depth, height) if step[0] > 0 else slice(0, height)
            cols = slice(0, depth) if step[1] < 0 else slice(breadth - depth, breadth) if step[1] > 0 else slice(0, breadth)
            piece = block[:, rows, cols]
            sends.append(piece)
            shapes.append(jax.ShapeDtypeStruct(piece.shape, piece.dtype))
    vmem = pl.BlockSpec(memory_space=pltpu.VMEM)
    count = len(DIRECTIONS)
    recvs = pl.pallas_call(
        halo_kernel,
        out_shape=tuple(shapes),
        in_specs=[vmem] * len(sends),
        out_specs=tuple([vmem] * len(sends)),
        scratch_shapes=[
            pltpu.SemaphoreType.DMA((count, 2)),
            pltpu.SemaphoreType.DMA((count, 2)),
        ],
        compiler_params=pltpu.CompilerParams(collective_id=1, has_side_effects=True),
    )(*sends)
    colat = lax.axis_index("colat")
    lon = lax.axis_index("lon")
    colat_count = lax.axis_size("colat")
    lon_count = lax.axis_size("lon")
    padded = []
    for part, block in enumerate((fields, coefs)):
        pieces = {}
        for index, step in enumerate(DIRECTIONS):
            row = colat + step[0]
            col = lon + step[1]
            exists = (row >= 0) & (row < colat_count) & (col >= 0) & (col < lon_count)
            got = recvs[2 * index + part]
            pieces[step] = jnp.where(exists, got, jnp.zeros_like(got))
        pieces[(0, 0)] = block
        bands = [
            jnp.concatenate([pieces[(r, -1)], pieces[(r, 0)], pieces[(r, 1)]], axis=2)
            for r in (-1, 0, 1)
        ]
        padded.append(jnp.concatenate(bands, axis=1))
    return padded


def gradient(stencil):
    return (8.0 * (stencil[3] - stencil[1]) - (stencil[4] - stencil[0])) / 12.0


def curvature(stencil):
    return (16.0 * (stencil[3] + stencil[1]) - (stencil[4] + stencil[0]) - 30.0 * stencil[2]) / 12.0


def advance(padded, thermal, viscous):
    height = padded.shape[1] - 4
    breadth = padded.shape[2] - 4
    center = padded[:, 2 : 2 + height, 2 : 2 + breadth]
    radial_len = center.shape[3]
    radial_pad = jnp.pad(center, ((0, 0), (0, 0), (0, 0), (2, 2)))
    along_lat = [padded[:, offset : offset + height, 2 : 2 + breadth] for offset in range(5)]
    along_lon = [padded[:, 2 : 2 + height, offset : offset + breadth] for offset in range(5)]
    along_rad = [radial_pad[..., offset : offset + radial_len] for offset in range(5)]
    laplace = curvature(along_rad) + curvature(along_lat) + curvature(along_lon)
    transport = (
        center[1:2] * gradient(along_rad)
        + center[2:3] * gradient(along_lat)
        + center[3:4] * gradient(along_lon)
    )
    diffusion = jnp.stack([thermal, viscous, viscous, viscous])
    change = diffusion * laplace - transport
    change = change.at[1].add(BUOYANCY * center[0])
    return center + TIME_STEP * change


def local(fields_now, diffusivity, viscosity, donor_row, donor_column, donor_offset, rim_angle):
    fields = fields_now[:, 0]
    thermal = diffusivity[0]
    viscous = viscosity[0]
    height = fields.shape[1]
    breadth = fields.shape[2]
    radial_len = fields.shape[3]
    colat_pos = lax.axis_index("colat")
    lon_pos = lax.axis_index("lon")
    colat_count = lax.axis_size("colat")
    lon_count = lax.axis_size("lon")
    row_share = 4 * breadth // colat_count
    coefs = jnp.concatenate([thermal[None], viscous[None]], axis=0)
    padded, coef_ext = halo_exchange(fields, coefs, 3)
    fresh_ext = advance(padded, coef_ext[0], coef_ext[1])
    row_ids = lax.broadcasted_iota(jnp.int32, (height + 2, breadth + 2), 0) + colat_pos * height - 1
    col_ids = lax.broadcasted_iota(jnp.int32, (height + 2, breadth + 2), 1) + lon_pos * breadth - 1
    in_panel = (
        (row_ids >= 0) & (row_ids < colat_count * height)
        & (col_ids >= 0) & (col_ids < lon_count * breadth)
    )
    extended = jnp.where(in_panel[None, :, :, None], fresh_ext, 0.0)
    fresh = fresh_ext[:, 1 : 1 + height, 1 : 1 + breadth]
    width = breadth + 2
    flattened = extended.reshape(4, (height + 2) * width, radial_len)
    anchor = donor_row.reshape(-1) * width + donor_column.reshape(-1)

    def corner(offset):
        return jnp.take(flattened, anchor + offset, axis=1)

    frac_row = donor_offset[0, 0, 0, 0][None, :, None]
    frac_lon = donor_offset[0, 0, 0, 1][None, :, None]
    blended = (1.0 - frac_row) * (
        (1.0 - frac_lon) * corner(0) + frac_lon * corner(1)
    ) + frac_row * ((1.0 - frac_lon) * corner(width) + frac_lon * corner(width + 1))
    angles = rim_angle.reshape(-1)
    cosine = jnp.cos(angles)[:, None]
    sine_part = jnp.sin(angles)[:, None]
    turned_lat = cosine * blended[2] - sine_part * blended[3]
    turned_lon = sine_part * blended[2] + cosine * blended[3]
    blended = jnp.stack([blended[0], blended[1], turned_lat, turned_lon])
    row_buf, col_buf = rim_exchange(blended[:, 0:row_share], blended[:, row_share:])
    col_share = blended.shape[1] - row_share
    col_strip = col_buf.reshape(2, col_buf.shape[0] // 2, 4, col_share, radial_len)
    col_strip = jnp.transpose(col_strip, (2, 0, 1, 3, 4)).reshape(4, 2, height, radial_len)
    west_strip = jnp.transpose(col_strip, (0, 2, 1, 3))
    east_strip = jnp.stack([col_strip[:, 1], col_strip[:, 0]], axis=2)
    fresh = fresh.at[:, :, 0:2].set(jnp.where(lon_pos == 0, west_strip, fresh[:, :, 0:2]))
    fresh = fresh.at[:, :, breadth - 2 :].set(
        jnp.where(lon_pos == lon_count - 1, east_strip, fresh[:, :, breadth - 2 :])
    )
    row_strip = row_buf.reshape(2, row_buf.shape[0] // 2, 4, row_share, radial_len)
    row_strip = jnp.transpose(row_strip, (2, 0, 1, 3, 4)).reshape(4, 2, breadth, radial_len)
    north_strip = row_strip
    south_strip = jnp.stack([row_strip[:, 1], row_strip[:, 0]], axis=1)
    fresh = fresh.at[:, 0:2].set(jnp.where(colat_pos == 0, north_strip, fresh[:, 0:2]))
    fresh = fresh.at[:, height - 2 :].set(
        jnp.where(colat_pos == colat_count - 1, south_strip, fresh[:, height - 2 :])
    )
    return fresh[:, None]


def solution(mesh):
    placed = (
        P(None, "panel", "colat", "lon", None),
        P("panel", "colat", "lon", None),
        P("panel", "colat", "lon", None),
        P("panel", "colat", "lon", None),
        P("panel", "colat", "lon", None),
        P("panel", "colat", "lon", None, None),
        P("panel", "colat", "lon", None),
    )
    return jax.shard_map(
        local,
        mesh=mesh,
        in_specs=placed,
        out_specs=P(None, "panel", "colat", "lon", None),
        check_vma=False,
    )
```

```python
import functools

import jax
import jax.numpy as jnp
from jax import lax
from jax.sharding import PartitionSpec as P
from jax.experimental import pallas as pl
from jax.experimental.pallas import tpu as pltpu

MESH = pl.DeviceIdType.MESH

TIME_STEP = 0.05
BUOYANCY = 1.0


def with_halo(x, sides, width):
    for axis, dim in sides:
        count, length = (lax.axis_size(axis), x.shape[dim])
        up = [(i, (i + 1) % count) for i in range(count - 1)]
        down = [(j, i) for i, j in up]
        last = lax.slice_in_dim(x, length - width, length, axis=dim)
        leading = lax.slice_in_dim(x, 0, width, axis=dim)
        before = lax.ppermute(last, axis, up)
        after = lax.ppermute(leading, axis, down)
        x = jnp.concatenate([before, x, after], axis=dim)
    return x


def swapped(block, axis, stride):
    count = lax.axis_size(axis)
    route = []
    for low in range(count):
        high = low | 1 << stride
        if high != low and high < count:
            route += [(low, high), (high, low)]
    return lax.ppermute(block, axis, route)


def rim_kernel(row_ref, col_ref, row_out, col_out, send_sem, row_sem, col_sem):
    panel = lax.axis_index("panel")
    colat = lax.axis_index("colat")
    lon = lax.axis_index("lon")
    colat_count = lax.axis_size("colat")
    lon_count = lax.axis_size("lon")
    row_types = row_out.shape[0] // 2
    col_types = col_out.shape[0] // 2
    other = 1 - panel

    def route(share, per_type, count):
        kind = share // per_type
        edge = (kind % 2) * (count - 1)
        slot = (kind // 2) * per_type + share % per_type
        return edge, slot

    row_edge, row_slot = route(colat, row_types, colat_count)
    col_edge, col_slot = route(lon, col_types, lon_count)
    row_dest = (other, row_edge, lon)
    col_dest = (other, colat, col_edge)
    at_row_edge = jnp.logical_or(colat == 0, colat == colat_count - 1)
    at_col_edge = jnp.logical_or(lon == 0, lon == lon_count - 1)
    parity_row = (colat // (colat_count - 1)).astype(jnp.int32)
    parity_col = (lon // (lon_count - 1)).astype(jnp.int32)

    def row_sender(slot):
        kind = 2 * (slot // row_types) + parity_row
        return (other, kind * row_types + slot % row_types, lon)

    def col_sender(slot):
        kind = 2 * (slot // col_types) + parity_col
        return (other, colat, kind * col_types + slot % col_types)

    barrier = pltpu.get_barrier_semaphore()
    pl.semaphore_signal(barrier, 1, device_id=row_dest, device_id_type=MESH)
    pl.semaphore_signal(barrier, 1, device_id=col_dest, device_id_type=MESH)

    @pl.when(at_row_edge)
    def _():
        for slot in range(2 * row_types):
            pl.semaphore_signal(barrier, 1, device_id=row_sender(slot), device_id_type=MESH)

    @pl.when(at_col_edge)
    def _():
        for slot in range(2 * col_types):
            pl.semaphore_signal(barrier, 1, device_id=col_sender(slot), device_id_type=MESH)

    expected = (
        2
        + at_row_edge.astype(jnp.int32) * (2 * row_types)
        + at_col_edge.astype(jnp.int32) * (2 * col_types)
    )
    pl.semaphore_wait(barrier, expected)

    row_copy = pltpu.make_async_remote_copy(
        row_ref, row_out.at[row_slot], send_sem.at[0], row_sem.at[row_slot],
        device_id=row_dest, device_id_type=MESH,
    )
    col_copy = pltpu.make_async_remote_copy(
        col_ref, col_out.at[col_slot], send_sem.at[1], col_sem.at[col_slot],
        device_id=col_dest, device_id_type=MESH,
    )
    row_copy.start()
    col_copy.start()
    row_copy.wait_send()
    col_copy.wait_send()

    @pl.when(at_row_edge)
    def _():
        for slot in range(2 * row_types):
            pltpu.make_async_remote_copy(
                row_ref, row_out.at[slot], send_sem.at[0], row_sem.at[slot],
                device_id=row_sender(slot), device_id_type=MESH,
            ).wait_recv()

    @pl.when(at_col_edge)
    def _():
        for slot in range(2 * col_types):
            pltpu.make_async_remote_copy(
                col_ref, col_out.at[slot], send_sem.at[1], col_sem.at[slot],
                device_id=col_sender(slot), device_id_type=MESH,
            ).wait_recv()


def rim_exchange(rows, cols):
    colat_count = lax.axis_size("colat")
    lon_count = lax.axis_size("lon")
    row_types = colat_count // 4
    col_types = lon_count // 4
    vmem = pl.BlockSpec(memory_space=pltpu.VMEM)
    return pl.pallas_call(
        rim_kernel,
        out_shape=(
            jax.ShapeDtypeStruct((2 * row_types,) + rows.shape, rows.dtype),
            jax.ShapeDtypeStruct((2 * col_types,) + cols.shape, cols.dtype),
        ),
        in_specs=[vmem, vmem],
        out_specs=(vmem, vmem),
        scratch_shapes=[
            pltpu.SemaphoreType.DMA((2,)),
            pltpu.SemaphoreType.DMA((2 * row_types,)),
            pltpu.SemaphoreType.DMA((2 * col_types,)),
        ],
        compiler_params=pltpu.CompilerParams(collective_id=0, has_side_effects=True),
    )(rows, cols)


DIRECTIONS = ((-1, -1), (-1, 0), (-1, 1), (0, -1), (0, 1), (1, -1), (1, 0), (1, 1))


def window(step, width, length, offset):
    if step < 0:
        return offset, width
    if step > 0:
        return offset + length - width, width
    return offset, length


def landing(step, width, length, offset):
    if step < 0:
        return offset - width, width
    if step > 0:
        return offset + length, width
    return offset, length


def halo_kernel(width, margins, fields_in, coefs_in, fields_out, coefs_out, send_sem, recv_sem):
    del fields_in, coefs_in
    count = len(DIRECTIONS)
    panel = lax.axis_index("panel")
    colat = lax.axis_index("colat")
    lon = lax.axis_index("lon")
    colat_count = lax.axis_size("colat")
    lon_count = lax.axis_size("lon")
    height = fields_out.shape[1] - 2 * margins[0][0]
    breadth = fields_out.shape[2] - 2 * margins[0][1]
    layers = ((fields_out, width, margins[0]), (coefs_out, 1, margins[1]))

    def present(step):
        row = colat + step[0]
        col = lon + step[1]
        inside = jnp.logical_and(row >= 0, row < colat_count)
        return jnp.logical_and(inside, jnp.logical_and(col >= 0, col < lon_count))

    def region(ref, rows, cols):
        return ref.at[:, pl.ds(rows[0], rows[1]), pl.ds(cols[0], cols[1]), :]

    def outgoing(index, part):
        step = DIRECTIONS[index]
        ref, depth, (row_pad, col_pad) = layers[part]
        source = region(
            ref, window(step[0], depth, height, row_pad), window(step[1], depth, breadth, col_pad)
        )
        target = region(
            ref, landing(-step[0], depth, height, row_pad), landing(-step[1], depth, breadth, col_pad)
        )
        return pltpu.make_async_remote_copy(
            source, target, send_sem.at[index, part], recv_sem.at[count - 1 - index, part],
            device_id=(panel, colat + step[0], lon + step[1]), device_id_type=MESH,
        )

    def incoming(index, part):
        step = DIRECTIONS[index]
        ref, depth, (row_pad, col_pad) = layers[part]
        target = region(
            ref, landing(step[0], depth, height, row_pad), landing(step[1], depth, breadth, col_pad)
        )
        return pltpu.make_async_remote_copy(
            target, target, send_sem.at[index, part], recv_sem.at[index, part],
            device_id=(panel, colat + step[0], lon + step[1]), device_id_type=MESH,
        )

    barrier = pltpu.get_barrier_semaphore()
    expected = jnp.int32(0)
    for index, step in enumerate(DIRECTIONS):
        exists = present(step)
        expected = expected + exists.astype(jnp.int32)

        @pl.when(exists)
        def _():
            pl.semaphore_signal(
                barrier, 1, device_id=(panel, colat + step[0], lon + step[1]),
                device_id_type=MESH,
            )

    pl.semaphore_wait(barrier, expected)
    for index, step in enumerate(DIRECTIONS):

        @pl.when(present(step))
        def _():
            outgoing(index, 0).start()
            outgoing(index, 1).start()

    for index, step in enumerate(DIRECTIONS):

        @pl.when(present(step))
        def _():
            outgoing(index, 0).wait_send()
            outgoing(index, 1).wait_send()
            incoming(index, 0).wait_recv()
            incoming(index, 1).wait_recv()


def halo_exchange(fields, coefs, width):
    lane_pad = 8
    margins = ((width, lane_pad), (1, lane_pad))
    fields_pad = jnp.pad(fields, ((0, 0), (width, width), (lane_pad, lane_pad), (0, 0)))
    coefs_pad = jnp.pad(coefs, ((0, 0), (1, 1), (lane_pad, lane_pad), (0, 0)))
    anywhere = pl.BlockSpec(memory_space=pl.ANY)
    count = len(DIRECTIONS)
    fields_pad, coefs_pad = pl.pallas_call(
        functools.partial(halo_kernel, width, margins),
        out_shape=(
            jax.ShapeDtypeStruct(fields_pad.shape, fields_pad.dtype),
            jax.ShapeDtypeStruct(coefs_pad.shape, coefs_pad.dtype),
        ),
        in_specs=[anywhere, anywhere],
        out_specs=(anywhere, anywhere),
        scratch_shapes=[
            pltpu.SemaphoreType.DMA((count, 2)),
            pltpu.SemaphoreType.DMA((count, 2)),
        ],
        input_output_aliases={0: 0, 1: 1},
        compiler_params=pltpu.CompilerParams(collective_id=1, has_side_effects=True),
    )(fields_pad, coefs_pad)
    return (
        fields_pad[:, :, lane_pad - width : lane_pad + fields.shape[2] + width],
        coefs_pad[:, :, lane_pad - 1 : lane_pad + fields.shape[2] + 1],
    )


def gradient(stencil):
    return (8.0 * (stencil[3] - stencil[1]) - (stencil[4] - stencil[0])) / 12.0


def curvature(stencil):
    return (16.0 * (stencil[3] + stencil[1]) - (stencil[4] + stencil[0]) - 30.0 * stencil[2]) / 12.0


def advance(padded, thermal, viscous):
    height = padded.shape[1] - 4
    breadth = padded.shape[2] - 4
    center = padded[:, 2 : 2 + height, 2 : 2 + breadth]
    radial_len = center.shape[3]
    radial_pad = jnp.pad(center, ((0, 0), (0, 0), (0, 0), (2, 2)))
    along_lat = [padded[:, offset : offset + height, 2 : 2 + breadth] for offset in range(5)]
    along_lon = [padded[:, 2 : 2 + height, offset : offset + breadth] for offset in range(5)]
    along_rad = [radial_pad[..., offset : offset + radial_len] for offset in range(5)]
    laplace = curvature(along_rad) + curvature(along_lat) + curvature(along_lon)
    transport = (
        center[1:2] * gradient(along_rad)
        + center[2:3] * gradient(along_lat)
        + center[3:4] * gradient(along_lon)
    )
    diffusion = jnp.stack([thermal, viscous, viscous, viscous])
    change = diffusion * laplace - transport
    change = change.at[1].add(BUOYANCY * center[0])
    return center + TIME_STEP * change


def local(fields_now, diffusivity, viscosity, donor_row, donor_column, donor_offset, rim_angle):
    fields = fields_now[:, 0]
    thermal = diffusivity[0]
    viscous = viscosity[0]
    height = fields.shape[1]
    breadth = fields.shape[2]
    radial_len = fields.shape[3]
    colat_pos = lax.axis_index("colat")
    lon_pos = lax.axis_index("lon")
    colat_count = lax.axis_size("colat")
    lon_count = lax.axis_size("lon")
    row_share = 4 * breadth // colat_count
    coefs = jnp.concatenate([thermal[None], viscous[None]], axis=0)
    padded, coef_ext = halo_exchange(fields, coefs, 3)
    fresh_ext = advance(padded, coef_ext[0], coef_ext[1])
    row_ids = lax.broadcasted_iota(jnp.int32, (height + 2, breadth + 2), 0) + colat_pos * height - 1
    col_ids = lax.broadcasted_iota(jnp.int32, (height + 2, breadth + 2), 1) + lon_pos * breadth - 1
    in_panel = (
        (row_ids >= 0) & (row_ids < colat_count * height)
        & (col_ids >= 0) & (col_ids < lon_count * breadth)
    )
    extended = jnp.where(in_panel[None, :, :, None], fresh_ext, 0.0)
    fresh = fresh_ext[:, 1 : 1 + height, 1 : 1 + breadth]
    width = breadth + 2
    flattened = extended.reshape(4, (height + 2) * width, radial_len)
    anchor = donor_row.reshape(-1) * width + donor_column.reshape(-1)

    def corner(offset):
        return jnp.take(flattened, anchor + offset, axis=1)

    frac_row = donor_offset[0, 0, 0, 0][None, :, None]
    frac_lon = donor_offset[0, 0, 0, 1][None, :, None]
    blended = (1.0 - frac_row) * (
        (1.0 - frac_lon) * corner(0) + frac_lon * corner(1)
    ) + frac_row * ((1.0 - frac_lon) * corner(width) + frac_lon * corner(width + 1))
    angles = rim_angle.reshape(-1)
    cosine = jnp.cos(angles)[:, None]
    sine_part = jnp.sin(angles)[:, None]
    turned_lat = cosine * blended[2] - sine_part * blended[3]
    turned_lon = sine_part * blended[2] + cosine * blended[3]
    blended = jnp.stack([blended[0], blended[1], turned_lat, turned_lon])
    row_buf, col_buf = rim_exchange(blended[:, 0:row_share], blended[:, row_share:])
    col_share = blended.shape[1] - row_share
    col_strip = col_buf.reshape(2, col_buf.shape[0] // 2, 4, col_share, radial_len)
    col_strip = jnp.transpose(col_strip, (2, 0, 1, 3, 4)).reshape(4, 2, height, radial_len)
    west_strip = jnp.transpose(col_strip, (0, 2, 1, 3))
    east_strip = jnp.stack([col_strip[:, 1], col_strip[:, 0]], axis=2)
    row_strip = row_buf.reshape(2, row_buf.shape[0] // 2, 4, row_share, radial_len)
    row_strip = jnp.transpose(row_strip, (2, 0, 1, 3, 4)).reshape(4, 2, breadth, radial_len)
    north_strip = row_strip
    south_strip = jnp.stack([row_strip[:, 1], row_strip[:, 0]], axis=1)
    gap_cols = jnp.zeros((4, height, breadth - 4, radial_len), fresh.dtype)
    col_rim = jnp.concatenate([west_strip, gap_cols, east_strip], axis=2)
    gap_rows = jnp.zeros((4, height - 4, breadth, radial_len), fresh.dtype)
    row_rim = jnp.concatenate([north_strip, gap_rows, south_strip], axis=1)
    row_ids = lax.broadcasted_iota(jnp.int32, (height, breadth), 0)
    col_ids = lax.broadcasted_iota(jnp.int32, (height, breadth), 1)
    use_col = ((lon_pos == 0) & (col_ids < 2)) | ((lon_pos == lon_count - 1) & (col_ids >= breadth - 2))
    use_row = ((colat_pos == 0) & (row_ids < 2)) | ((colat_pos == colat_count - 1) & (row_ids >= height - 2))
    fresh = jnp.where(use_col[None, :, :, None], col_rim, fresh)
    fresh = jnp.where(use_row[None, :, :, None], row_rim, fresh)
    return fresh[:, None]


def solution(mesh):
    placed = (
        P(None, "panel", "colat", "lon", None),
        P("panel", "colat", "lon", None),
        P("panel", "colat", "lon", None),
        P("panel", "colat", "lon", None),
        P("panel", "colat", "lon", None),
        P("panel", "colat", "lon", None, None),
        P("panel", "colat", "lon", None),
    )
    return jax.shard_map(
        local,
        mesh=mesh,
        in_specs=placed,
        out_specs=P(None, "panel", "colat", "lon", None),
        check_vma=False,
    )
```

```python
import functools

import jax
import jax.numpy as jnp
from jax import lax
from jax.sharding import PartitionSpec as P
from jax.experimental import pallas as pl
from jax.experimental.pallas import tpu as pltpu

MESH = pl.DeviceIdType.MESH

TIME_STEP = 0.05
BUOYANCY = 1.0


def with_halo(x, sides, width):
    for axis, dim in sides:
        count, length = (lax.axis_size(axis), x.shape[dim])
        up = [(i, (i + 1) % count) for i in range(count - 1)]
        down = [(j, i) for i, j in up]
        last = lax.slice_in_dim(x, length - width, length, axis=dim)
        leading = lax.slice_in_dim(x, 0, width, axis=dim)
        before = lax.ppermute(last, axis, up)
        after = lax.ppermute(leading, axis, down)
        x = jnp.concatenate([before, x, after], axis=dim)
    return x


def swapped(block, axis, stride):
    count = lax.axis_size(axis)
    route = []
    for low in range(count):
        high = low | 1 << stride
        if high != low and high < count:
            route += [(low, high), (high, low)]
    return lax.ppermute(block, axis, route)


def rim_kernel(row_ref, col_ref, row_out, col_out, send_sem, row_sem, col_sem):
    panel = lax.axis_index("panel")
    colat = lax.axis_index("colat")
    lon = lax.axis_index("lon")
    colat_count = lax.axis_size("colat")
    lon_count = lax.axis_size("lon")
    row_types = row_out.shape[0] // 2
    col_types = col_out.shape[0] // 2
    other = 1 - panel

    def route(share, per_type, count):
        kind = share // per_type
        edge = (kind % 2) * (count - 1)
        slot = (kind // 2) * per_type + share % per_type
        return edge, slot

    row_edge, row_slot = route(colat, row_types, colat_count)
    col_edge, col_slot = route(lon, col_types, lon_count)
    row_dest = (other, row_edge, lon)
    col_dest = (other, colat, col_edge)
    at_row_edge = jnp.logical_or(colat == 0, colat == colat_count - 1)
    at_col_edge = jnp.logical_or(lon == 0, lon == lon_count - 1)
    parity_row = (colat // (colat_count - 1)).astype(jnp.int32)
    parity_col = (lon // (lon_count - 1)).astype(jnp.int32)

    def row_sender(slot):
        kind = 2 * (slot // row_types) + parity_row
        return (other, kind * row_types + slot % row_types, lon)

    def col_sender(slot):
        kind = 2 * (slot // col_types) + parity_col
        return (other, colat, kind * col_types + slot % col_types)

    barrier = pltpu.get_barrier_semaphore()
    pl.semaphore_signal(barrier, 1, device_id=row_dest, device_id_type=MESH)
    pl.semaphore_signal(barrier, 1, device_id=col_dest, device_id_type=MESH)

    @pl.when(at_row_edge)
    def _():
        for slot in range(2 * row_types):
            pl.semaphore_signal(barrier, 1, device_id=row_sender(slot), device_id_type=MESH)

    @pl.when(at_col_edge)
    def _():
        for slot in range(2 * col_types):
            pl.semaphore_signal(barrier, 1, device_id=col_sender(slot), device_id_type=MESH)

    expected = (
        2
        + at_row_edge.astype(jnp.int32) * (2 * row_types)
        + at_col_edge.astype(jnp.int32) * (2 * col_types)
    )
    pl.semaphore_wait(barrier, expected)

    row_copy = pltpu.make_async_remote_copy(
        row_ref, row_out.at[row_slot], send_sem.at[0], row_sem.at[row_slot],
        device_id=row_dest, device_id_type=MESH,
    )
    col_copy = pltpu.make_async_remote_copy(
        col_ref, col_out.at[col_slot], send_sem.at[1], col_sem.at[col_slot],
        device_id=col_dest, device_id_type=MESH,
    )
    row_copy.start()
    col_copy.start()
    row_copy.wait_send()
    col_copy.wait_send()

    @pl.when(at_row_edge)
    def _():
        for slot in range(2 * row_types):
            pltpu.make_async_remote_copy(
                row_ref, row_out.at[slot], send_sem.at[0], row_sem.at[slot],
                device_id=row_sender(slot), device_id_type=MESH,
            ).wait_recv()

    @pl.when(at_col_edge)
    def _():
        for slot in range(2 * col_types):
            pltpu.make_async_remote_copy(
                col_ref, col_out.at[slot], send_sem.at[1], col_sem.at[slot],
                device_id=col_sender(slot), device_id_type=MESH,
            ).wait_recv()


def rim_exchange(rows, cols):
    colat_count = lax.axis_size("colat")
    lon_count = lax.axis_size("lon")
    row_types = colat_count // 4
    col_types = lon_count // 4
    vmem = pl.BlockSpec(memory_space=pltpu.VMEM)
    return pl.pallas_call(
        rim_kernel,
        out_shape=(
            jax.ShapeDtypeStruct((2 * row_types,) + rows.shape, rows.dtype),
            jax.ShapeDtypeStruct((2 * col_types,) + cols.shape, cols.dtype),
        ),
        in_specs=[vmem, vmem],
        out_specs=(vmem, vmem),
        scratch_shapes=[
            pltpu.SemaphoreType.DMA((2,)),
            pltpu.SemaphoreType.DMA((2 * row_types,)),
            pltpu.SemaphoreType.DMA((2 * col_types,)),
        ],
        compiler_params=pltpu.CompilerParams(collective_id=0, has_side_effects=True),
    )(rows, cols)


DIRECTIONS = ((-1, -1), (-1, 0), (-1, 1), (0, -1), (0, 1), (1, -1), (1, 0), (1, 1))


def window(step, width, length, offset):
    if step < 0:
        return offset, width
    if step > 0:
        return offset + length - width, width
    return offset, length


def landing(step, width, length, offset):
    if step < 0:
        return offset - width, width
    if step > 0:
        return offset + length, width
    return offset, length


def halo_kernel(width, margins, fields_in, coefs_in, fields_out, coefs_out, send_sem, recv_sem):
    del fields_in, coefs_in
    count = len(DIRECTIONS)
    panel = lax.axis_index("panel")
    colat = lax.axis_index("colat")
    lon = lax.axis_index("lon")
    colat_count = lax.axis_size("colat")
    lon_count = lax.axis_size("lon")
    height = fields_out.shape[1] - 2 * margins[0][0]
    breadth = fields_out.shape[2] - 2 * margins[0][1]
    layers = ((fields_out, width, margins[0]), (coefs_out, 1, margins[1]))

    def present(step):
        row = colat + step[0]
        col = lon + step[1]
        inside = jnp.logical_and(row >= 0, row < colat_count)
        return jnp.logical_and(inside, jnp.logical_and(col >= 0, col < lon_count))

    def region(ref, rows, cols):
        return ref.at[:, pl.ds(rows[0], rows[1]), pl.ds(cols[0], cols[1]), :]

    def outgoing(index, part):
        step = DIRECTIONS[index]
        ref, depth, (row_pad, col_pad) = layers[part]
        source = region(
            ref, window(step[0], depth, height, row_pad), window(step[1], depth, breadth, col_pad)
        )
        target = region(
            ref, landing(-step[0], depth, height, row_pad), landing(-step[1], depth, breadth, col_pad)
        )
        return pltpu.make_async_remote_copy(
            source, target, send_sem.at[index, part], recv_sem.at[count - 1 - index, part],
            device_id=(panel, colat + step[0], lon + step[1]), device_id_type=MESH,
        )

    def incoming(index, part):
        step = DIRECTIONS[index]
        ref, depth, (row_pad, col_pad) = layers[part]
        target = region(
            ref, landing(step[0], depth, height, row_pad), landing(step[1], depth, breadth, col_pad)
        )
        return pltpu.make_async_remote_copy(
            target, target, send_sem.at[index, part], recv_sem.at[index, part],
            device_id=(panel, colat + step[0], lon + step[1]), device_id_type=MESH,
        )

    barrier = pltpu.get_barrier_semaphore()
    expected = jnp.int32(0)
    for index, step in enumerate(DIRECTIONS):
        exists = present(step)
        expected = expected + exists.astype(jnp.int32)

        @pl.when(exists)
        def _():
            pl.semaphore_signal(
                barrier, 1, device_id=(panel, colat + step[0], lon + step[1]),
                device_id_type=MESH,
            )

    pl.semaphore_wait(barrier, expected)
    for index, step in enumerate(DIRECTIONS):

        @pl.when(present(step))
        def _():
            outgoing(index, 0).start()
            outgoing(index, 1).start()

    for index, step in enumerate(DIRECTIONS):

        @pl.when(present(step))
        def _():
            outgoing(index, 0).wait_send()
            outgoing(index, 1).wait_send()
            incoming(index, 0).wait_recv()
            incoming(index, 1).wait_recv()


def halo_exchange(fields, coefs, width):
    lane_pad = 8
    margins = ((width, lane_pad), (1, lane_pad))
    fields_pad = jnp.pad(fields, ((0, 0), (width, width), (lane_pad, lane_pad), (0, 0)))
    coefs_pad = jnp.pad(coefs, ((0, 0), (1, 1), (lane_pad, lane_pad), (0, 0)))
    anywhere = pl.BlockSpec(memory_space=pl.ANY)
    count = len(DIRECTIONS)
    fields_pad, coefs_pad = pl.pallas_call(
        functools.partial(halo_kernel, width, margins),
        out_shape=(
            jax.ShapeDtypeStruct(fields_pad.shape, fields_pad.dtype),
            jax.ShapeDtypeStruct(coefs_pad.shape, coefs_pad.dtype),
        ),
        in_specs=[anywhere, anywhere],
        out_specs=(anywhere, anywhere),
        scratch_shapes=[
            pltpu.SemaphoreType.DMA((count, 2)),
            pltpu.SemaphoreType.DMA((count, 2)),
        ],
        input_output_aliases={0: 0, 1: 1},
        compiler_params=pltpu.CompilerParams(collective_id=1, has_side_effects=True),
    )(fields_pad, coefs_pad)
    return fields_pad, coefs_pad


def gradient(stencil):
    return (8.0 * (stencil[3] - stencil[1]) - (stencil[4] - stencil[0])) / 12.0


def curvature(stencil):
    return (16.0 * (stencil[3] + stencil[1]) - (stencil[4] + stencil[0]) - 30.0 * stencil[2]) / 12.0


def shifted(block, step):
    size = block.shape[-1]
    lane = lax.broadcasted_iota(jnp.int32, block.shape, block.ndim - 1)
    moved = pltpu.roll(block, (size - step) % size, block.ndim - 1)
    keep = jnp.logical_and(lane + step >= 0, lane + step < size)
    return jnp.where(keep, moved, 0.0)


def stencil_kernel(row_pad, col_pad, fields_ref, coefs_ref, out_ref):
    colat = lax.axis_index("colat")
    lon = lax.axis_index("lon")
    colat_count = lax.axis_size("colat")
    lon_count = lax.axis_size("lon")
    ext_rows, span, radial_len = out_ref.shape[1], out_ref.shape[2], out_ref.shape[3]
    height = ext_rows - 2
    breadth = fields_ref.shape[2] - 2 * col_pad
    lead = (span - breadth) // 2
    col_ids = lax.broadcasted_iota(jnp.int32, (span, radial_len), 0) - lead + lon * breadth
    col_ok = jnp.logical_and(col_ids >= 0, col_ids < lon_count * breadth)

    def body(row, carry):
        global_row = row - 1 + colat * height
        ok = jnp.logical_and(col_ok, jnp.logical_and(global_row >= 0, global_row < colat_count * height))

        def load(field, down, across):
            return fields_ref[field, row + row_pad - 1 + down, pl.ds(col_pad - lead + across, span), :]

        center = [load(field, 0, 0) for field in range(4)]
        thermal = coefs_ref[0, row, pl.ds(col_pad - lead, span), :]
        viscous = coefs_ref[1, row, pl.ds(col_pad - lead, span), :]
        for field in range(4):
            along_lat = [load(field, offset - 2, 0) for offset in range(5)]
            along_lon = [load(field, 0, offset - 2) for offset in range(5)]
            along_rad = [shifted(center[field], offset - 2) for offset in range(5)]
            laplace = curvature(along_rad) + curvature(along_lat) + curvature(along_lon)
            transport = (
                center[1] * gradient(along_rad)
                + center[2] * gradient(along_lat)
                + center[3] * gradient(along_lon)
            )
            change = (thermal if field == 0 else viscous) * laplace - transport
            if field == 1:
                change = change + BUOYANCY * center[0]
            out_ref[field, row] = jnp.where(ok, center[field] + TIME_STEP * change, 0.0)
        return carry

    lax.fori_loop(0, ext_rows, body, 0)


def stepped(fields_pad, coefs_pad, row_pad, col_pad, lead):
    height = coefs_pad.shape[1] - 2
    breadth = fields_pad.shape[2] - 2 * col_pad
    span = breadth + 2 * lead
    vmem = pl.BlockSpec(memory_space=pltpu.VMEM)
    return pl.pallas_call(
        functools.partial(stencil_kernel, row_pad, col_pad),
        out_shape=jax.ShapeDtypeStruct(
            (4, height + 2, span, fields_pad.shape[3]), fields_pad.dtype
        ),
        in_specs=[vmem, vmem],
        out_specs=vmem,
    )(fields_pad, coefs_pad)


def advance(padded, thermal, viscous):
    height = padded.shape[1] - 4
    breadth = padded.shape[2] - 4
    center = padded[:, 2 : 2 + height, 2 : 2 + breadth]
    radial_len = center.shape[3]
    radial_pad = jnp.pad(center, ((0, 0), (0, 0), (0, 0), (2, 2)))
    along_lat = [padded[:, offset : offset + height, 2 : 2 + breadth] for offset in range(5)]
    along_lon = [padded[:, 2 : 2 + height, offset : offset + breadth] for offset in range(5)]
    along_rad = [radial_pad[..., offset : offset + radial_len] for offset in range(5)]
    laplace = curvature(along_rad) + curvature(along_lat) + curvature(along_lon)
    transport = (
        center[1:2] * gradient(along_rad)
        + center[2:3] * gradient(along_lat)
        + center[3:4] * gradient(along_lon)
    )
    diffusion = jnp.stack([thermal, viscous, viscous, viscous])
    change = diffusion * laplace - transport
    change = change.at[1].add(BUOYANCY * center[0])
    return center + TIME_STEP * change


def local(fields_now, diffusivity, viscosity, donor_row, donor_column, donor_offset, rim_angle):
    fields = fields_now[:, 0]
    thermal = diffusivity[0]
    viscous = viscosity[0]
    height = fields.shape[1]
    breadth = fields.shape[2]
    radial_len = fields.shape[3]
    colat_pos = lax.axis_index("colat")
    lon_pos = lax.axis_index("lon")
    colat_count = lax.axis_size("colat")
    lon_count = lax.axis_size("lon")
    row_share = 4 * breadth // colat_count
    coefs = jnp.concatenate([thermal[None], viscous[None]], axis=0)
    fields_pad, coefs_pad = halo_exchange(fields, coefs, 3)
    lead = 4
    extended = stepped(fields_pad, coefs_pad, 3, 8, lead)
    fresh = extended[:, 1 : 1 + height, lead : lead + breadth]
    width = extended.shape[2]
    flattened = extended.reshape(4, (height + 2) * width, radial_len)
    anchor = donor_row.reshape(-1) * width + donor_column.reshape(-1) + (lead - 1)

    def corner(offset):
        return jnp.take(flattened, anchor + offset, axis=1)

    frac_row = donor_offset[0, 0, 0, 0][None, :, None]
    frac_lon = donor_offset[0, 0, 0, 1][None, :, None]
    blended = (1.0 - frac_row) * (
        (1.0 - frac_lon) * corner(0) + frac_lon * corner(1)
    ) + frac_row * ((1.0 - frac_lon) * corner(width) + frac_lon * corner(width + 1))
    angles = rim_angle.reshape(-1)
    cosine = jnp.cos(angles)[:, None]
    sine_part = jnp.sin(angles)[:, None]
    turned_lat = cosine * blended[2] - sine_part * blended[3]
    turned_lon = sine_part * blended[2] + cosine * blended[3]
    blended = jnp.stack([blended[0], blended[1], turned_lat, turned_lon])
    row_buf, col_buf = rim_exchange(blended[:, 0:row_share], blended[:, row_share:])
    col_share = blended.shape[1] - row_share
    col_strip = col_buf.reshape(2, col_buf.shape[0] // 2, 4, col_share, radial_len)
    col_strip = jnp.transpose(col_strip, (2, 0, 1, 3, 4)).reshape(4, 2, height, radial_len)
    west_strip = jnp.transpose(col_strip, (0, 2, 1, 3))
    east_strip = jnp.stack([col_strip[:, 1], col_strip[:, 0]], axis=2)
    row_strip = row_buf.reshape(2, row_buf.shape[0] // 2, 4, row_share, radial_len)
    row_strip = jnp.transpose(row_strip, (2, 0, 1, 3, 4)).reshape(4, 2, breadth, radial_len)
    north_strip = row_strip
    south_strip = jnp.stack([row_strip[:, 1], row_strip[:, 0]], axis=1)
    gap_cols = jnp.zeros((4, height, breadth - 4, radial_len), fresh.dtype)
    col_rim = jnp.concatenate([west_strip, gap_cols, east_strip], axis=2)
    gap_rows = jnp.zeros((4, height - 4, breadth, radial_len), fresh.dtype)
    row_rim = jnp.concatenate([north_strip, gap_rows, south_strip], axis=1)
    row_ids = lax.broadcasted_iota(jnp.int32, (height, breadth), 0)
    col_ids = lax.broadcasted_iota(jnp.int32, (height, breadth), 1)
    use_col = ((lon_pos == 0) & (col_ids < 2)) | ((lon_pos == lon_count - 1) & (col_ids >= breadth - 2))
    use_row = ((colat_pos == 0) & (row_ids < 2)) | ((colat_pos == colat_count - 1) & (row_ids >= height - 2))
    fresh = jnp.where(use_col[None, :, :, None], col_rim, fresh)
    fresh = jnp.where(use_row[None, :, :, None], row_rim, fresh)
    return fresh[:, None]


def solution(mesh):
    placed = (
        P(None, "panel", "colat", "lon", None),
        P("panel", "colat", "lon", None),
        P("panel", "colat", "lon", None),
        P("panel", "colat", "lon", None),
        P("panel", "colat", "lon", None),
        P("panel", "colat", "lon", None, None),
        P("panel", "colat", "lon", None),
    )
    return jax.shard_map(
        local,
        mesh=mesh,
        in_specs=placed,
        out_specs=P(None, "panel", "colat", "lon", None),
        check_vma=False,
    )
```

```python
import functools

import jax
import jax.numpy as jnp
from jax import lax
from jax.sharding import PartitionSpec as P
from jax.experimental import pallas as pl
from jax.experimental.pallas import tpu as pltpu

MESH = pl.DeviceIdType.MESH

TIME_STEP = 0.05
BUOYANCY = 1.0


def with_halo(x, sides, width):
    for axis, dim in sides:
        count, length = (lax.axis_size(axis), x.shape[dim])
        up = [(i, (i + 1) % count) for i in range(count - 1)]
        down = [(j, i) for i, j in up]
        last = lax.slice_in_dim(x, length - width, length, axis=dim)
        leading = lax.slice_in_dim(x, 0, width, axis=dim)
        before = lax.ppermute(last, axis, up)
        after = lax.ppermute(leading, axis, down)
        x = jnp.concatenate([before, x, after], axis=dim)
    return x


def swapped(block, axis, stride):
    count = lax.axis_size(axis)
    route = []
    for low in range(count):
        high = low | 1 << stride
        if high != low and high < count:
            route += [(low, high), (high, low)]
    return lax.ppermute(block, axis, route)


def rim_kernel(row_ref, col_ref, row_out, col_out, send_sem, row_sem, col_sem):
    panel = lax.axis_index("panel")
    colat = lax.axis_index("colat")
    lon = lax.axis_index("lon")
    colat_count = lax.axis_size("colat")
    lon_count = lax.axis_size("lon")
    row_types = row_out.shape[0] // 2
    col_types = col_out.shape[0] // 2
    other = 1 - panel

    def route(share, per_type, count):
        kind = share // per_type
        edge = (kind % 2) * (count - 1)
        slot = (kind // 2) * per_type + share % per_type
        return edge, slot

    row_edge, row_slot = route(colat, row_types, colat_count)
    col_edge, col_slot = route(lon, col_types, lon_count)
    row_dest = (other, row_edge, lon)
    col_dest = (other, colat, col_edge)
    at_row_edge = jnp.logical_or(colat == 0, colat == colat_count - 1)
    at_col_edge = jnp.logical_or(lon == 0, lon == lon_count - 1)
    parity_row = (colat // (colat_count - 1)).astype(jnp.int32)
    parity_col = (lon // (lon_count - 1)).astype(jnp.int32)

    def row_sender(slot):
        kind = 2 * (slot // row_types) + parity_row
        return (other, kind * row_types + slot % row_types, lon)

    def col_sender(slot):
        kind = 2 * (slot // col_types) + parity_col
        return (other, colat, kind * col_types + slot % col_types)

    barrier = pltpu.get_barrier_semaphore()
    pl.semaphore_signal(barrier, 1, device_id=row_dest, device_id_type=MESH)
    pl.semaphore_signal(barrier, 1, device_id=col_dest, device_id_type=MESH)

    @pl.when(at_row_edge)
    def _():
        for slot in range(2 * row_types):
            pl.semaphore_signal(barrier, 1, device_id=row_sender(slot), device_id_type=MESH)

    @pl.when(at_col_edge)
    def _():
        for slot in range(2 * col_types):
            pl.semaphore_signal(barrier, 1, device_id=col_sender(slot), device_id_type=MESH)

    expected = (
        2
        + at_row_edge.astype(jnp.int32) * (2 * row_types)
        + at_col_edge.astype(jnp.int32) * (2 * col_types)
    )
    pl.semaphore_wait(barrier, expected)

    row_copy = pltpu.make_async_remote_copy(
        row_ref, row_out.at[row_slot], send_sem.at[0], row_sem.at[row_slot],
        device_id=row_dest, device_id_type=MESH,
    )
    col_copy = pltpu.make_async_remote_copy(
        col_ref, col_out.at[col_slot], send_sem.at[1], col_sem.at[col_slot],
        device_id=col_dest, device_id_type=MESH,
    )
    row_copy.start()
    col_copy.start()
    row_copy.wait_send()
    col_copy.wait_send()

    @pl.when(at_row_edge)
    def _():
        for slot in range(2 * row_types):
            pltpu.make_async_remote_copy(
                row_ref, row_out.at[slot], send_sem.at[0], row_sem.at[slot],
                device_id=row_sender(slot), device_id_type=MESH,
            ).wait_recv()

    @pl.when(at_col_edge)
    def _():
        for slot in range(2 * col_types):
            pltpu.make_async_remote_copy(
                col_ref, col_out.at[slot], send_sem.at[1], col_sem.at[slot],
                device_id=col_sender(slot), device_id_type=MESH,
            ).wait_recv()


def rim_exchange(rows, cols):
    colat_count = lax.axis_size("colat")
    lon_count = lax.axis_size("lon")
    row_types = colat_count // 4
    col_types = lon_count // 4
    vmem = pl.BlockSpec(memory_space=pltpu.VMEM)
    return pl.pallas_call(
        rim_kernel,
        out_shape=(
            jax.ShapeDtypeStruct((2 * row_types,) + rows.shape, rows.dtype),
            jax.ShapeDtypeStruct((2 * col_types,) + cols.shape, cols.dtype),
        ),
        in_specs=[vmem, vmem],
        out_specs=(vmem, vmem),
        scratch_shapes=[
            pltpu.SemaphoreType.DMA((2,)),
            pltpu.SemaphoreType.DMA((2 * row_types,)),
            pltpu.SemaphoreType.DMA((2 * col_types,)),
        ],
        compiler_params=pltpu.CompilerParams(collective_id=0, has_side_effects=True),
    )(rows, cols)


DIRECTIONS = ((-1, -1), (-1, 0), (-1, 1), (0, -1), (0, 1), (1, -1), (1, 0), (1, 1))


def window(step, width, length, offset):
    if step < 0:
        return offset, width
    if step > 0:
        return offset + length - width, width
    return offset, length


def landing(step, width, length, offset):
    if step < 0:
        return offset - width, width
    if step > 0:
        return offset + length, width
    return offset, length


def halo_kernel(width, margins, fields_in, coefs_in, fields_out, coefs_out, send_sem, recv_sem):
    del fields_in, coefs_in
    count = len(DIRECTIONS)
    panel = lax.axis_index("panel")
    colat = lax.axis_index("colat")
    lon = lax.axis_index("lon")
    colat_count = lax.axis_size("colat")
    lon_count = lax.axis_size("lon")
    height = fields_out.shape[1] - 2 * margins[0][0]
    breadth = fields_out.shape[2] - 2 * margins[0][1]
    layers = ((fields_out, width, margins[0]), (coefs_out, 1, margins[1]))

    def present(step):
        row = colat + step[0]
        col = lon + step[1]
        inside = jnp.logical_and(row >= 0, row < colat_count)
        return jnp.logical_and(inside, jnp.logical_and(col >= 0, col < lon_count))

    def region(ref, rows, cols):
        return ref.at[:, pl.ds(rows[0], rows[1]), pl.ds(cols[0], cols[1]), :]

    def outgoing(index, part):
        step = DIRECTIONS[index]
        ref, depth, (row_pad, col_pad) = layers[part]
        source = region(
            ref, window(step[0], depth, height, row_pad), window(step[1], depth, breadth, col_pad)
        )
        target = region(
            ref, landing(-step[0], depth, height, row_pad), landing(-step[1], depth, breadth, col_pad)
        )
        return pltpu.make_async_remote_copy(
            source, target, send_sem.at[index, part], recv_sem.at[count - 1 - index, part],
            device_id=(panel, colat + step[0], lon + step[1]), device_id_type=MESH,
        )

    def incoming(index, part):
        step = DIRECTIONS[index]
        ref, depth, (row_pad, col_pad) = layers[part]
        target = region(
            ref, landing(step[0], depth, height, row_pad), landing(step[1], depth, breadth, col_pad)
        )
        return pltpu.make_async_remote_copy(
            target, target, send_sem.at[index, part], recv_sem.at[index, part],
            device_id=(panel, colat + step[0], lon + step[1]), device_id_type=MESH,
        )

    barrier = pltpu.get_barrier_semaphore()
    expected = jnp.int32(0)
    for index, step in enumerate(DIRECTIONS):
        exists = present(step)
        expected = expected + exists.astype(jnp.int32)

        @pl.when(exists)
        def _():
            pl.semaphore_signal(
                barrier, 1, device_id=(panel, colat + step[0], lon + step[1]),
                device_id_type=MESH,
            )

    pl.semaphore_wait(barrier, expected)
    for index, step in enumerate(DIRECTIONS):

        @pl.when(present(step))
        def _():
            outgoing(index, 0).start()
            outgoing(index, 1).start()

    for index, step in enumerate(DIRECTIONS):

        @pl.when(present(step))
        def _():
            outgoing(index, 0).wait_send()
            outgoing(index, 1).wait_send()
            incoming(index, 0).wait_recv()
            incoming(index, 1).wait_recv()


def halo_exchange(fields, coefs, width):
    lane_pad = 8
    margins = ((width, lane_pad), (1, lane_pad))
    fields_pad = jnp.pad(fields, ((0, 0), (width, width), (lane_pad, lane_pad), (0, 0)))
    coefs_pad = jnp.pad(coefs, ((0, 0), (1, 1), (lane_pad, lane_pad), (0, 0)))
    anywhere = pl.BlockSpec(memory_space=pl.ANY)
    count = len(DIRECTIONS)
    fields_pad, coefs_pad = pl.pallas_call(
        functools.partial(halo_kernel, width, margins),
        out_shape=(
            jax.ShapeDtypeStruct(fields_pad.shape, fields_pad.dtype),
            jax.ShapeDtypeStruct(coefs_pad.shape, coefs_pad.dtype),
        ),
        in_specs=[anywhere, anywhere],
        out_specs=(anywhere, anywhere),
        scratch_shapes=[
            pltpu.SemaphoreType.DMA((count, 2)),
            pltpu.SemaphoreType.DMA((count, 2)),
        ],
        input_output_aliases={0: 0, 1: 1},
        compiler_params=pltpu.CompilerParams(collective_id=1, has_side_effects=True),
    )(fields_pad, coefs_pad)
    return fields_pad, coefs_pad


def gradient(stencil):
    return (8.0 * (stencil[3] - stencil[1]) - (stencil[4] - stencil[0])) / 12.0


def curvature(stencil):
    return (16.0 * (stencil[3] + stencil[1]) - (stencil[4] + stencil[0]) - 30.0 * stencil[2]) / 12.0


def shifted(block, step):
    size = block.shape[-1]
    lane = lax.broadcasted_iota(jnp.int32, block.shape, block.ndim - 1)
    moved = pltpu.roll(block, (size - step) % size, block.ndim - 1)
    keep = jnp.logical_and(lane + step >= 0, lane + step < size)
    return jnp.where(keep, moved, 0.0)


def step_kernel(
    row_pad, col_pad, fields_ref, coefs_ref, rows_ref, cols_ref, frac_ref, trig_ref,
    out_ref, row_out, col_out, row_send, col_send, send_sem, row_sem, col_sem,
):
    panel = lax.axis_index("panel")
    colat = lax.axis_index("colat")
    lon = lax.axis_index("lon")
    colat_count = lax.axis_size("colat")
    lon_count = lax.axis_size("lon")
    row_types = row_out.shape[0] // 2
    col_types = col_out.shape[0] // 2
    row_share = row_send.shape[1]
    other = 1 - panel

    def route(share, per_type, count):
        kind = share // per_type
        edge = (kind % 2) * (count - 1)
        slot = (kind // 2) * per_type + share % per_type
        return edge, slot

    row_edge, row_slot = route(colat, row_types, colat_count)
    col_edge, col_slot = route(lon, col_types, lon_count)
    row_dest = (other, row_edge, lon)
    col_dest = (other, colat, col_edge)
    at_row_edge = jnp.logical_or(colat == 0, colat == colat_count - 1)
    at_col_edge = jnp.logical_or(lon == 0, lon == lon_count - 1)
    parity_row = (colat // (colat_count - 1)).astype(jnp.int32)
    parity_col = (lon // (lon_count - 1)).astype(jnp.int32)

    def row_sender(slot):
        kind = 2 * (slot // row_types) + parity_row
        return (other, kind * row_types + slot % row_types, lon)

    def col_sender(slot):
        kind = 2 * (slot // col_types) + parity_col
        return (other, colat, kind * col_types + slot % col_types)

    barrier = pltpu.get_barrier_semaphore()
    pl.semaphore_signal(barrier, 1, device_id=row_dest, device_id_type=MESH)
    pl.semaphore_signal(barrier, 1, device_id=col_dest, device_id_type=MESH)

    @pl.when(at_row_edge)
    def _():
        for slot in range(2 * row_types):
            pl.semaphore_signal(barrier, 1, device_id=row_sender(slot), device_id_type=MESH)

    @pl.when(at_col_edge)
    def _():
        for slot in range(2 * col_types):
            pl.semaphore_signal(barrier, 1, device_id=col_sender(slot), device_id_type=MESH)

    ext_rows, span, radial_len = out_ref.shape[1], out_ref.shape[2], out_ref.shape[3]
    height = ext_rows - 2
    breadth = fields_ref.shape[2] - 2 * col_pad
    lead = (span - breadth) // 2
    col_ids = lax.broadcasted_iota(jnp.int32, (span, radial_len), 0) - lead + lon * breadth
    col_ok = jnp.logical_and(col_ids >= 0, col_ids < lon_count * breadth)

    def body(row, carry):
        global_row = row - 1 + colat * height
        ok = jnp.logical_and(col_ok, jnp.logical_and(global_row >= 0, global_row < colat_count * height))

        def load(field, down, across):
            return fields_ref[field, row + row_pad - 1 + down, pl.ds(col_pad - lead + across, span), :]

        center = [load(field, 0, 0) for field in range(4)]
        thermal = coefs_ref[0, row, pl.ds(col_pad - lead, span), :]
        viscous = coefs_ref[1, row, pl.ds(col_pad - lead, span), :]
        for field in range(4):
            along_lat = [load(field, offset - 2, 0) for offset in range(5)]
            along_lon = [load(field, 0, offset - 2) for offset in range(5)]
            along_rad = [shifted(center[field], offset - 2) for offset in range(5)]
            laplace = curvature(along_rad) + curvature(along_lat) + curvature(along_lon)
            transport = (
                center[1] * gradient(along_rad)
                + center[2] * gradient(along_lat)
                + center[3] * gradient(along_lon)
            )
            change = (thermal if field == 0 else viscous) * laplace - transport
            if field == 1:
                change = change + BUOYANCY * center[0]
            out_ref[field, row] = jnp.where(ok, center[field] + TIME_STEP * change, 0.0)
        return carry

    lax.fori_loop(0, ext_rows, body, 0)

    slots = rows_ref.shape[0]
    column = lax.broadcasted_iota(jnp.int32, (span, radial_len), 0)
    for slot in range(slots):
        first = rows_ref[slot]
        across = cols_ref[slot] + (lead - 1)
        frac_row = frac_ref[0, slot]
        frac_lon = frac_ref[1, slot]
        weight = jnp.where(
            column == across, 1.0 - frac_lon, jnp.where(column == across + 1, frac_lon, 0.0)
        )
        mixed = []
        for field in range(4):
            upper = jnp.sum(weight * out_ref[field, first], axis=0, keepdims=True)
            lower = jnp.sum(weight * out_ref[field, first + 1], axis=0, keepdims=True)
            mixed.append((1.0 - frac_row) * upper + frac_row * lower)
        cosine = trig_ref[0, slot]
        sine_part = trig_ref[1, slot]
        turned = [
            mixed[0],
            mixed[1],
            cosine * mixed[2] - sine_part * mixed[3],
            sine_part * mixed[2] + cosine * mixed[3],
        ]
        for field in range(4):
            if slot < row_share:
                row_send[field, pl.ds(slot, 1), :] = turned[field]
            else:
                col_send[field, pl.ds(slot - row_share, 1), :] = turned[field]

    expected = (
        2
        + at_row_edge.astype(jnp.int32) * (2 * row_types)
        + at_col_edge.astype(jnp.int32) * (2 * col_types)
    )
    pl.semaphore_wait(barrier, expected)

    row_copy = pltpu.make_async_remote_copy(
        row_send, row_out.at[row_slot], send_sem.at[0], row_sem.at[row_slot],
        device_id=row_dest, device_id_type=MESH,
    )
    col_copy = pltpu.make_async_remote_copy(
        col_send, col_out.at[col_slot], send_sem.at[1], col_sem.at[col_slot],
        device_id=col_dest, device_id_type=MESH,
    )
    row_copy.start()
    col_copy.start()
    row_copy.wait_send()
    col_copy.wait_send()

    @pl.when(at_row_edge)
    def _():
        for slot in range(2 * row_types):
            pltpu.make_async_remote_copy(
                row_send, row_out.at[slot], send_sem.at[0], row_sem.at[slot],
                device_id=row_sender(slot), device_id_type=MESH,
            ).wait_recv()

    @pl.when(at_col_edge)
    def _():
        for slot in range(2 * col_types):
            pltpu.make_async_remote_copy(
                col_send, col_out.at[slot], send_sem.at[1], col_sem.at[slot],
                device_id=col_sender(slot), device_id_type=MESH,
            ).wait_recv()


def stepped(fields_pad, coefs_pad, row_pad, col_pad, lead, rows, cols, frac, trig, row_share):
    height = coefs_pad.shape[1] - 2
    breadth = fields_pad.shape[2] - 2 * col_pad
    span = breadth + 2 * lead
    radial_len = fields_pad.shape[3]
    slots = rows.shape[0]
    row_types = lax.axis_size("colat") // 4
    col_types = lax.axis_size("lon") // 4
    dtype = fields_pad.dtype
    vmem = pl.BlockSpec(memory_space=pltpu.VMEM)
    smem = pl.BlockSpec(memory_space=pltpu.SMEM)
    return pl.pallas_call(
        functools.partial(step_kernel, row_pad, col_pad),
        out_shape=(
            jax.ShapeDtypeStruct((4, height + 2, span, radial_len), dtype),
            jax.ShapeDtypeStruct((2 * row_types, 4, row_share, radial_len), dtype),
            jax.ShapeDtypeStruct((2 * col_types, 4, slots - row_share, radial_len), dtype),
        ),
        in_specs=[vmem, vmem, smem, smem, smem, smem],
        out_specs=(vmem, vmem, vmem),
        scratch_shapes=[
            pltpu.VMEM((4, row_share, radial_len), dtype),
            pltpu.VMEM((4, slots - row_share, radial_len), dtype),
            pltpu.SemaphoreType.DMA((2,)),
            pltpu.SemaphoreType.DMA((2 * row_types,)),
            pltpu.SemaphoreType.DMA((2 * col_types,)),
        ],
        compiler_params=pltpu.CompilerParams(collective_id=0, has_side_effects=True),
    )(fields_pad, coefs_pad, rows, cols, frac, trig)


def advance(padded, thermal, viscous):
    height = padded.shape[1] - 4
    breadth = padded.shape[2] - 4
    center = padded[:, 2 : 2 + height, 2 : 2 + breadth]
    radial_len = center.shape[3]
    radial_pad = jnp.pad(center, ((0, 0), (0, 0), (0, 0), (2, 2)))
    along_lat = [padded[:, offset : offset + height, 2 : 2 + breadth] for offset in range(5)]
    along_lon = [padded[:, 2 : 2 + height, offset : offset + breadth] for offset in range(5)]
    along_rad = [radial_pad[..., offset : offset + radial_len] for offset in range(5)]
    laplace = curvature(along_rad) + curvature(along_lat) + curvature(along_lon)
    transport = (
        center[1:2] * gradient(along_rad)
        + center[2:3] * gradient(along_lat)
        + center[3:4] * gradient(along_lon)
    )
    diffusion = jnp.stack([thermal, viscous, viscous, viscous])
    change = diffusion * laplace - transport
    change = change.at[1].add(BUOYANCY * center[0])
    return center + TIME_STEP * change


def local(fields_now, diffusivity, viscosity, donor_row, donor_column, donor_offset, rim_angle):
    fields = fields_now[:, 0]
    thermal = diffusivity[0]
    viscous = viscosity[0]
    height = fields.shape[1]
    breadth = fields.shape[2]
    radial_len = fields.shape[3]
    colat_pos = lax.axis_index("colat")
    lon_pos = lax.axis_index("lon")
    colat_count = lax.axis_size("colat")
    lon_count = lax.axis_size("lon")
    row_share = 4 * breadth // colat_count
    coefs = jnp.concatenate([thermal[None], viscous[None]], axis=0)
    fields_pad, coefs_pad = halo_exchange(fields, coefs, 3)
    lead = 4
    angles = rim_angle.reshape(-1)
    trig = jnp.stack([jnp.cos(angles), jnp.sin(angles)])
    frac = donor_offset.reshape(2, -1)
    extended, row_buf, col_buf = stepped(
        fields_pad, coefs_pad, 3, 8, lead, donor_row.reshape(-1), donor_column.reshape(-1),
        frac, trig, row_share,
    )
    fresh = extended[:, 1 : 1 + height, lead : lead + breadth]
    slot_count = donor_row.shape[-1]
    col_share = slot_count - row_share
    col_strip = col_buf.reshape(2, col_buf.shape[0] // 2, 4, col_share, radial_len)
    col_strip = jnp.transpose(col_strip, (2, 0, 1, 3, 4)).reshape(4, 2, height, radial_len)
    west_strip = jnp.transpose(col_strip, (0, 2, 1, 3))
    east_strip = jnp.stack([col_strip[:, 1], col_strip[:, 0]], axis=2)
    row_strip = row_buf.reshape(2, row_buf.shape[0] // 2, 4, row_share, radial_len)
    row_strip = jnp.transpose(row_strip, (2, 0, 1, 3, 4)).reshape(4, 2, breadth, radial_len)
    north_strip = row_strip
    south_strip = jnp.stack([row_strip[:, 1], row_strip[:, 0]], axis=1)
    gap_cols = jnp.zeros((4, height, breadth - 4, radial_len), fresh.dtype)
    col_rim = jnp.concatenate([west_strip, gap_cols, east_strip], axis=2)
    gap_rows = jnp.zeros((4, height - 4, breadth, radial_len), fresh.dtype)
    row_rim = jnp.concatenate([north_strip, gap_rows, south_strip], axis=1)
    row_ids = lax.broadcasted_iota(jnp.int32, (height, breadth), 0)
    col_ids = lax.broadcasted_iota(jnp.int32, (height, breadth), 1)
    use_col = ((lon_pos == 0) & (col_ids < 2)) | ((lon_pos == lon_count - 1) & (col_ids >= breadth - 2))
    use_row = ((colat_pos == 0) & (row_ids < 2)) | ((colat_pos == colat_count - 1) & (row_ids >= height - 2))
    fresh = jnp.where(use_col[None, :, :, None], col_rim, fresh)
    fresh = jnp.where(use_row[None, :, :, None], row_rim, fresh)
    return fresh[:, None]


def solution(mesh):
    placed = (
        P(None, "panel", "colat", "lon", None),
        P("panel", "colat", "lon", None),
        P("panel", "colat", "lon", None),
        P("panel", "colat", "lon", None),
        P("panel", "colat", "lon", None),
        P("panel", "colat", "lon", None, None),
        P("panel", "colat", "lon", None),
    )
    return jax.shard_map(
        local,
        mesh=mesh,
        in_specs=placed,
        out_specs=P(None, "panel", "colat", "lon", None),
        check_vma=False,
    )
```

```python
import functools

import jax
import jax.numpy as jnp
from jax import lax
from jax.sharding import PartitionSpec as P
from jax.experimental import pallas as pl
from jax.experimental.pallas import tpu as pltpu

MESH = pl.DeviceIdType.MESH

TIME_STEP = 0.05
BUOYANCY = 1.0


def with_halo(x, sides, width):
    for axis, dim in sides:
        count, length = (lax.axis_size(axis), x.shape[dim])
        up = [(i, (i + 1) % count) for i in range(count - 1)]
        down = [(j, i) for i, j in up]
        last = lax.slice_in_dim(x, length - width, length, axis=dim)
        leading = lax.slice_in_dim(x, 0, width, axis=dim)
        before = lax.ppermute(last, axis, up)
        after = lax.ppermute(leading, axis, down)
        x = jnp.concatenate([before, x, after], axis=dim)
    return x


def swapped(block, axis, stride):
    count = lax.axis_size(axis)
    route = []
    for low in range(count):
        high = low | 1 << stride
        if high != low and high < count:
            route += [(low, high), (high, low)]
    return lax.ppermute(block, axis, route)


DIRECTIONS = ((-1, -1), (-1, 0), (-1, 1), (0, -1), (0, 1), (1, -1), (1, 0), (1, 1))


def window(step, width, length, offset):
    if step < 0:
        return offset, width
    if step > 0:
        return offset + length - width, width
    return offset, length


def landing(step, width, length, offset):
    if step < 0:
        return offset - width, width
    if step > 0:
        return offset + length, width
    return offset, length


def halo_kernel(width, margins, fields_in, coefs_in, fields_out, coefs_out, send_sem, recv_sem):
    del fields_in, coefs_in
    count = len(DIRECTIONS)
    panel = lax.axis_index("panel")
    colat = lax.axis_index("colat")
    lon = lax.axis_index("lon")
    colat_count = lax.axis_size("colat")
    lon_count = lax.axis_size("lon")
    height = fields_out.shape[1] - 2 * margins[0][0]
    breadth = fields_out.shape[2] - 2 * margins[0][1]
    layers = ((fields_out, width, margins[0]), (coefs_out, 1, margins[1]))

    def present(step):
        row = colat + step[0]
        col = lon + step[1]
        inside = jnp.logical_and(row >= 0, row < colat_count)
        return jnp.logical_and(inside, jnp.logical_and(col >= 0, col < lon_count))

    def region(ref, rows, cols):
        return ref.at[:, pl.ds(rows[0], rows[1]), pl.ds(cols[0], cols[1]), :]

    def outgoing(index, part):
        step = DIRECTIONS[index]
        ref, depth, (row_pad, col_pad) = layers[part]
        source = region(
            ref, window(step[0], depth, height, row_pad), window(step[1], depth, breadth, col_pad)
        )
        target = region(
            ref, landing(-step[0], depth, height, row_pad), landing(-step[1], depth, breadth, col_pad)
        )
        return pltpu.make_async_remote_copy(
            source, target, send_sem.at[index, part], recv_sem.at[count - 1 - index, part],
            device_id=(panel, colat + step[0], lon + step[1]), device_id_type=MESH,
        )

    def incoming(index, part):
        step = DIRECTIONS[index]
        ref, depth, (row_pad, col_pad) = layers[part]
        target = region(
            ref, landing(step[0], depth, height, row_pad), landing(step[1], depth, breadth, col_pad)
        )
        return pltpu.make_async_remote_copy(
            target, target, send_sem.at[index, part], recv_sem.at[index, part],
            device_id=(panel, colat + step[0], lon + step[1]), device_id_type=MESH,
        )

    barrier = pltpu.get_barrier_semaphore()
    expected = jnp.int32(0)
    for index, step in enumerate(DIRECTIONS):
        exists = present(step)
        expected = expected + exists.astype(jnp.int32)

        @pl.when(exists)
        def _():
            pl.semaphore_signal(
                barrier, 1, device_id=(panel, colat + step[0], lon + step[1]),
                device_id_type=MESH,
            )

    pl.semaphore_wait(barrier, expected)
    for index, step in enumerate(DIRECTIONS):

        @pl.when(present(step))
        def _():
            outgoing(index, 0).start()
            outgoing(index, 1).start()

    for index, step in enumerate(DIRECTIONS):

        @pl.when(present(step))
        def _():
            outgoing(index, 0).wait_send()
            outgoing(index, 1).wait_send()
            incoming(index, 0).wait_recv()
            incoming(index, 1).wait_recv()


def halo_exchange(fields, coefs, width):
    lane_pad = 8
    margins = ((width, lane_pad), (1, lane_pad))
    fields_pad = jnp.pad(fields, ((0, 0), (width, width), (lane_pad, lane_pad), (0, 0)))
    coefs_pad = jnp.pad(coefs, ((0, 0), (1, 1), (lane_pad, lane_pad), (0, 0)))
    anywhere = pl.BlockSpec(memory_space=pl.ANY)
    count = len(DIRECTIONS)
    fields_pad, coefs_pad = pl.pallas_call(
        functools.partial(halo_kernel, width, margins),
        out_shape=(
            jax.ShapeDtypeStruct(fields_pad.shape, fields_pad.dtype),
            jax.ShapeDtypeStruct(coefs_pad.shape, coefs_pad.dtype),
        ),
        in_specs=[anywhere, anywhere],
        out_specs=(anywhere, anywhere),
        scratch_shapes=[
            pltpu.SemaphoreType.DMA((count, 2)),
            pltpu.SemaphoreType.DMA((count, 2)),
        ],
        input_output_aliases={0: 0, 1: 1},
        compiler_params=pltpu.CompilerParams(collective_id=1, has_side_effects=True),
    )(fields_pad, coefs_pad)
    return fields_pad, coefs_pad


def gradient(stencil):
    return (8.0 * (stencil[3] - stencil[1]) - (stencil[4] - stencil[0])) / 12.0


def curvature(stencil):
    return (16.0 * (stencil[3] + stencil[1]) - (stencil[4] + stencil[0]) - 30.0 * stencil[2]) / 12.0


def shifted(block, step):
    size = block.shape[-1]
    lane = lax.broadcasted_iota(jnp.int32, block.shape, block.ndim - 1)
    moved = pltpu.roll(block, (size - step) % size, block.ndim - 1)
    keep = jnp.logical_and(lane + step >= 0, lane + step < size)
    return jnp.where(keep, moved, 0.0)


def step_kernel(
    row_pad, col_pad, fields_ref, coefs_ref, rows_ref, cols_ref, frac_ref, trig_ref,
    out_ref, final_ref, row_out, col_out, row_send, col_send, send_sem, row_sem, col_sem,
):
    panel = lax.axis_index("panel")
    colat = lax.axis_index("colat")
    lon = lax.axis_index("lon")
    colat_count = lax.axis_size("colat")
    lon_count = lax.axis_size("lon")
    row_types = row_out.shape[0] // 2
    col_types = col_out.shape[0] // 2
    row_share = row_send.shape[1]
    other = 1 - panel

    def route(share, per_type, count):
        kind = share // per_type
        edge = (kind % 2) * (count - 1)
        slot = (kind // 2) * per_type + share % per_type
        return edge, slot

    row_edge, row_slot = route(colat, row_types, colat_count)
    col_edge, col_slot = route(lon, col_types, lon_count)
    row_dest = (other, row_edge, lon)
    col_dest = (other, colat, col_edge)
    at_row_edge = jnp.logical_or(colat == 0, colat == colat_count - 1)
    at_col_edge = jnp.logical_or(lon == 0, lon == lon_count - 1)
    parity_row = (colat // (colat_count - 1)).astype(jnp.int32)
    parity_col = (lon // (lon_count - 1)).astype(jnp.int32)

    def row_sender(slot):
        kind = 2 * (slot // row_types) + parity_row
        return (other, kind * row_types + slot % row_types, lon)

    def col_sender(slot):
        kind = 2 * (slot // col_types) + parity_col
        return (other, colat, kind * col_types + slot % col_types)

    barrier = pltpu.get_barrier_semaphore()
    pl.semaphore_signal(barrier, 1, device_id=row_dest, device_id_type=MESH)
    pl.semaphore_signal(barrier, 1, device_id=col_dest, device_id_type=MESH)

    @pl.when(at_row_edge)
    def _():
        for slot in range(2 * row_types):
            pl.semaphore_signal(barrier, 1, device_id=row_sender(slot), device_id_type=MESH)

    @pl.when(at_col_edge)
    def _():
        for slot in range(2 * col_types):
            pl.semaphore_signal(barrier, 1, device_id=col_sender(slot), device_id_type=MESH)

    ext_rows, span, radial_len = out_ref.shape[1], out_ref.shape[2], out_ref.shape[3]
    height = ext_rows - 2
    breadth = fields_ref.shape[2] - 2 * col_pad
    lead = (span - breadth) // 2
    col_ids = lax.broadcasted_iota(jnp.int32, (span, radial_len), 0) - lead + lon * breadth
    col_ok = jnp.logical_and(col_ids >= 0, col_ids < lon_count * breadth)

    def body(row, carry):
        global_row = row - 1 + colat * height
        ok = jnp.logical_and(col_ok, jnp.logical_and(global_row >= 0, global_row < colat_count * height))

        def load(field, down, across):
            return fields_ref[field, row + row_pad - 1 + down, pl.ds(col_pad - lead + across, span), :]

        center = [load(field, 0, 0) for field in range(4)]
        thermal = coefs_ref[0, row, pl.ds(col_pad - lead, span), :]
        viscous = coefs_ref[1, row, pl.ds(col_pad - lead, span), :]
        for field in range(4):
            along_lat = [load(field, offset - 2, 0) for offset in range(5)]
            along_lon = [load(field, 0, offset - 2) for offset in range(5)]
            along_rad = [shifted(center[field], offset - 2) for offset in range(5)]
            laplace = curvature(along_rad) + curvature(along_lat) + curvature(along_lon)
            transport = (
                center[1] * gradient(along_rad)
                + center[2] * gradient(along_lat)
                + center[3] * gradient(along_lon)
            )
            change = (thermal if field == 0 else viscous) * laplace - transport
            if field == 1:
                change = change + BUOYANCY * center[0]
            out_ref[field, row] = jnp.where(ok, center[field] + TIME_STEP * change, 0.0)
        return carry

    lax.fori_loop(0, ext_rows, body, 0)
    for field in range(4):
        final_ref[field] = out_ref[field, pl.ds(1, height), pl.ds(lead, breadth), :]

    slots = rows_ref.shape[0]
    column = lax.broadcasted_iota(jnp.int32, (span, radial_len), 0)
    for slot in range(slots):
        first = rows_ref[slot]
        across = cols_ref[slot] + (lead - 1)
        frac_row = frac_ref[0, slot]
        frac_lon = frac_ref[1, slot]
        weight = jnp.where(
            column == across, 1.0 - frac_lon, jnp.where(column == across + 1, frac_lon, 0.0)
        )
        mixed = []
        for field in range(4):
            upper = jnp.sum(weight * out_ref[field, first], axis=0, keepdims=True)
            lower = jnp.sum(weight * out_ref[field, first + 1], axis=0, keepdims=True)
            mixed.append((1.0 - frac_row) * upper + frac_row * lower)
        cosine = trig_ref[0, slot]
        sine_part = trig_ref[1, slot]
        turned = [
            mixed[0],
            mixed[1],
            cosine * mixed[2] - sine_part * mixed[3],
            sine_part * mixed[2] + cosine * mixed[3],
        ]
        for field in range(4):
            if slot < row_share:
                row_send[field, pl.ds(slot, 1), :] = turned[field]
            else:
                col_send[field, pl.ds(slot - row_share, 1), :] = turned[field]

    expected = (
        2
        + at_row_edge.astype(jnp.int32) * (2 * row_types)
        + at_col_edge.astype(jnp.int32) * (2 * col_types)
    )
    pl.semaphore_wait(barrier, expected)

    row_copy = pltpu.make_async_remote_copy(
        row_send, row_out.at[row_slot], send_sem.at[0], row_sem.at[row_slot],
        device_id=row_dest, device_id_type=MESH,
    )
    col_copy = pltpu.make_async_remote_copy(
        col_send, col_out.at[col_slot], send_sem.at[1], col_sem.at[col_slot],
        device_id=col_dest, device_id_type=MESH,
    )
    row_copy.start()
    col_copy.start()
    row_copy.wait_send()
    col_copy.wait_send()

    @pl.when(at_row_edge)
    def _():
        for slot in range(2 * row_types):
            pltpu.make_async_remote_copy(
                row_send, row_out.at[slot], send_sem.at[0], row_sem.at[slot],
                device_id=row_sender(slot), device_id_type=MESH,
            ).wait_recv()

    @pl.when(at_col_edge)
    def _():
        for slot in range(2 * col_types):
            pltpu.make_async_remote_copy(
                col_send, col_out.at[slot], send_sem.at[1], col_sem.at[slot],
                device_id=col_sender(slot), device_id_type=MESH,
            ).wait_recv()

    col_share = col_out.shape[2]

    def put_columns(first, second):
        for slot in range(2 * col_types):
            column = first if slot < col_types else second
            base = (slot % col_types) * col_share
            for field in range(4):
                for offset in range(col_share):
                    final_ref[field, base + offset, pl.ds(column, 1), :] = (
                        col_out[slot, field, pl.ds(offset, 1), :]
                    )

    def put_rows(first, second):
        for slot in range(2 * row_types):
            line = first if slot < row_types else second
            base = (slot % row_types) * row_share
            for field in range(4):
                final_ref[field, line, pl.ds(base, row_share), :] = row_out[slot, field]

    @pl.when(lon == 0)
    def _():
        put_columns(0, 1)

    @pl.when(lon == lon_count - 1)
    def _():
        put_columns(breadth - 1, breadth - 2)

    @pl.when(colat == 0)
    def _():
        put_rows(0, 1)

    @pl.when(colat == colat_count - 1)
    def _():
        put_rows(height - 1, height - 2)


def stepped(fields_pad, coefs_pad, row_pad, col_pad, lead, rows, cols, frac, trig, row_share):
    height = coefs_pad.shape[1] - 2
    breadth = fields_pad.shape[2] - 2 * col_pad
    span = breadth + 2 * lead
    radial_len = fields_pad.shape[3]
    slots = rows.shape[0]
    row_types = lax.axis_size("colat") // 4
    col_types = lax.axis_size("lon") // 4
    dtype = fields_pad.dtype
    vmem = pl.BlockSpec(memory_space=pltpu.VMEM)
    smem = pl.BlockSpec(memory_space=pltpu.SMEM)
    return pl.pallas_call(
        functools.partial(step_kernel, row_pad, col_pad),
        out_shape=(
            jax.ShapeDtypeStruct((4, height + 2, span, radial_len), dtype),
            jax.ShapeDtypeStruct((4, height, breadth, radial_len), dtype),
            jax.ShapeDtypeStruct((2 * row_types, 4, row_share, radial_len), dtype),
            jax.ShapeDtypeStruct((2 * col_types, 4, slots - row_share, radial_len), dtype),
        ),
        in_specs=[vmem, vmem, smem, smem, smem, smem],
        out_specs=(vmem, vmem, vmem, vmem),
        scratch_shapes=[
            pltpu.VMEM((4, row_share, radial_len), dtype),
            pltpu.VMEM((4, slots - row_share, radial_len), dtype),
            pltpu.SemaphoreType.DMA((2,)),
            pltpu.SemaphoreType.DMA((2 * row_types,)),
            pltpu.SemaphoreType.DMA((2 * col_types,)),
        ],
        compiler_params=pltpu.CompilerParams(collective_id=0, has_side_effects=True),
    )(fields_pad, coefs_pad, rows, cols, frac, trig)


def advance(padded, thermal, viscous):
    height = padded.shape[1] - 4
    breadth = padded.shape[2] - 4
    center = padded[:, 2 : 2 + height, 2 : 2 + breadth]
    radial_len = center.shape[3]
    radial_pad = jnp.pad(center, ((0, 0), (0, 0), (0, 0), (2, 2)))
    along_lat = [padded[:, offset : offset + height, 2 : 2 + breadth] for offset in range(5)]
    along_lon = [padded[:, 2 : 2 + height, offset : offset + breadth] for offset in range(5)]
    along_rad = [radial_pad[..., offset : offset + radial_len] for offset in range(5)]
    laplace = curvature(along_rad) + curvature(along_lat) + curvature(along_lon)
    transport = (
        center[1:2] * gradient(along_rad)
        + center[2:3] * gradient(along_lat)
        + center[3:4] * gradient(along_lon)
    )
    diffusion = jnp.stack([thermal, viscous, viscous, viscous])
    change = diffusion * laplace - transport
    change = change.at[1].add(BUOYANCY * center[0])
    return center + TIME_STEP * change


def local(fields_now, diffusivity, viscosity, donor_row, donor_column, donor_offset, rim_angle):
    fields = fields_now[:, 0]
    thermal = diffusivity[0]
    viscous = viscosity[0]
    height = fields.shape[1]
    breadth = fields.shape[2]
    radial_len = fields.shape[3]
    colat_pos = lax.axis_index("colat")
    lon_pos = lax.axis_index("lon")
    colat_count = lax.axis_size("colat")
    lon_count = lax.axis_size("lon")
    row_share = 4 * breadth // colat_count
    coefs = jnp.concatenate([thermal[None], viscous[None]], axis=0)
    fields_pad, coefs_pad = halo_exchange(fields, coefs, 3)
    lead = 4
    angles = rim_angle.reshape(-1)
    trig = jnp.stack([jnp.cos(angles), jnp.sin(angles)])
    frac = donor_offset.reshape(2, -1)
    extended, fresh, row_buf, col_buf = stepped(
        fields_pad, coefs_pad, 3, 8, lead, donor_row.reshape(-1), donor_column.reshape(-1),
        frac, trig, row_share,
    )
    return fresh[:, None]


def solution(mesh):
    placed = (
        P(None, "panel", "colat", "lon", None),
        P("panel", "colat", "lon", None),
        P("panel", "colat", "lon", None),
        P("panel", "colat", "lon", None),
        P("panel", "colat", "lon", None),
        P("panel", "colat", "lon", None, None),
        P("panel", "colat", "lon", None),
    )
    return jax.shard_map(
        local,
        mesh=mesh,
        in_specs=placed,
        out_specs=P(None, "panel", "colat", "lon", None),
        check_vma=False,
    )
```

```python
import functools

import jax
import jax.numpy as jnp
from jax import lax
from jax.sharding import PartitionSpec as P
from jax.experimental import pallas as pl
from jax.experimental.pallas import tpu as pltpu

MESH = pl.DeviceIdType.MESH

TIME_STEP = 0.05
BUOYANCY = 1.0


def with_halo(x, sides, width):
    for axis, dim in sides:
        count, length = (lax.axis_size(axis), x.shape[dim])
        up = [(i, (i + 1) % count) for i in range(count - 1)]
        down = [(j, i) for i, j in up]
        last = lax.slice_in_dim(x, length - width, length, axis=dim)
        leading = lax.slice_in_dim(x, 0, width, axis=dim)
        before = lax.ppermute(last, axis, up)
        after = lax.ppermute(leading, axis, down)
        x = jnp.concatenate([before, x, after], axis=dim)
    return x


def swapped(block, axis, stride):
    count = lax.axis_size(axis)
    route = []
    for low in range(count):
        high = low | 1 << stride
        if high != low and high < count:
            route += [(low, high), (high, low)]
    return lax.ppermute(block, axis, route)


DIRECTIONS = ((-1, -1), (-1, 0), (-1, 1), (0, -1), (0, 1), (1, -1), (1, 0), (1, 1))


def window(step, width, length, offset):
    if step < 0:
        return offset, width
    if step > 0:
        return offset + length - width, width
    return offset, length


def landing(step, width, length, offset):
    if step < 0:
        return offset - width, width
    if step > 0:
        return offset + length, width
    return offset, length


def halo_kernel(width, margins, fields_in, coefs_in, fields_out, coefs_out, send_sem, recv_sem):
    del fields_in, coefs_in
    count = len(DIRECTIONS)
    panel = lax.axis_index("panel")
    colat = lax.axis_index("colat")
    lon = lax.axis_index("lon")
    colat_count = lax.axis_size("colat")
    lon_count = lax.axis_size("lon")
    height = fields_out.shape[1] - 2 * margins[0][0]
    breadth = fields_out.shape[2] - 2 * margins[0][1]
    layers = ((fields_out, width, margins[0]), (coefs_out, 1, margins[1]))

    def present(step):
        row = colat + step[0]
        col = lon + step[1]
        inside = jnp.logical_and(row >= 0, row < colat_count)
        return jnp.logical_and(inside, jnp.logical_and(col >= 0, col < lon_count))

    def region(ref, rows, cols):
        return ref.at[:, pl.ds(rows[0], rows[1]), pl.ds(cols[0], cols[1]), :]

    def outgoing(index, part):
        step = DIRECTIONS[index]
        ref, depth, (row_pad, col_pad) = layers[part]
        source = region(
            ref, window(step[0], depth, height, row_pad), window(step[1], depth, breadth, col_pad)
        )
        target = region(
            ref, landing(-step[0], depth, height, row_pad), landing(-step[1], depth, breadth, col_pad)
        )
        return pltpu.make_async_remote_copy(
            source, target, send_sem.at[index, part], recv_sem.at[count - 1 - index, part],
            device_id=(panel, colat + step[0], lon + step[1]), device_id_type=MESH,
        )

    def incoming(index, part):
        step = DIRECTIONS[index]
        ref, depth, (row_pad, col_pad) = layers[part]
        target = region(
            ref, landing(step[0], depth, height, row_pad), landing(step[1], depth, breadth, col_pad)
        )
        return pltpu.make_async_remote_copy(
            target, target, send_sem.at[index, part], recv_sem.at[index, part],
            device_id=(panel, colat + step[0], lon + step[1]), device_id_type=MESH,
        )

    barrier = pltpu.get_barrier_semaphore()
    expected = jnp.int32(0)
    for index, step in enumerate(DIRECTIONS):
        exists = present(step)
        expected = expected + exists.astype(jnp.int32)

        @pl.when(exists)
        def _():
            pl.semaphore_signal(
                barrier, 1, device_id=(panel, colat + step[0], lon + step[1]),
                device_id_type=MESH,
            )

    pl.semaphore_wait(barrier, expected)
    for index, step in enumerate(DIRECTIONS):

        @pl.when(present(step))
        def _():
            outgoing(index, 0).start()
            outgoing(index, 1).start()

    for index, step in enumerate(DIRECTIONS):

        @pl.when(present(step))
        def _():
            outgoing(index, 0).wait_send()
            outgoing(index, 1).wait_send()
            incoming(index, 0).wait_recv()
            incoming(index, 1).wait_recv()


def halo_exchange(fields, coefs, width):
    lane_pad = 8
    margins = ((width, lane_pad), (1, lane_pad))
    fields_pad = jnp.pad(fields, ((0, 0), (width, width), (lane_pad, lane_pad), (0, 0)))
    coefs_pad = jnp.pad(coefs, ((0, 0), (1, 1), (lane_pad, lane_pad), (0, 0)))
    anywhere = pl.BlockSpec(memory_space=pl.ANY)
    count = len(DIRECTIONS)
    fields_pad, coefs_pad = pl.pallas_call(
        functools.partial(halo_kernel, width, margins),
        out_shape=(
            jax.ShapeDtypeStruct(fields_pad.shape, fields_pad.dtype),
            jax.ShapeDtypeStruct(coefs_pad.shape, coefs_pad.dtype),
        ),
        in_specs=[anywhere, anywhere],
        out_specs=(anywhere, anywhere),
        scratch_shapes=[
            pltpu.SemaphoreType.DMA((count, 2)),
            pltpu.SemaphoreType.DMA((count, 2)),
        ],
        input_output_aliases={0: 0, 1: 1},
        compiler_params=pltpu.CompilerParams(collective_id=1, has_side_effects=True),
    )(fields_pad, coefs_pad)
    return fields_pad, coefs_pad


def gradient(stencil):
    return (8.0 * (stencil[3] - stencil[1]) - (stencil[4] - stencil[0])) / 12.0


def curvature(stencil):
    return (16.0 * (stencil[3] + stencil[1]) - (stencil[4] + stencil[0]) - 30.0 * stencil[2]) / 12.0


def slope(stencil):
    return 8.0 * (stencil[3] - stencil[1]) - (stencil[4] - stencil[0])


def spread(stencil):
    return 16.0 * (stencil[3] + stencil[1]) - (stencil[4] + stencil[0]) - 30.0 * stencil[2]


def shifted(block, step):
    size = block.shape[-1]
    lane = lax.broadcasted_iota(jnp.int32, block.shape, block.ndim - 1)
    moved = pltpu.roll(block, (size - step) % size, block.ndim - 1)
    keep = jnp.logical_and(lane + step >= 0, lane + step < size)
    return jnp.where(keep, moved, 0.0)


def step_kernel(
    row_pad, col_pad, fields_ref, coefs_ref, rows_ref, cols_ref, frac_ref, trig_ref,
    out_ref, final_ref, row_out, col_out, row_send, col_send, send_sem, row_sem, col_sem,
):
    panel = lax.axis_index("panel")
    colat = lax.axis_index("colat")
    lon = lax.axis_index("lon")
    colat_count = lax.axis_size("colat")
    lon_count = lax.axis_size("lon")
    row_types = row_out.shape[0] // 2
    col_types = col_out.shape[0] // 2
    row_share = row_send.shape[1]
    other = 1 - panel

    def route(share, per_type, count):
        kind = share // per_type
        edge = (kind % 2) * (count - 1)
        slot = (kind // 2) * per_type + share % per_type
        return edge, slot

    row_edge, row_slot = route(colat, row_types, colat_count)
    col_edge, col_slot = route(lon, col_types, lon_count)
    row_dest = (other, row_edge, lon)
    col_dest = (other, colat, col_edge)
    at_row_edge = jnp.logical_or(colat == 0, colat == colat_count - 1)
    at_col_edge = jnp.logical_or(lon == 0, lon == lon_count - 1)
    parity_row = (colat // (colat_count - 1)).astype(jnp.int32)
    parity_col = (lon // (lon_count - 1)).astype(jnp.int32)

    def row_sender(slot):
        kind = 2 * (slot // row_types) + parity_row
        return (other, kind * row_types + slot % row_types, lon)

    def col_sender(slot):
        kind = 2 * (slot // col_types) + parity_col
        return (other, colat, kind * col_types + slot % col_types)

    barrier = pltpu.get_barrier_semaphore()
    pl.semaphore_signal(barrier, 1, device_id=row_dest, device_id_type=MESH)
    pl.semaphore_signal(barrier, 1, device_id=col_dest, device_id_type=MESH)

    @pl.when(at_row_edge)
    def _():
        for slot in range(2 * row_types):
            pl.semaphore_signal(barrier, 1, device_id=row_sender(slot), device_id_type=MESH)

    @pl.when(at_col_edge)
    def _():
        for slot in range(2 * col_types):
            pl.semaphore_signal(barrier, 1, device_id=col_sender(slot), device_id_type=MESH)

    ext_rows, span, radial_len = out_ref.shape[1], out_ref.shape[2], out_ref.shape[3]
    height = ext_rows - 2
    breadth = fields_ref.shape[2] - 2 * col_pad
    lead = (span - breadth) // 2
    col_ids = lax.broadcasted_iota(jnp.int32, (span, radial_len), 0) - lead + lon * breadth
    col_ok = jnp.logical_and(col_ids >= 0, col_ids < lon_count * breadth)

    def body(row, carry):
        global_row = row - 1 + colat * height
        ok = jnp.logical_and(col_ok, jnp.logical_and(global_row >= 0, global_row < colat_count * height))

        def load(field, down, across):
            return fields_ref[field, row + row_pad - 1 + down, pl.ds(col_pad - lead + across, span), :]

        center = [load(field, 0, 0) for field in range(4)]
        thermal = coefs_ref[0, row, pl.ds(col_pad - lead, span), :]
        viscous = coefs_ref[1, row, pl.ds(col_pad - lead, span), :]
        for field in range(4):
            along_lat = [load(field, offset - 2, 0) for offset in range(5)]
            along_lon = [load(field, 0, offset - 2) for offset in range(5)]
            along_rad = [shifted(center[field], offset - 2) for offset in range(5)]
            laplace = spread(along_rad) + spread(along_lat) + spread(along_lon)
            transport = (
                center[1] * slope(along_rad)
                + center[2] * slope(along_lat)
                + center[3] * slope(along_lon)
            )
            change = (thermal if field == 0 else viscous) * laplace - transport
            stepped_value = center[field] + (TIME_STEP / 12.0) * change
            if field == 1:
                stepped_value = stepped_value + (TIME_STEP * BUOYANCY) * center[0]
            out_ref[field, row] = jnp.where(ok, stepped_value, 0.0)
        return carry

    lax.fori_loop(0, ext_rows, body, 0)
    for field in range(4):
        final_ref[field] = out_ref[field, pl.ds(1, height), pl.ds(lead, breadth), :]

    slots = rows_ref.shape[0]
    column = lax.broadcasted_iota(jnp.int32, (span, radial_len), 0)
    for slot in range(slots):
        first = rows_ref[slot]
        across = cols_ref[slot] + (lead - 1)
        frac_row = frac_ref[0, slot]
        frac_lon = frac_ref[1, slot]
        weight = jnp.where(
            column == across, 1.0 - frac_lon, jnp.where(column == across + 1, frac_lon, 0.0)
        )
        mixed = []
        for field in range(4):
            upper = jnp.sum(weight * out_ref[field, first], axis=0, keepdims=True)
            lower = jnp.sum(weight * out_ref[field, first + 1], axis=0, keepdims=True)
            mixed.append((1.0 - frac_row) * upper + frac_row * lower)
        cosine = trig_ref[0, slot]
        sine_part = trig_ref[1, slot]
        turned = [
            mixed[0],
            mixed[1],
            cosine * mixed[2] - sine_part * mixed[3],
            sine_part * mixed[2] + cosine * mixed[3],
        ]
        for field in range(4):
            if slot < row_share:
                row_send[field, pl.ds(slot, 1), :] = turned[field]
            else:
                col_send[field, pl.ds(slot - row_share, 1), :] = turned[field]

    expected = (
        2
        + at_row_edge.astype(jnp.int32) * (2 * row_types)
        + at_col_edge.astype(jnp.int32) * (2 * col_types)
    )
    pl.semaphore_wait(barrier, expected)

    row_copy = pltpu.make_async_remote_copy(
        row_send, row_out.at[row_slot], send_sem.at[0], row_sem.at[row_slot],
        device_id=row_dest, device_id_type=MESH,
    )
    col_copy = pltpu.make_async_remote_copy(
        col_send, col_out.at[col_slot], send_sem.at[1], col_sem.at[col_slot],
        device_id=col_dest, device_id_type=MESH,
    )
    row_copy.start()
    col_copy.start()
    row_copy.wait_send()
    col_copy.wait_send()

    @pl.when(at_row_edge)
    def _():
        for slot in range(2 * row_types):
            pltpu.make_async_remote_copy(
                row_send, row_out.at[slot], send_sem.at[0], row_sem.at[slot],
                device_id=row_sender(slot), device_id_type=MESH,
            ).wait_recv()

    @pl.when(at_col_edge)
    def _():
        for slot in range(2 * col_types):
            pltpu.make_async_remote_copy(
                col_send, col_out.at[slot], send_sem.at[1], col_sem.at[slot],
                device_id=col_sender(slot), device_id_type=MESH,
            ).wait_recv()

    col_share = col_out.shape[2]

    def put_columns(first, second):
        for slot in range(2 * col_types):
            column = first if slot < col_types else second
            base = (slot % col_types) * col_share
            for field in range(4):
                for offset in range(col_share):
                    final_ref[field, base + offset, pl.ds(column, 1), :] = (
                        col_out[slot, field, pl.ds(offset, 1), :]
                    )

    def put_rows(first, second):
        for slot in range(2 * row_types):
            line = first if slot < row_types else second
            base = (slot % row_types) * row_share
            for field in range(4):
                final_ref[field, line, pl.ds(base, row_share), :] = row_out[slot, field]

    @pl.when(lon == 0)
    def _():
        put_columns(0, 1)

    @pl.when(lon == lon_count - 1)
    def _():
        put_columns(breadth - 1, breadth - 2)

    @pl.when(colat == 0)
    def _():
        put_rows(0, 1)

    @pl.when(colat == colat_count - 1)
    def _():
        put_rows(height - 1, height - 2)


def stepped(fields_pad, coefs_pad, row_pad, col_pad, lead, rows, cols, frac, trig, row_share):
    height = coefs_pad.shape[1] - 2
    breadth = fields_pad.shape[2] - 2 * col_pad
    span = breadth + 2 * lead
    radial_len = fields_pad.shape[3]
    slots = rows.shape[0]
    row_types = lax.axis_size("colat") // 4
    col_types = lax.axis_size("lon") // 4
    dtype = fields_pad.dtype
    vmem = pl.BlockSpec(memory_space=pltpu.VMEM)
    smem = pl.BlockSpec(memory_space=pltpu.SMEM)
    return pl.pallas_call(
        functools.partial(step_kernel, row_pad, col_pad),
        out_shape=(
            jax.ShapeDtypeStruct((4, height + 2, span, radial_len), dtype),
            jax.ShapeDtypeStruct((4, height, breadth, radial_len), dtype),
            jax.ShapeDtypeStruct((2 * row_types, 4, row_share, radial_len), dtype),
            jax.ShapeDtypeStruct((2 * col_types, 4, slots - row_share, radial_len), dtype),
        ),
        in_specs=[vmem, vmem, smem, smem, smem, smem],
        out_specs=(vmem, vmem, vmem, vmem),
        scratch_shapes=[
            pltpu.VMEM((4, row_share, radial_len), dtype),
            pltpu.VMEM((4, slots - row_share, radial_len), dtype),
            pltpu.SemaphoreType.DMA((2,)),
            pltpu.SemaphoreType.DMA((2 * row_types,)),
            pltpu.SemaphoreType.DMA((2 * col_types,)),
        ],
        compiler_params=pltpu.CompilerParams(collective_id=0, has_side_effects=True),
    )(fields_pad, coefs_pad, rows, cols, frac, trig)


def advance(padded, thermal, viscous):
    height = padded.shape[1] - 4
    breadth = padded.shape[2] - 4
    center = padded[:, 2 : 2 + height, 2 : 2 + breadth]
    radial_len = center.shape[3]
    radial_pad = jnp.pad(center, ((0, 0), (0, 0), (0, 0), (2, 2)))
    along_lat = [padded[:, offset : offset + height, 2 : 2 + breadth] for offset in range(5)]
    along_lon = [padded[:, 2 : 2 + height, offset : offset + breadth] for offset in range(5)]
    along_rad = [radial_pad[..., offset : offset + radial_len] for offset in range(5)]
    laplace = curvature(along_rad) + curvature(along_lat) + curvature(along_lon)
    transport = (
        center[1:2] * gradient(along_rad)
        + center[2:3] * gradient(along_lat)
        + center[3:4] * gradient(along_lon)
    )
    diffusion = jnp.stack([thermal, viscous, viscous, viscous])
    change = diffusion * laplace - transport
    change = change.at[1].add(BUOYANCY * center[0])
    return center + TIME_STEP * change


def local(fields_now, diffusivity, viscosity, donor_row, donor_column, donor_offset, rim_angle):
    fields = fields_now[:, 0]
    thermal = diffusivity[0]
    viscous = viscosity[0]
    height = fields.shape[1]
    breadth = fields.shape[2]
    radial_len = fields.shape[3]
    colat_pos = lax.axis_index("colat")
    lon_pos = lax.axis_index("lon")
    colat_count = lax.axis_size("colat")
    lon_count = lax.axis_size("lon")
    row_share = 4 * breadth // colat_count
    coefs = jnp.concatenate([thermal[None], viscous[None]], axis=0)
    fields_pad, coefs_pad = halo_exchange(fields, coefs, 3)
    lead = 4
    angles = rim_angle.reshape(-1)
    trig = jnp.stack([jnp.cos(angles), jnp.sin(angles)])
    frac = donor_offset.reshape(2, -1)
    extended, fresh, row_buf, col_buf = stepped(
        fields_pad, coefs_pad, 3, 8, lead, donor_row.reshape(-1), donor_column.reshape(-1),
        frac, trig, row_share,
    )
    return fresh[:, None]


def solution(mesh):
    placed = (
        P(None, "panel", "colat", "lon", None),
        P("panel", "colat", "lon", None),
        P("panel", "colat", "lon", None),
        P("panel", "colat", "lon", None),
        P("panel", "colat", "lon", None),
        P("panel", "colat", "lon", None, None),
        P("panel", "colat", "lon", None),
    )
    return jax.shard_map(
        local,
        mesh=mesh,
        in_specs=placed,
        out_specs=P(None, "panel", "colat", "lon", None),
        check_vma=False,
    )
```

```python
import functools

import jax
import jax.numpy as jnp
from jax import lax
from jax.sharding import PartitionSpec as P
from jax.experimental import pallas as pl
from jax.experimental.pallas import tpu as pltpu

MESH = pl.DeviceIdType.MESH

TIME_STEP = 0.05
BUOYANCY = 1.0


def with_halo(x, sides, width):
    for axis, dim in sides:
        count, length = (lax.axis_size(axis), x.shape[dim])
        up = [(i, (i + 1) % count) for i in range(count - 1)]
        down = [(j, i) for i, j in up]
        last = lax.slice_in_dim(x, length - width, length, axis=dim)
        leading = lax.slice_in_dim(x, 0, width, axis=dim)
        before = lax.ppermute(last, axis, up)
        after = lax.ppermute(leading, axis, down)
        x = jnp.concatenate([before, x, after], axis=dim)
    return x


def swapped(block, axis, stride):
    count = lax.axis_size(axis)
    route = []
    for low in range(count):
        high = low | 1 << stride
        if high != low and high < count:
            route += [(low, high), (high, low)]
    return lax.ppermute(block, axis, route)


DIRECTIONS = ((-1, -1), (-1, 0), (-1, 1), (0, -1), (0, 1), (1, -1), (1, 0), (1, 1))


def window(step, width, length, offset):
    if step < 0:
        return offset, width
    if step > 0:
        return offset + length - width, width
    return offset, length


def landing(step, width, length, offset):
    if step < 0:
        return offset - width, width
    if step > 0:
        return offset + length, width
    return offset, length


def halo_kernel(width, margins, fields_in, thermal_in, viscous_in, fields_out, coefs_out, send_sem, recv_sem):
    count = len(DIRECTIONS)
    panel = lax.axis_index("panel")
    colat = lax.axis_index("colat")
    lon = lax.axis_index("lon")
    colat_count = lax.axis_size("colat")
    lon_count = lax.axis_size("lon")
    height, breadth = fields_in.shape[1], fields_in.shape[2]

    for out, (row_pad, col_pad) in ((fields_out, margins[0]), (coefs_out, margins[1])):
        lead = out.shape[:1]
        total_rows, total_cols = out.shape[1], out.shape[2]
        out[:, pl.ds(0, row_pad)] = jnp.zeros(lead + (row_pad, total_cols, out.shape[3]), out.dtype)
        out[:, pl.ds(row_pad + height, row_pad)] = jnp.zeros(
            lead + (row_pad, total_cols, out.shape[3]), out.dtype
        )
        side = jnp.zeros(lead + (height, col_pad, out.shape[3]), out.dtype)
        out[:, pl.ds(row_pad, height), pl.ds(0, col_pad)] = side
        out[:, pl.ds(row_pad, height), pl.ds(col_pad + breadth, total_cols - col_pad - breadth)] = side
    fields_out[:, pl.ds(margins[0][0], height), pl.ds(margins[0][1], breadth)] = fields_in[...]
    coefs_out[0, pl.ds(margins[1][0], height), pl.ds(margins[1][1], breadth)] = thermal_in[...]
    coefs_out[1, pl.ds(margins[1][0], height), pl.ds(margins[1][1], breadth)] = viscous_in[...]

    def present(step):
        row = colat + step[0]
        col = lon + step[1]
        inside = jnp.logical_and(row >= 0, row < colat_count)
        return jnp.logical_and(inside, jnp.logical_and(col >= 0, col < lon_count))

    def source(part, step):
        depth = width if part == 0 else 1
        rows = window(step[0], depth, height, 0)
        cols = window(step[1], depth, breadth, 0)
        ref = (fields_in, thermal_in, viscous_in)[part]
        if part == 0:
            return ref.at[:, pl.ds(rows[0], rows[1]), pl.ds(cols[0], cols[1]), :]
        return ref.at[pl.ds(rows[0], rows[1]), pl.ds(cols[0], cols[1]), :]

    def target(part, step):
        depth = width if part == 0 else 1
        row_pad, col_pad = margins[0] if part == 0 else margins[1]
        rows = landing(step[0], depth, height, row_pad)
        cols = landing(step[1], depth, breadth, col_pad)
        if part == 0:
            return fields_out.at[:, pl.ds(rows[0], rows[1]), pl.ds(cols[0], cols[1]), :]
        return coefs_out.at[part - 1, pl.ds(rows[0], rows[1]), pl.ds(cols[0], cols[1]), :]

    def outgoing(index, part):
        step = DIRECTIONS[index]
        back = tuple(-s for s in step)
        return pltpu.make_async_remote_copy(
            source(part, step), target(part, back),
            send_sem.at[index, part], recv_sem.at[count - 1 - index, part],
            device_id=(panel, colat + step[0], lon + step[1]), device_id_type=MESH,
        )

    def incoming(index, part):
        step = DIRECTIONS[index]
        spot = target(part, step)
        return pltpu.make_async_remote_copy(
            spot, spot, send_sem.at[index, part], recv_sem.at[index, part],
            device_id=(panel, colat + step[0], lon + step[1]), device_id_type=MESH,
        )

    barrier = pltpu.get_barrier_semaphore()
    expected = jnp.int32(0)
    for index, step in enumerate(DIRECTIONS):
        exists = present(step)
        expected = expected + exists.astype(jnp.int32)

        @pl.when(exists)
        def _():
            pl.semaphore_signal(
                barrier, 1, device_id=(panel, colat + step[0], lon + step[1]),
                device_id_type=MESH,
            )

    pl.semaphore_wait(barrier, expected)
    for index, step in enumerate(DIRECTIONS):

        @pl.when(present(step))
        def _():
            for part in range(3):
                outgoing(index, part).start()

    for index, step in enumerate(DIRECTIONS):

        @pl.when(present(step))
        def _():
            for part in range(3):
                outgoing(index, part).wait_send()
            for part in range(3):
                incoming(index, part).wait_recv()


def halo_exchange(fields, thermal, viscous, width):
    lane_pad = 8
    height, breadth, radial_len = fields.shape[1], fields.shape[2], fields.shape[3]
    margins = ((width, lane_pad), (1, lane_pad))
    vmem = pl.BlockSpec(memory_space=pltpu.VMEM)
    count = len(DIRECTIONS)
    return pl.pallas_call(
        functools.partial(halo_kernel, width, margins),
        out_shape=(
            jax.ShapeDtypeStruct(
                (4, height + 2 * width, breadth + 2 * lane_pad, radial_len), fields.dtype
            ),
            jax.ShapeDtypeStruct((2, height + 2, breadth + 2 * lane_pad, radial_len), fields.dtype),
        ),
        in_specs=[vmem, vmem, vmem],
        out_specs=(vmem, vmem),
        scratch_shapes=[
            pltpu.SemaphoreType.DMA((count, 3)),
            pltpu.SemaphoreType.DMA((count, 3)),
        ],
        compiler_params=pltpu.CompilerParams(collective_id=1, has_side_effects=True),
    )(fields, thermal, viscous)


def gradient(stencil):
    return (8.0 * (stencil[3] - stencil[1]) - (stencil[4] - stencil[0])) / 12.0


def curvature(stencil):
    return (16.0 * (stencil[3] + stencil[1]) - (stencil[4] + stencil[0]) - 30.0 * stencil[2]) / 12.0


def slope(stencil):
    return 8.0 * (stencil[3] - stencil[1]) - (stencil[4] - stencil[0])


def spread(stencil):
    return 16.0 * (stencil[3] + stencil[1]) - (stencil[4] + stencil[0]) - 30.0 * stencil[2]


def shifted(block, step):
    size = block.shape[-1]
    lane = lax.broadcasted_iota(jnp.int32, block.shape, block.ndim - 1)
    moved = pltpu.roll(block, (size - step) % size, block.ndim - 1)
    keep = jnp.logical_and(lane + step >= 0, lane + step < size)
    return jnp.where(keep, moved, 0.0)


def step_kernel(
    row_pad, col_pad, fields_ref, coefs_ref, rows_ref, cols_ref, frac_ref, trig_ref,
    out_ref, final_ref, row_out, col_out, row_send, col_send, send_sem, row_sem, col_sem,
):
    panel = lax.axis_index("panel")
    colat = lax.axis_index("colat")
    lon = lax.axis_index("lon")
    colat_count = lax.axis_size("colat")
    lon_count = lax.axis_size("lon")
    row_types = row_out.shape[0] // 2
    col_types = col_out.shape[0] // 2
    row_share = row_send.shape[1]
    other = 1 - panel

    def route(share, per_type, count):
        kind = share // per_type
        edge = (kind % 2) * (count - 1)
        slot = (kind // 2) * per_type + share % per_type
        return edge, slot

    row_edge, row_slot = route(colat, row_types, colat_count)
    col_edge, col_slot = route(lon, col_types, lon_count)
    row_dest = (other, row_edge, lon)
    col_dest = (other, colat, col_edge)
    at_row_edge = jnp.logical_or(colat == 0, colat == colat_count - 1)
    at_col_edge = jnp.logical_or(lon == 0, lon == lon_count - 1)
    parity_row = (colat // (colat_count - 1)).astype(jnp.int32)
    parity_col = (lon // (lon_count - 1)).astype(jnp.int32)

    def row_sender(slot):
        kind = 2 * (slot // row_types) + parity_row
        return (other, kind * row_types + slot % row_types, lon)

    def col_sender(slot):
        kind = 2 * (slot // col_types) + parity_col
        return (other, colat, kind * col_types + slot % col_types)

    barrier = pltpu.get_barrier_semaphore()
    pl.semaphore_signal(barrier, 1, device_id=row_dest, device_id_type=MESH)
    pl.semaphore_signal(barrier, 1, device_id=col_dest, device_id_type=MESH)

    @pl.when(at_row_edge)
    def _():
        for slot in range(2 * row_types):
            pl.semaphore_signal(barrier, 1, device_id=row_sender(slot), device_id_type=MESH)

    @pl.when(at_col_edge)
    def _():
        for slot in range(2 * col_types):
            pl.semaphore_signal(barrier, 1, device_id=col_sender(slot), device_id_type=MESH)

    ext_rows, span, radial_len = out_ref.shape[1], out_ref.shape[2], out_ref.shape[3]
    height = ext_rows - 2
    breadth = fields_ref.shape[2] - 2 * col_pad
    lead = (span - breadth) // 2
    col_ids = lax.broadcasted_iota(jnp.int32, (span, radial_len), 0) - lead + lon * breadth
    col_ok = jnp.logical_and(col_ids >= 0, col_ids < lon_count * breadth)

    def body(row, carry):
        global_row = row - 1 + colat * height
        ok = jnp.logical_and(col_ok, jnp.logical_and(global_row >= 0, global_row < colat_count * height))

        def load(field, down, across):
            return fields_ref[field, row + row_pad - 1 + down, pl.ds(col_pad - lead + across, span), :]

        center = [load(field, 0, 0) for field in range(4)]
        thermal = coefs_ref[0, row, pl.ds(col_pad - lead, span), :]
        viscous = coefs_ref[1, row, pl.ds(col_pad - lead, span), :]
        for field in range(4):
            along_lat = [load(field, offset - 2, 0) for offset in range(5)]
            along_lon = [load(field, 0, offset - 2) for offset in range(5)]
            along_rad = [shifted(center[field], offset - 2) for offset in range(5)]
            laplace = spread(along_rad) + spread(along_lat) + spread(along_lon)
            transport = (
                center[1] * slope(along_rad)
                + center[2] * slope(along_lat)
                + center[3] * slope(along_lon)
            )
            change = (thermal if field == 0 else viscous) * laplace - transport
            stepped_value = center[field] + (TIME_STEP / 12.0) * change
            if field == 1:
                stepped_value = stepped_value + (TIME_STEP * BUOYANCY) * center[0]
            out_ref[field, row] = jnp.where(ok, stepped_value, 0.0)
        return carry

    lax.fori_loop(0, ext_rows, body, 0)
    for field in range(4):
        final_ref[field] = out_ref[field, pl.ds(1, height), pl.ds(lead, breadth), :]

    slots = rows_ref.shape[0]
    column = lax.broadcasted_iota(jnp.int32, (span, radial_len), 0)
    for slot in range(slots):
        first = rows_ref[slot]
        across = cols_ref[slot] + (lead - 1)
        frac_row = frac_ref[0, slot]
        frac_lon = frac_ref[1, slot]
        weight = jnp.where(
            column == across, 1.0 - frac_lon, jnp.where(column == across + 1, frac_lon, 0.0)
        )
        mixed = []
        for field in range(4):
            upper = jnp.sum(weight * out_ref[field, first], axis=0, keepdims=True)
            lower = jnp.sum(weight * out_ref[field, first + 1], axis=0, keepdims=True)
            mixed.append((1.0 - frac_row) * upper + frac_row * lower)
        cosine = trig_ref[0, slot]
        sine_part = trig_ref[1, slot]
        turned = [
            mixed[0],
            mixed[1],
            cosine * mixed[2] - sine_part * mixed[3],
            sine_part * mixed[2] + cosine * mixed[3],
        ]
        for field in range(4):
            if slot < row_share:
                row_send[field, pl.ds(slot, 1), :] = turned[field]
            else:
                col_send[field, pl.ds(slot - row_share, 1), :] = turned[field]

    expected = (
        2
        + at_row_edge.astype(jnp.int32) * (2 * row_types)
        + at_col_edge.astype(jnp.int32) * (2 * col_types)
    )
    pl.semaphore_wait(barrier, expected)

    row_copy = pltpu.make_async_remote_copy(
        row_send, row_out.at[row_slot], send_sem.at[0], row_sem.at[row_slot],
        device_id=row_dest, device_id_type=MESH,
    )
    col_copy = pltpu.make_async_remote_copy(
        col_send, col_out.at[col_slot], send_sem.at[1], col_sem.at[col_slot],
        device_id=col_dest, device_id_type=MESH,
    )
    row_copy.start()
    col_copy.start()
    row_copy.wait_send()
    col_copy.wait_send()

    @pl.when(at_row_edge)
    def _():
        for slot in range(2 * row_types):
            pltpu.make_async_remote_copy(
                row_send, row_out.at[slot], send_sem.at[0], row_sem.at[slot],
                device_id=row_sender(slot), device_id_type=MESH,
            ).wait_recv()

    @pl.when(at_col_edge)
    def _():
        for slot in range(2 * col_types):
            pltpu.make_async_remote_copy(
                col_send, col_out.at[slot], send_sem.at[1], col_sem.at[slot],
                device_id=col_sender(slot), device_id_type=MESH,
            ).wait_recv()

    col_share = col_out.shape[2]

    def put_columns(first, second):
        for slot in range(2 * col_types):
            column = first if slot < col_types else second
            base = (slot % col_types) * col_share
            for field in range(4):
                for offset in range(col_share):
                    final_ref[field, base + offset, pl.ds(column, 1), :] = (
                        col_out[slot, field, pl.ds(offset, 1), :]
                    )

    def put_rows(first, second):
        for slot in range(2 * row_types):
            line = first if slot < row_types else second
            base = (slot % row_types) * row_share
            for field in range(4):
                final_ref[field, line, pl.ds(base, row_share), :] = row_out[slot, field]

    @pl.when(lon == 0)
    def _():
        put_columns(0, 1)

    @pl.when(lon == lon_count - 1)
    def _():
        put_columns(breadth - 1, breadth - 2)

    @pl.when(colat == 0)
    def _():
        put_rows(0, 1)

    @pl.when(colat == colat_count - 1)
    def _():
        put_rows(height - 1, height - 2)


def stepped(fields_pad, coefs_pad, row_pad, col_pad, lead, rows, cols, frac, trig, row_share):
    height = coefs_pad.shape[1] - 2
    breadth = fields_pad.shape[2] - 2 * col_pad
    span = breadth + 2 * lead
    radial_len = fields_pad.shape[3]
    slots = rows.shape[0]
    row_types = lax.axis_size("colat") // 4
    col_types = lax.axis_size("lon") // 4
    dtype = fields_pad.dtype
    vmem = pl.BlockSpec(memory_space=pltpu.VMEM)
    smem = pl.BlockSpec(memory_space=pltpu.SMEM)
    return pl.pallas_call(
        functools.partial(step_kernel, row_pad, col_pad),
        out_shape=(
            jax.ShapeDtypeStruct((4, height + 2, span, radial_len), dtype),
            jax.ShapeDtypeStruct((4, height, breadth, radial_len), dtype),
            jax.ShapeDtypeStruct((2 * row_types, 4, row_share, radial_len), dtype),
            jax.ShapeDtypeStruct((2 * col_types, 4, slots - row_share, radial_len), dtype),
        ),
        in_specs=[vmem, vmem, smem, smem, smem, smem],
        out_specs=(vmem, vmem, vmem, vmem),
        scratch_shapes=[
            pltpu.VMEM((4, row_share, radial_len), dtype),
            pltpu.VMEM((4, slots - row_share, radial_len), dtype),
            pltpu.SemaphoreType.DMA((2,)),
            pltpu.SemaphoreType.DMA((2 * row_types,)),
            pltpu.SemaphoreType.DMA((2 * col_types,)),
        ],
        compiler_params=pltpu.CompilerParams(collective_id=0, has_side_effects=True),
    )(fields_pad, coefs_pad, rows, cols, frac, trig)


def advance(padded, thermal, viscous):
    height = padded.shape[1] - 4
    breadth = padded.shape[2] - 4
    center = padded[:, 2 : 2 + height, 2 : 2 + breadth]
    radial_len = center.shape[3]
    radial_pad = jnp.pad(center, ((0, 0), (0, 0), (0, 0), (2, 2)))
    along_lat = [padded[:, offset : offset + height, 2 : 2 + breadth] for offset in range(5)]
    along_lon = [padded[:, 2 : 2 + height, offset : offset + breadth] for offset in range(5)]
    along_rad = [radial_pad[..., offset : offset + radial_len] for offset in range(5)]
    laplace = curvature(along_rad) + curvature(along_lat) + curvature(along_lon)
    transport = (
        center[1:2] * gradient(along_rad)
        + center[2:3] * gradient(along_lat)
        + center[3:4] * gradient(along_lon)
    )
    diffusion = jnp.stack([thermal, viscous, viscous, viscous])
    change = diffusion * laplace - transport
    change = change.at[1].add(BUOYANCY * center[0])
    return center + TIME_STEP * change


def local(fields_now, diffusivity, viscosity, donor_row, donor_column, donor_offset, rim_angle):
    fields = fields_now[:, 0]
    thermal = diffusivity[0]
    viscous = viscosity[0]
    height = fields.shape[1]
    breadth = fields.shape[2]
    radial_len = fields.shape[3]
    colat_pos = lax.axis_index("colat")
    lon_pos = lax.axis_index("lon")
    colat_count = lax.axis_size("colat")
    lon_count = lax.axis_size("lon")
    row_share = 4 * breadth // colat_count
    fields_pad, coefs_pad = halo_exchange(fields, thermal, viscous, 3)
    lead = 4
    angles = rim_angle.reshape(-1)
    trig = jnp.stack([jnp.cos(angles), jnp.sin(angles)])
    frac = donor_offset.reshape(2, -1)
    extended, fresh, row_buf, col_buf = stepped(
        fields_pad, coefs_pad, 3, 8, lead, donor_row.reshape(-1), donor_column.reshape(-1),
        frac, trig, row_share,
    )
    return fresh[:, None]


def solution(mesh):
    placed = (
        P(None, "panel", "colat", "lon", None),
        P("panel", "colat", "lon", None),
        P("panel", "colat", "lon", None),
        P("panel", "colat", "lon", None),
        P("panel", "colat", "lon", None),
        P("panel", "colat", "lon", None, None),
        P("panel", "colat", "lon", None),
    )
    return jax.shard_map(
        local,
        mesh=mesh,
        in_specs=placed,
        out_specs=P(None, "panel", "colat", "lon", None),
        check_vma=False,
    )
```

```python
import functools

import jax
import jax.numpy as jnp
from jax import lax
from jax.sharding import PartitionSpec as P
from jax.experimental import pallas as pl
from jax.experimental.pallas import tpu as pltpu

MESH = pl.DeviceIdType.MESH

TIME_STEP = 0.05
BUOYANCY = 1.0


def with_halo(x, sides, width):
    for axis, dim in sides:
        count, length = (lax.axis_size(axis), x.shape[dim])
        up = [(i, (i + 1) % count) for i in range(count - 1)]
        down = [(j, i) for i, j in up]
        last = lax.slice_in_dim(x, length - width, length, axis=dim)
        leading = lax.slice_in_dim(x, 0, width, axis=dim)
        before = lax.ppermute(last, axis, up)
        after = lax.ppermute(leading, axis, down)
        x = jnp.concatenate([before, x, after], axis=dim)
    return x


def swapped(block, axis, stride):
    count = lax.axis_size(axis)
    route = []
    for low in range(count):
        high = low | 1 << stride
        if high != low and high < count:
            route += [(low, high), (high, low)]
    return lax.ppermute(block, axis, route)


DIRECTIONS = ((-1, -1), (-1, 0), (-1, 1), (0, -1), (0, 1), (1, -1), (1, 0), (1, 1))


def window(step, width, length, offset):
    if step < 0:
        return offset, width
    if step > 0:
        return offset + length - width, width
    return offset, length


def landing(step, width, length, offset):
    if step < 0:
        return offset - width, width
    if step > 0:
        return offset + length, width
    return offset, length


def halo_kernel(width, margins, fields_in, thermal_in, viscous_in, fields_out, coefs_out, send_sem, recv_sem):
    count = len(DIRECTIONS)
    panel = lax.axis_index("panel")
    colat = lax.axis_index("colat")
    lon = lax.axis_index("lon")
    colat_count = lax.axis_size("colat")
    lon_count = lax.axis_size("lon")
    height, breadth = fields_in.shape[1], fields_in.shape[2]

    for out, (row_pad, col_pad) in ((fields_out, margins[0]), (coefs_out, margins[1])):
        lead = out.shape[:1]
        total_rows, total_cols = out.shape[1], out.shape[2]
        out[:, pl.ds(0, row_pad)] = jnp.zeros(lead + (row_pad, total_cols, out.shape[3]), out.dtype)
        out[:, pl.ds(row_pad + height, row_pad)] = jnp.zeros(
            lead + (row_pad, total_cols, out.shape[3]), out.dtype
        )
        side = jnp.zeros(lead + (height, col_pad, out.shape[3]), out.dtype)
        out[:, pl.ds(row_pad, height), pl.ds(0, col_pad)] = side
        out[:, pl.ds(row_pad, height), pl.ds(col_pad + breadth, total_cols - col_pad - breadth)] = side
    fields_out[:, pl.ds(margins[0][0], height), pl.ds(margins[0][1], breadth)] = fields_in[...]
    coefs_out[0, pl.ds(margins[1][0], height), pl.ds(margins[1][1], breadth)] = thermal_in[...]
    coefs_out[1, pl.ds(margins[1][0], height), pl.ds(margins[1][1], breadth)] = viscous_in[...]

    def present(step):
        row = colat + step[0]
        col = lon + step[1]
        inside = jnp.logical_and(row >= 0, row < colat_count)
        return jnp.logical_and(inside, jnp.logical_and(col >= 0, col < lon_count))

    def source(part, step):
        depth = width if part == 0 else 1
        rows = window(step[0], depth, height, 0)
        cols = window(step[1], margins[0][1], breadth, 0)
        ref = (fields_in, thermal_in, viscous_in)[part]
        if part == 0:
            return ref.at[:, pl.ds(rows[0], rows[1]), pl.ds(cols[0], cols[1]), :]
        return ref.at[pl.ds(rows[0], rows[1]), pl.ds(cols[0], cols[1]), :]

    def target(part, step):
        depth = width if part == 0 else 1
        row_pad, col_pad = margins[0] if part == 0 else margins[1]
        rows = landing(step[0], depth, height, row_pad)
        cols = landing(step[1], col_pad, breadth, col_pad)
        if part == 0:
            return fields_out.at[:, pl.ds(rows[0], rows[1]), pl.ds(cols[0], cols[1]), :]
        return coefs_out.at[part - 1, pl.ds(rows[0], rows[1]), pl.ds(cols[0], cols[1]), :]

    def outgoing(index, part):
        step = DIRECTIONS[index]
        back = tuple(-s for s in step)
        return pltpu.make_async_remote_copy(
            source(part, step), target(part, back),
            send_sem.at[index, part], recv_sem.at[count - 1 - index, part],
            device_id=(panel, colat + step[0], lon + step[1]), device_id_type=MESH,
        )

    def incoming(index, part):
        step = DIRECTIONS[index]
        spot = target(part, step)
        return pltpu.make_async_remote_copy(
            spot, spot, send_sem.at[index, part], recv_sem.at[index, part],
            device_id=(panel, colat + step[0], lon + step[1]), device_id_type=MESH,
        )

    barrier = pltpu.get_barrier_semaphore()
    expected = jnp.int32(0)
    for index, step in enumerate(DIRECTIONS):
        exists = present(step)
        expected = expected + exists.astype(jnp.int32)

        @pl.when(exists)
        def _():
            pl.semaphore_signal(
                barrier, 1, device_id=(panel, colat + step[0], lon + step[1]),
                device_id_type=MESH,
            )

    pl.semaphore_wait(barrier, expected)
    for index, step in enumerate(DIRECTIONS):

        @pl.when(present(step))
        def _():
            for part in range(3):
                outgoing(index, part).start()

    for index, step in enumerate(DIRECTIONS):

        @pl.when(present(step))
        def _():
            for part in range(3):
                outgoing(index, part).wait_send()
            for part in range(3):
                incoming(index, part).wait_recv()


def halo_exchange(fields, thermal, viscous, width):
    lane_pad = 8
    height, breadth, radial_len = fields.shape[1], fields.shape[2], fields.shape[3]
    margins = ((width, lane_pad), (1, lane_pad))
    vmem = pl.BlockSpec(memory_space=pltpu.VMEM)
    count = len(DIRECTIONS)
    return pl.pallas_call(
        functools.partial(halo_kernel, width, margins),
        out_shape=(
            jax.ShapeDtypeStruct(
                (4, height + 2 * width, breadth + 2 * lane_pad, radial_len), fields.dtype
            ),
            jax.ShapeDtypeStruct((2, height + 2, breadth + 2 * lane_pad, radial_len), fields.dtype),
        ),
        in_specs=[vmem, vmem, vmem],
        out_specs=(vmem, vmem),
        scratch_shapes=[
            pltpu.SemaphoreType.DMA((count, 3)),
            pltpu.SemaphoreType.DMA((count, 3)),
        ],
        compiler_params=pltpu.CompilerParams(collective_id=1, has_side_effects=True),
    )(fields, thermal, viscous)


def gradient(stencil):
    return (8.0 * (stencil[3] - stencil[1]) - (stencil[4] - stencil[0])) / 12.0


def curvature(stencil):
    return (16.0 * (stencil[3] + stencil[1]) - (stencil[4] + stencil[0]) - 30.0 * stencil[2]) / 12.0


def slope(stencil):
    return 8.0 * (stencil[3] - stencil[1]) - (stencil[4] - stencil[0])


def spread(stencil):
    return 16.0 * (stencil[3] + stencil[1]) - (stencil[4] + stencil[0]) - 30.0 * stencil[2]


def shifted(block, step):
    size = block.shape[-1]
    lane = lax.broadcasted_iota(jnp.int32, block.shape, block.ndim - 1)
    moved = pltpu.roll(block, (size - step) % size, block.ndim - 1)
    keep = jnp.logical_and(lane + step >= 0, lane + step < size)
    return jnp.where(keep, moved, 0.0)


def step_kernel(
    row_pad, col_pad, fields_ref, coefs_ref, rows_ref, cols_ref, frac_ref, trig_ref,
    out_ref, final_ref, row_out, col_out, row_send, col_send, send_sem, row_sem, col_sem,
):
    panel = lax.axis_index("panel")
    colat = lax.axis_index("colat")
    lon = lax.axis_index("lon")
    colat_count = lax.axis_size("colat")
    lon_count = lax.axis_size("lon")
    row_types = row_out.shape[0] // 2
    col_types = col_out.shape[0] // 2
    row_share = row_send.shape[1]
    other = 1 - panel

    def route(share, per_type, count):
        kind = share // per_type
        edge = (kind % 2) * (count - 1)
        slot = (kind // 2) * per_type + share % per_type
        return edge, slot

    row_edge, row_slot = route(colat, row_types, colat_count)
    col_edge, col_slot = route(lon, col_types, lon_count)
    row_dest = (other, row_edge, lon)
    col_dest = (other, colat, col_edge)
    at_row_edge = jnp.logical_or(colat == 0, colat == colat_count - 1)
    at_col_edge = jnp.logical_or(lon == 0, lon == lon_count - 1)
    parity_row = (colat // (colat_count - 1)).astype(jnp.int32)
    parity_col = (lon // (lon_count - 1)).astype(jnp.int32)

    def row_sender(slot):
        kind = 2 * (slot // row_types) + parity_row
        return (other, kind * row_types + slot % row_types, lon)

    def col_sender(slot):
        kind = 2 * (slot // col_types) + parity_col
        return (other, colat, kind * col_types + slot % col_types)

    barrier = pltpu.get_barrier_semaphore()
    pl.semaphore_signal(barrier, 1, device_id=row_dest, device_id_type=MESH)
    pl.semaphore_signal(barrier, 1, device_id=col_dest, device_id_type=MESH)

    @pl.when(at_row_edge)
    def _():
        for slot in range(2 * row_types):
            pl.semaphore_signal(barrier, 1, device_id=row_sender(slot), device_id_type=MESH)

    @pl.when(at_col_edge)
    def _():
        for slot in range(2 * col_types):
            pl.semaphore_signal(barrier, 1, device_id=col_sender(slot), device_id_type=MESH)

    ext_rows, span, radial_len = out_ref.shape[1], out_ref.shape[2], out_ref.shape[3]
    height = ext_rows - 2
    breadth = fields_ref.shape[2] - 2 * col_pad
    lead = (span - breadth) // 2
    col_ids = lax.broadcasted_iota(jnp.int32, (span, radial_len), 0) - lead + lon * breadth
    col_ok = jnp.logical_and(col_ids >= 0, col_ids < lon_count * breadth)

    def body(row, carry):
        global_row = row - 1 + colat * height
        ok = jnp.logical_and(col_ok, jnp.logical_and(global_row >= 0, global_row < colat_count * height))

        def load(field, down, across):
            return fields_ref[field, row + row_pad - 1 + down, pl.ds(col_pad - lead + across, span), :]

        center = [load(field, 0, 0) for field in range(4)]
        thermal = coefs_ref[0, row, pl.ds(col_pad - lead, span), :]
        viscous = coefs_ref[1, row, pl.ds(col_pad - lead, span), :]
        for field in range(4):
            along_lat = [load(field, offset - 2, 0) for offset in range(5)]
            along_lon = [load(field, 0, offset - 2) for offset in range(5)]
            along_rad = [shifted(center[field], offset - 2) for offset in range(5)]
            laplace = spread(along_rad) + spread(along_lat) + spread(along_lon)
            transport = (
                center[1] * slope(along_rad)
                + center[2] * slope(along_lat)
                + center[3] * slope(along_lon)
            )
            change = (thermal if field == 0 else viscous) * laplace - transport
            stepped_value = center[field] + (TIME_STEP / 12.0) * change
            if field == 1:
                stepped_value = stepped_value + (TIME_STEP * BUOYANCY) * center[0]
            out_ref[field, row] = jnp.where(ok, stepped_value, 0.0)
        return carry

    lax.fori_loop(0, ext_rows, body, 0)
    for field in range(4):
        final_ref[field] = out_ref[field, pl.ds(1, height), pl.ds(lead, breadth), :]

    slots = rows_ref.shape[0]
    column = lax.broadcasted_iota(jnp.int32, (span, radial_len), 0)
    for slot in range(slots):
        first = rows_ref[slot]
        across = cols_ref[slot] + (lead - 1)
        frac_row = frac_ref[0, slot]
        frac_lon = frac_ref[1, slot]
        weight = jnp.where(
            column == across, 1.0 - frac_lon, jnp.where(column == across + 1, frac_lon, 0.0)
        )
        mixed = []
        for field in range(4):
            upper = jnp.sum(weight * out_ref[field, first], axis=0, keepdims=True)
            lower = jnp.sum(weight * out_ref[field, first + 1], axis=0, keepdims=True)
            mixed.append((1.0 - frac_row) * upper + frac_row * lower)
        cosine = trig_ref[0, slot]
        sine_part = trig_ref[1, slot]
        turned = [
            mixed[0],
            mixed[1],
            cosine * mixed[2] - sine_part * mixed[3],
            sine_part * mixed[2] + cosine * mixed[3],
        ]
        for field in range(4):
            if slot < row_share:
                row_send[field, pl.ds(slot, 1), :] = turned[field]
            else:
                col_send[field, pl.ds(slot - row_share, 1), :] = turned[field]

    expected = (
        2
        + at_row_edge.astype(jnp.int32) * (2 * row_types)
        + at_col_edge.astype(jnp.int32) * (2 * col_types)
    )
    pl.semaphore_wait(barrier, expected)

    row_copy = pltpu.make_async_remote_copy(
        row_send, row_out.at[row_slot], send_sem.at[0], row_sem.at[row_slot],
        device_id=row_dest, device_id_type=MESH,
    )
    col_copy = pltpu.make_async_remote_copy(
        col_send, col_out.at[col_slot], send_sem.at[1], col_sem.at[col_slot],
        device_id=col_dest, device_id_type=MESH,
    )
    row_copy.start()
    col_copy.start()
    row_copy.wait_send()
    col_copy.wait_send()

    @pl.when(at_row_edge)
    def _():
        for slot in range(2 * row_types):
            pltpu.make_async_remote_copy(
                row_send, row_out.at[slot], send_sem.at[0], row_sem.at[slot],
                device_id=row_sender(slot), device_id_type=MESH,
            ).wait_recv()

    @pl.when(at_col_edge)
    def _():
        for slot in range(2 * col_types):
            pltpu.make_async_remote_copy(
                col_send, col_out.at[slot], send_sem.at[1], col_sem.at[slot],
                device_id=col_sender(slot), device_id_type=MESH,
            ).wait_recv()

    col_share = col_out.shape[2]

    def put_columns(first, second):
        for slot in range(2 * col_types):
            column = first if slot < col_types else second
            base = (slot % col_types) * col_share
            for field in range(4):
                for offset in range(col_share):
                    final_ref[field, base + offset, pl.ds(column, 1), :] = (
                        col_out[slot, field, pl.ds(offset, 1), :]
                    )

    def put_rows(first, second):
        for slot in range(2 * row_types):
            line = first if slot < row_types else second
            base = (slot % row_types) * row_share
            for field in range(4):
                final_ref[field, line, pl.ds(base, row_share), :] = row_out[slot, field]

    @pl.when(lon == 0)
    def _():
        put_columns(0, 1)

    @pl.when(lon == lon_count - 1)
    def _():
        put_columns(breadth - 1, breadth - 2)

    @pl.when(colat == 0)
    def _():
        put_rows(0, 1)

    @pl.when(colat == colat_count - 1)
    def _():
        put_rows(height - 1, height - 2)


def stepped(fields_pad, coefs_pad, row_pad, col_pad, lead, rows, cols, frac, trig, row_share):
    height = coefs_pad.shape[1] - 2
    breadth = fields_pad.shape[2] - 2 * col_pad
    span = breadth + 2 * lead
    radial_len = fields_pad.shape[3]
    slots = rows.shape[0]
    row_types = lax.axis_size("colat") // 4
    col_types = lax.axis_size("lon") // 4
    dtype = fields_pad.dtype
    vmem = pl.BlockSpec(memory_space=pltpu.VMEM)
    smem = pl.BlockSpec(memory_space=pltpu.SMEM)
    return pl.pallas_call(
        functools.partial(step_kernel, row_pad, col_pad),
        out_shape=(
            jax.ShapeDtypeStruct((4, height + 2, span, radial_len), dtype),
            jax.ShapeDtypeStruct((4, height, breadth, radial_len), dtype),
            jax.ShapeDtypeStruct((2 * row_types, 4, row_share, radial_len), dtype),
            jax.ShapeDtypeStruct((2 * col_types, 4, slots - row_share, radial_len), dtype),
        ),
        in_specs=[vmem, vmem, smem, smem, smem, smem],
        out_specs=(vmem, vmem, vmem, vmem),
        scratch_shapes=[
            pltpu.VMEM((4, row_share, radial_len), dtype),
            pltpu.VMEM((4, slots - row_share, radial_len), dtype),
            pltpu.SemaphoreType.DMA((2,)),
            pltpu.SemaphoreType.DMA((2 * row_types,)),
            pltpu.SemaphoreType.DMA((2 * col_types,)),
        ],
        compiler_params=pltpu.CompilerParams(collective_id=0, has_side_effects=True),
    )(fields_pad, coefs_pad, rows, cols, frac, trig)


def advance(padded, thermal, viscous):
    height = padded.shape[1] - 4
    breadth = padded.shape[2] - 4
    center = padded[:, 2 : 2 + height, 2 : 2 + breadth]
    radial_len = center.shape[3]
    radial_pad = jnp.pad(center, ((0, 0), (0, 0), (0, 0), (2, 2)))
    along_lat = [padded[:, offset : offset + height, 2 : 2 + breadth] for offset in range(5)]
    along_lon = [padded[:, 2 : 2 + height, offset : offset + breadth] for offset in range(5)]
    along_rad = [radial_pad[..., offset : offset + radial_len] for offset in range(5)]
    laplace = curvature(along_rad) + curvature(along_lat) + curvature(along_lon)
    transport = (
        center[1:2] * gradient(along_rad)
        + center[2:3] * gradient(along_lat)
        + center[3:4] * gradient(along_lon)
    )
    diffusion = jnp.stack([thermal, viscous, viscous, viscous])
    change = diffusion * laplace - transport
    change = change.at[1].add(BUOYANCY * center[0])
    return center + TIME_STEP * change


def local(fields_now, diffusivity, viscosity, donor_row, donor_column, donor_offset, rim_angle):
    fields = fields_now[:, 0]
    thermal = diffusivity[0]
    viscous = viscosity[0]
    height = fields.shape[1]
    breadth = fields.shape[2]
    radial_len = fields.shape[3]
    colat_pos = lax.axis_index("colat")
    lon_pos = lax.axis_index("lon")
    colat_count = lax.axis_size("colat")
    lon_count = lax.axis_size("lon")
    row_share = 4 * breadth // colat_count
    fields_pad, coefs_pad = halo_exchange(fields, thermal, viscous, 3)
    lead = 4
    angles = rim_angle.reshape(-1)
    trig = jnp.stack([jnp.cos(angles), jnp.sin(angles)])
    frac = donor_offset.reshape(2, -1)
    extended, fresh, row_buf, col_buf = stepped(
        fields_pad, coefs_pad, 3, 8, lead, donor_row.reshape(-1), donor_column.reshape(-1),
        frac, trig, row_share,
    )
    return fresh[:, None]


def solution(mesh):
    placed = (
        P(None, "panel", "colat", "lon", None),
        P("panel", "colat", "lon", None),
        P("panel", "colat", "lon", None),
        P("panel", "colat", "lon", None),
        P("panel", "colat", "lon", None),
        P("panel", "colat", "lon", None, None),
        P("panel", "colat", "lon", None),
    )
    return jax.shard_map(
        local,
        mesh=mesh,
        in_specs=placed,
        out_specs=P(None, "panel", "colat", "lon", None),
        check_vma=False,
    )
```

```python
import functools

import jax
import jax.numpy as jnp
from jax import lax
from jax.sharding import PartitionSpec as P
from jax.experimental import pallas as pl
from jax.experimental.pallas import tpu as pltpu

MESH = pl.DeviceIdType.MESH

TIME_STEP = 0.05
BUOYANCY = 1.0


def with_halo(x, sides, width):
    for axis, dim in sides:
        count, length = (lax.axis_size(axis), x.shape[dim])
        up = [(i, (i + 1) % count) for i in range(count - 1)]
        down = [(j, i) for i, j in up]
        last = lax.slice_in_dim(x, length - width, length, axis=dim)
        leading = lax.slice_in_dim(x, 0, width, axis=dim)
        before = lax.ppermute(last, axis, up)
        after = lax.ppermute(leading, axis, down)
        x = jnp.concatenate([before, x, after], axis=dim)
    return x


def swapped(block, axis, stride):
    count = lax.axis_size(axis)
    route = []
    for low in range(count):
        high = low | 1 << stride
        if high != low and high < count:
            route += [(low, high), (high, low)]
    return lax.ppermute(block, axis, route)


DIRECTIONS = ((-1, -1), (-1, 0), (-1, 1), (0, -1), (0, 1), (1, -1), (1, 0), (1, 1))


def window(step, width, length, offset):
    if step < 0:
        return offset, width
    if step > 0:
        return offset + length - width, width
    return offset, length


def landing(step, width, length, offset):
    if step < 0:
        return offset - width, width
    if step > 0:
        return offset + length, width
    return offset, length


def halo_kernel(width, margins, fields_in, thermal_in, viscous_in, fields_out, coefs_out, send_sem, recv_sem):
    count = len(DIRECTIONS)
    panel = lax.axis_index("panel")
    colat = lax.axis_index("colat")
    lon = lax.axis_index("lon")
    colat_count = lax.axis_size("colat")
    lon_count = lax.axis_size("lon")
    height, breadth = fields_in.shape[1], fields_in.shape[2]

    for out, (row_pad, col_pad) in ((fields_out, margins[0]), (coefs_out, margins[1])):
        lead = out.shape[:1]
        total_rows, total_cols = out.shape[1], out.shape[2]
        out[:, pl.ds(0, row_pad)] = jnp.zeros(lead + (row_pad, total_cols, out.shape[3]), out.dtype)
        out[:, pl.ds(row_pad + height, row_pad)] = jnp.zeros(
            lead + (row_pad, total_cols, out.shape[3]), out.dtype
        )
        side = jnp.zeros(lead + (height, col_pad, out.shape[3]), out.dtype)
        out[:, pl.ds(row_pad, height), pl.ds(0, col_pad)] = side
        out[:, pl.ds(row_pad, height), pl.ds(col_pad + breadth, total_cols - col_pad - breadth)] = side
    fields_out[:, pl.ds(margins[0][0], height), pl.ds(margins[0][1], breadth)] = fields_in[...]
    coefs_out[0, pl.ds(margins[1][0], height), pl.ds(margins[1][1], breadth)] = thermal_in[...]
    coefs_out[1, pl.ds(margins[1][0], height), pl.ds(margins[1][1], breadth)] = viscous_in[...]

    def present(step):
        row = colat + step[0]
        col = lon + step[1]
        inside = jnp.logical_and(row >= 0, row < colat_count)
        return jnp.logical_and(inside, jnp.logical_and(col >= 0, col < lon_count))

    def source(part, step):
        depth = width if part == 0 else 1
        rows = window(step[0], depth, height, 0)
        cols = window(step[1], depth, breadth, 0)
        ref = (fields_in, thermal_in, viscous_in)[part]
        if part == 0:
            return ref.at[:, pl.ds(rows[0], rows[1]), pl.ds(cols[0], cols[1]), :]
        return ref.at[pl.ds(rows[0], rows[1]), pl.ds(cols[0], cols[1]), :]

    def target(part, step):
        depth = width if part == 0 else 1
        row_pad, col_pad = margins[0] if part == 0 else margins[1]
        rows = landing(step[0], depth, height, row_pad)
        cols = landing(step[1], depth, breadth, col_pad)
        if part == 0:
            return fields_out.at[:, pl.ds(rows[0], rows[1]), pl.ds(cols[0], cols[1]), :]
        return coefs_out.at[part - 1, pl.ds(rows[0], rows[1]), pl.ds(cols[0], cols[1]), :]

    def outgoing(index, part):
        step = DIRECTIONS[index]
        back = tuple(-s for s in step)
        return pltpu.make_async_remote_copy(
            source(part, step), target(part, back),
            send_sem.at[index, part], recv_sem.at[count - 1 - index, part],
            device_id=(panel, colat + step[0], lon + step[1]), device_id_type=MESH,
        )

    def incoming(index, part):
        step = DIRECTIONS[index]
        spot = target(part, step)
        return pltpu.make_async_remote_copy(
            spot, spot, send_sem.at[index, part], recv_sem.at[index, part],
            device_id=(panel, colat + step[0], lon + step[1]), device_id_type=MESH,
        )

    barrier = pltpu.get_barrier_semaphore()
    expected = jnp.int32(0)
    for index, step in enumerate(DIRECTIONS):
        exists = present(step)
        expected = expected + exists.astype(jnp.int32)

        @pl.when(exists)
        def _():
            pl.semaphore_signal(
                barrier, 1, device_id=(panel, colat + step[0], lon + step[1]),
                device_id_type=MESH,
            )

    pl.semaphore_wait(barrier, expected)
    for index, step in enumerate(DIRECTIONS):

        @pl.when(present(step))
        def _():
            for part in range(3):
                outgoing(index, part).start()

    for index, step in enumerate(DIRECTIONS):

        @pl.when(present(step))
        def _():
            for part in range(3):
                outgoing(index, part).wait_send()
            for part in range(3):
                incoming(index, part).wait_recv()


def halo_exchange(fields, thermal, viscous, width):
    lane_pad = 12
    height, breadth, radial_len = fields.shape[1], fields.shape[2], fields.shape[3]
    margins = ((width, lane_pad), (1, lane_pad))
    vmem = pl.BlockSpec(memory_space=pltpu.VMEM)
    count = len(DIRECTIONS)
    return pl.pallas_call(
        functools.partial(halo_kernel, width, margins),
        out_shape=(
            jax.ShapeDtypeStruct(
                (4, height + 2 * width, breadth + 2 * lane_pad, radial_len), fields.dtype
            ),
            jax.ShapeDtypeStruct((2, height + 2, breadth + 2 * lane_pad, radial_len), fields.dtype),
        ),
        in_specs=[vmem, vmem, vmem],
        out_specs=(vmem, vmem),
        scratch_shapes=[
            pltpu.SemaphoreType.DMA((count, 3)),
            pltpu.SemaphoreType.DMA((count, 3)),
        ],
        compiler_params=pltpu.CompilerParams(collective_id=1, has_side_effects=True),
    )(fields, thermal, viscous)


def gradient(stencil):
    return (8.0 * (stencil[3] - stencil[1]) - (stencil[4] - stencil[0])) / 12.0


def curvature(stencil):
    return (16.0 * (stencil[3] + stencil[1]) - (stencil[4] + stencil[0]) - 30.0 * stencil[2]) / 12.0


def slope(stencil):
    return 8.0 * (stencil[3] - stencil[1]) - (stencil[4] - stencil[0])


def spread(stencil):
    return 16.0 * (stencil[3] + stencil[1]) - (stencil[4] + stencil[0]) - 30.0 * stencil[2]


def shifted(block, step):
    size = block.shape[-1]
    lane = lax.broadcasted_iota(jnp.int32, block.shape, block.ndim - 1)
    moved = pltpu.roll(block, (size - step) % size, block.ndim - 1)
    keep = jnp.logical_and(lane + step >= 0, lane + step < size)
    return jnp.where(keep, moved, 0.0)


def step_kernel(
    row_pad, col_pad, fields_ref, coefs_ref, rows_ref, cols_ref, frac_ref, trig_ref,
    out_ref, final_ref, row_out, col_out, row_send, col_send, send_sem, row_sem, col_sem,
):
    panel = lax.axis_index("panel")
    colat = lax.axis_index("colat")
    lon = lax.axis_index("lon")
    colat_count = lax.axis_size("colat")
    lon_count = lax.axis_size("lon")
    row_types = row_out.shape[0] // 2
    col_types = col_out.shape[0] // 2
    row_share = row_send.shape[1]
    other = 1 - panel

    def route(share, per_type, count):
        kind = share // per_type
        edge = (kind % 2) * (count - 1)
        slot = (kind // 2) * per_type + share % per_type
        return edge, slot

    row_edge, row_slot = route(colat, row_types, colat_count)
    col_edge, col_slot = route(lon, col_types, lon_count)
    row_dest = (other, row_edge, lon)
    col_dest = (other, colat, col_edge)
    at_row_edge = jnp.logical_or(colat == 0, colat == colat_count - 1)
    at_col_edge = jnp.logical_or(lon == 0, lon == lon_count - 1)
    parity_row = (colat // (colat_count - 1)).astype(jnp.int32)
    parity_col = (lon // (lon_count - 1)).astype(jnp.int32)

    def row_sender(slot):
        kind = 2 * (slot // row_types) + parity_row
        return (other, kind * row_types + slot % row_types, lon)

    def col_sender(slot):
        kind = 2 * (slot // col_types) + parity_col
        return (other, colat, kind * col_types + slot % col_types)

    barrier = pltpu.get_barrier_semaphore()
    pl.semaphore_signal(barrier, 1, device_id=row_dest, device_id_type=MESH)
    pl.semaphore_signal(barrier, 1, device_id=col_dest, device_id_type=MESH)

    @pl.when(at_row_edge)
    def _():
        for slot in range(2 * row_types):
            pl.semaphore_signal(barrier, 1, device_id=row_sender(slot), device_id_type=MESH)

    @pl.when(at_col_edge)
    def _():
        for slot in range(2 * col_types):
            pl.semaphore_signal(barrier, 1, device_id=col_sender(slot), device_id_type=MESH)

    ext_rows, span, radial_len = out_ref.shape[1], out_ref.shape[2], out_ref.shape[3]
    height = ext_rows - 2
    breadth = fields_ref.shape[2] - 2 * col_pad
    lead = (span - breadth) // 2
    col_ids = lax.broadcasted_iota(jnp.int32, (span, radial_len), 0) - lead + lon * breadth
    col_ok = jnp.logical_and(col_ids >= 0, col_ids < lon_count * breadth)

    def body(row, carry):
        global_row = row - 1 + colat * height
        ok = jnp.logical_and(col_ok, jnp.logical_and(global_row >= 0, global_row < colat_count * height))

        def load(field, down, across):
            return fields_ref[field, row + row_pad - 1 + down, pl.ds(col_pad - lead + across, span), :]

        center = [load(field, 0, 0) for field in range(4)]
        thermal = coefs_ref[0, row, pl.ds(col_pad - lead, span), :]
        viscous = coefs_ref[1, row, pl.ds(col_pad - lead, span), :]
        for field in range(4):
            along_lat = [load(field, offset - 2, 0) for offset in range(5)]
            along_lon = [load(field, 0, offset - 2) for offset in range(5)]
            along_rad = [shifted(center[field], offset - 2) for offset in range(5)]
            laplace = spread(along_rad) + spread(along_lat) + spread(along_lon)
            transport = (
                center[1] * slope(along_rad)
                + center[2] * slope(along_lat)
                + center[3] * slope(along_lon)
            )
            change = (thermal if field == 0 else viscous) * laplace - transport
            stepped_value = center[field] + (TIME_STEP / 12.0) * change
            if field == 1:
                stepped_value = stepped_value + (TIME_STEP * BUOYANCY) * center[0]
            out_ref[field, row] = jnp.where(ok, stepped_value, 0.0)
        return carry

    lax.fori_loop(0, ext_rows, body, 0)
    for field in range(4):
        final_ref[field] = out_ref[field, pl.ds(1, height), pl.ds(lead, breadth), :]

    slots = rows_ref.shape[0]
    column = lax.broadcasted_iota(jnp.int32, (span, radial_len), 0)
    for slot in range(slots):
        first = rows_ref[slot]
        across = cols_ref[slot] + (lead - 1)
        frac_row = frac_ref[0, slot]
        frac_lon = frac_ref[1, slot]
        weight = jnp.where(
            column == across, 1.0 - frac_lon, jnp.where(column == across + 1, frac_lon, 0.0)
        )
        mixed = []
        for field in range(4):
            upper = jnp.sum(weight * out_ref[field, first], axis=0, keepdims=True)
            lower = jnp.sum(weight * out_ref[field, first + 1], axis=0, keepdims=True)
            mixed.append((1.0 - frac_row) * upper + frac_row * lower)
        cosine = trig_ref[0, slot]
        sine_part = trig_ref[1, slot]
        turned = [
            mixed[0],
            mixed[1],
            cosine * mixed[2] - sine_part * mixed[3],
            sine_part * mixed[2] + cosine * mixed[3],
        ]
        for field in range(4):
            if slot < row_share:
                row_send[field, pl.ds(slot, 1), :] = turned[field]
            else:
                col_send[field, pl.ds(slot - row_share, 1), :] = turned[field]

    expected = (
        2
        + at_row_edge.astype(jnp.int32) * (2 * row_types)
        + at_col_edge.astype(jnp.int32) * (2 * col_types)
    )
    pl.semaphore_wait(barrier, expected)

    row_copy = pltpu.make_async_remote_copy(
        row_send, row_out.at[row_slot], send_sem.at[0], row_sem.at[row_slot],
        device_id=row_dest, device_id_type=MESH,
    )
    col_copy = pltpu.make_async_remote_copy(
        col_send, col_out.at[col_slot], send_sem.at[1], col_sem.at[col_slot],
        device_id=col_dest, device_id_type=MESH,
    )
    row_copy.start()
    col_copy.start()
    row_copy.wait_send()
    col_copy.wait_send()

    @pl.when(at_row_edge)
    def _():
        for slot in range(2 * row_types):
            pltpu.make_async_remote_copy(
                row_send, row_out.at[slot], send_sem.at[0], row_sem.at[slot],
                device_id=row_sender(slot), device_id_type=MESH,
            ).wait_recv()

    @pl.when(at_col_edge)
    def _():
        for slot in range(2 * col_types):
            pltpu.make_async_remote_copy(
                col_send, col_out.at[slot], send_sem.at[1], col_sem.at[slot],
                device_id=col_sender(slot), device_id_type=MESH,
            ).wait_recv()

    col_share = col_out.shape[2]

    def put_columns(first, second):
        for slot in range(2 * col_types):
            column = first if slot < col_types else second
            base = (slot % col_types) * col_share
            for field in range(4):
                for offset in range(col_share):
                    final_ref[field, base + offset, pl.ds(column, 1), :] = (
                        col_out[slot, field, pl.ds(offset, 1), :]
                    )

    def put_rows(first, second):
        for slot in range(2 * row_types):
            line = first if slot < row_types else second
            base = (slot % row_types) * row_share
            for field in range(4):
                final_ref[field, line, pl.ds(base, row_share), :] = row_out[slot, field]

    @pl.when(lon == 0)
    def _():
        put_columns(0, 1)

    @pl.when(lon == lon_count - 1)
    def _():
        put_columns(breadth - 1, breadth - 2)

    @pl.when(colat == 0)
    def _():
        put_rows(0, 1)

    @pl.when(colat == colat_count - 1)
    def _():
        put_rows(height - 1, height - 2)


def stepped(fields_pad, coefs_pad, row_pad, col_pad, lead, rows, cols, frac, trig, row_share):
    height = coefs_pad.shape[1] - 2
    breadth = fields_pad.shape[2] - 2 * col_pad
    span = breadth + 2 * lead
    radial_len = fields_pad.shape[3]
    slots = rows.shape[0]
    row_types = lax.axis_size("colat") // 4
    col_types = lax.axis_size("lon") // 4
    dtype = fields_pad.dtype
    vmem = pl.BlockSpec(memory_space=pltpu.VMEM)
    smem = pl.BlockSpec(memory_space=pltpu.SMEM)
    return pl.pallas_call(
        functools.partial(step_kernel, row_pad, col_pad),
        out_shape=(
            jax.ShapeDtypeStruct((4, height + 2, span, radial_len), dtype),
            jax.ShapeDtypeStruct((4, height, breadth, radial_len), dtype),
            jax.ShapeDtypeStruct((2 * row_types, 4, row_share, radial_len), dtype),
            jax.ShapeDtypeStruct((2 * col_types, 4, slots - row_share, radial_len), dtype),
        ),
        in_specs=[vmem, vmem, smem, smem, smem, smem],
        out_specs=(vmem, vmem, vmem, vmem),
        scratch_shapes=[
            pltpu.VMEM((4, row_share, radial_len), dtype),
            pltpu.VMEM((4, slots - row_share, radial_len), dtype),
            pltpu.SemaphoreType.DMA((2,)),
            pltpu.SemaphoreType.DMA((2 * row_types,)),
            pltpu.SemaphoreType.DMA((2 * col_types,)),
        ],
        compiler_params=pltpu.CompilerParams(collective_id=0, has_side_effects=True),
    )(fields_pad, coefs_pad, rows, cols, frac, trig)


def advance(padded, thermal, viscous):
    height = padded.shape[1] - 4
    breadth = padded.shape[2] - 4
    center = padded[:, 2 : 2 + height, 2 : 2 + breadth]
    radial_len = center.shape[3]
    radial_pad = jnp.pad(center, ((0, 0), (0, 0), (0, 0), (2, 2)))
    along_lat = [padded[:, offset : offset + height, 2 : 2 + breadth] for offset in range(5)]
    along_lon = [padded[:, 2 : 2 + height, offset : offset + breadth] for offset in range(5)]
    along_rad = [radial_pad[..., offset : offset + radial_len] for offset in range(5)]
    laplace = curvature(along_rad) + curvature(along_lat) + curvature(along_lon)
    transport = (
        center[1:2] * gradient(along_rad)
        + center[2:3] * gradient(along_lat)
        + center[3:4] * gradient(along_lon)
    )
    diffusion = jnp.stack([thermal, viscous, viscous, viscous])
    change = diffusion * laplace - transport
    change = change.at[1].add(BUOYANCY * center[0])
    return center + TIME_STEP * change


def local(fields_now, diffusivity, viscosity, donor_row, donor_column, donor_offset, rim_angle):
    fields = fields_now[:, 0]
    thermal = diffusivity[0]
    viscous = viscosity[0]
    height = fields.shape[1]
    breadth = fields.shape[2]
    radial_len = fields.shape[3]
    colat_pos = lax.axis_index("colat")
    lon_pos = lax.axis_index("lon")
    colat_count = lax.axis_size("colat")
    lon_count = lax.axis_size("lon")
    row_share = 4 * breadth // colat_count
    fields_pad, coefs_pad = halo_exchange(fields, thermal, viscous, 3)
    lead = 4
    angles = rim_angle.reshape(-1)
    trig = jnp.stack([jnp.cos(angles), jnp.sin(angles)])
    frac = donor_offset.reshape(2, -1)
    extended, fresh, row_buf, col_buf = stepped(
        fields_pad, coefs_pad, 3, 12, lead, donor_row.reshape(-1), donor_column.reshape(-1),
        frac, trig, row_share,
    )
    return fresh[:, None]


def solution(mesh):
    placed = (
        P(None, "panel", "colat", "lon", None),
        P("panel", "colat", "lon", None),
        P("panel", "colat", "lon", None),
        P("panel", "colat", "lon", None),
        P("panel", "colat", "lon", None),
        P("panel", "colat", "lon", None, None),
        P("panel", "colat", "lon", None),
    )
    return jax.shard_map(
        local,
        mesh=mesh,
        in_specs=placed,
        out_specs=P(None, "panel", "colat", "lon", None),
        check_vma=False,
    )
```

```python
import functools

import jax
import jax.numpy as jnp
from jax import lax
from jax.sharding import PartitionSpec as P
from jax.experimental import pallas as pl
from jax.experimental.pallas import tpu as pltpu

MESH = pl.DeviceIdType.MESH

TIME_STEP = 0.05
BUOYANCY = 1.0


def with_halo(x, sides, width):
    for axis, dim in sides:
        count, length = (lax.axis_size(axis), x.shape[dim])
        up = [(i, (i + 1) % count) for i in range(count - 1)]
        down = [(j, i) for i, j in up]
        last = lax.slice_in_dim(x, length - width, length, axis=dim)
        leading = lax.slice_in_dim(x, 0, width, axis=dim)
        before = lax.ppermute(last, axis, up)
        after = lax.ppermute(leading, axis, down)
        x = jnp.concatenate([before, x, after], axis=dim)
    return x


def swapped(block, axis, stride):
    count = lax.axis_size(axis)
    route = []
    for low in range(count):
        high = low | 1 << stride
        if high != low and high < count:
            route += [(low, high), (high, low)]
    return lax.ppermute(block, axis, route)


DIRECTIONS = ((-1, -1), (-1, 0), (-1, 1), (0, -1), (0, 1), (1, -1), (1, 0), (1, 1))


def window(step, width, length, offset):
    if step < 0:
        return offset, width
    if step > 0:
        return offset + length - width, width
    return offset, length


def landing(step, width, length, offset):
    if step < 0:
        return offset - width, width
    if step > 0:
        return offset + length, width
    return offset, length


def halo_kernel(width, margins, fields_in, thermal_in, viscous_in, fields_out, coefs_out, send_sem, recv_sem):
    count = len(DIRECTIONS)
    panel = lax.axis_index("panel")
    colat = lax.axis_index("colat")
    lon = lax.axis_index("lon")
    colat_count = lax.axis_size("colat")
    lon_count = lax.axis_size("lon")
    height, breadth = fields_in.shape[1], fields_in.shape[2]

    for out, (row_pad, col_pad) in ((fields_out, margins[0]), (coefs_out, margins[1])):
        lead = out.shape[:1]
        total_rows, total_cols = out.shape[1], out.shape[2]
        out[:, pl.ds(0, row_pad)] = jnp.zeros(lead + (row_pad, total_cols, out.shape[3]), out.dtype)
        out[:, pl.ds(row_pad + height, row_pad)] = jnp.zeros(
            lead + (row_pad, total_cols, out.shape[3]), out.dtype
        )
        side = jnp.zeros(lead + (height, col_pad, out.shape[3]), out.dtype)
        out[:, pl.ds(row_pad, height), pl.ds(0, col_pad)] = side
        out[:, pl.ds(row_pad, height), pl.ds(col_pad + breadth, total_cols - col_pad - breadth)] = side
    fields_out[:, pl.ds(margins[0][0], height), pl.ds(margins[0][1], breadth)] = fields_in[...]
    coefs_out[0, pl.ds(margins[1][0], height), pl.ds(margins[1][1], breadth)] = thermal_in[...]
    coefs_out[1, pl.ds(margins[1][0], height), pl.ds(margins[1][1], breadth)] = viscous_in[...]

    def present(step):
        row = colat + step[0]
        col = lon + step[1]
        inside = jnp.logical_and(row >= 0, row < colat_count)
        return jnp.logical_and(inside, jnp.logical_and(col >= 0, col < lon_count))

    def source(part, step):
        depth = width if part == 0 else 1
        rows = window(step[0], depth, height, 0)
        cols = window(step[1], depth, breadth, 0)
        ref = (fields_in, thermal_in, viscous_in)[part]
        if part == 0:
            return ref.at[:, pl.ds(rows[0], rows[1]), pl.ds(cols[0], cols[1]), :]
        return ref.at[pl.ds(rows[0], rows[1]), pl.ds(cols[0], cols[1]), :]

    def target(part, step):
        depth = width if part == 0 else 1
        row_pad, col_pad = margins[0] if part == 0 else margins[1]
        rows = landing(step[0], depth, height, row_pad)
        cols = landing(step[1], depth, breadth, col_pad)
        if part == 0:
            return fields_out.at[:, pl.ds(rows[0], rows[1]), pl.ds(cols[0], cols[1]), :]
        return coefs_out.at[part - 1, pl.ds(rows[0], rows[1]), pl.ds(cols[0], cols[1]), :]

    def outgoing(index, part):
        step = DIRECTIONS[index]
        back = tuple(-s for s in step)
        return pltpu.make_async_remote_copy(
            source(part, step), target(part, back),
            send_sem.at[index, part], recv_sem.at[count - 1 - index, part],
            device_id=(panel, colat + step[0], lon + step[1]), device_id_type=MESH,
        )

    def incoming(index, part):
        step = DIRECTIONS[index]
        spot = target(part, step)
        return pltpu.make_async_remote_copy(
            spot, spot, send_sem.at[index, part], recv_sem.at[index, part],
            device_id=(panel, colat + step[0], lon + step[1]), device_id_type=MESH,
        )

    barrier = pltpu.get_barrier_semaphore()
    expected = jnp.int32(0)
    for index, step in enumerate(DIRECTIONS):
        exists = present(step)
        expected = expected + exists.astype(jnp.int32)

        @pl.when(exists)
        def _():
            pl.semaphore_signal(
                barrier, 1, device_id=(panel, colat + step[0], lon + step[1]),
                device_id_type=MESH,
            )

    pl.semaphore_wait(barrier, expected)
    for index, step in enumerate(DIRECTIONS):

        @pl.when(present(step))
        def _():
            for part in range(3):
                outgoing(index, part).start()

    for index, step in enumerate(DIRECTIONS):

        @pl.when(present(step))
        def _():
            for part in range(3):
                outgoing(index, part).wait_send()
            for part in range(3):
                incoming(index, part).wait_recv()


def halo_exchange(fields, thermal, viscous, width):
    lane_pad = 8
    height, breadth, radial_len = fields.shape[1], fields.shape[2], fields.shape[3]
    margins = ((width, lane_pad), (1, lane_pad))
    vmem = pl.BlockSpec(memory_space=pltpu.VMEM)
    count = len(DIRECTIONS)
    return pl.pallas_call(
        functools.partial(halo_kernel, width, margins),
        out_shape=(
            jax.ShapeDtypeStruct(
                (4, height + 2 * width, breadth + 2 * lane_pad, radial_len), fields.dtype
            ),
            jax.ShapeDtypeStruct((2, height + 2, breadth + 2 * lane_pad, radial_len), fields.dtype),
        ),
        in_specs=[vmem, vmem, vmem],
        out_specs=(vmem, vmem),
        scratch_shapes=[
            pltpu.SemaphoreType.DMA((count, 3)),
            pltpu.SemaphoreType.DMA((count, 3)),
        ],
        compiler_params=pltpu.CompilerParams(collective_id=1, has_side_effects=True),
    )(fields, thermal, viscous)


def gradient(stencil):
    return (8.0 * (stencil[3] - stencil[1]) - (stencil[4] - stencil[0])) / 12.0


def curvature(stencil):
    return (16.0 * (stencil[3] + stencil[1]) - (stencil[4] + stencil[0]) - 30.0 * stencil[2]) / 12.0


def slope(stencil):
    return 8.0 * (stencil[3] - stencil[1]) - (stencil[4] - stencil[0])


def spread(stencil):
    return 16.0 * (stencil[3] + stencil[1]) - (stencil[4] + stencil[0]) - 30.0 * stencil[2]


def shifted(block, step):
    size = block.shape[-1]
    lane = lax.broadcasted_iota(jnp.int32, block.shape, block.ndim - 1)
    moved = pltpu.roll(block, (size - step) % size, block.ndim - 1)
    keep = jnp.logical_and(lane + step >= 0, lane + step < size)
    return jnp.where(keep, moved, 0.0)


def step_kernel(
    row_pad, col_pad, fields_ref, coefs_ref, rows_ref, cols_ref, frac_ref, trig_ref,
    out_ref, final_hbm, row_out, col_out, row_send, col_send, block_sem,
    send_sem, row_sem, col_sem,
):
    panel = lax.axis_index("panel")
    colat = lax.axis_index("colat")
    lon = lax.axis_index("lon")
    colat_count = lax.axis_size("colat")
    lon_count = lax.axis_size("lon")
    row_types = row_out.shape[0] // 2
    col_types = col_out.shape[0] // 2
    row_share = row_send.shape[1]
    other = 1 - panel

    def route(share, per_type, count):
        kind = share // per_type
        edge = (kind % 2) * (count - 1)
        slot = (kind // 2) * per_type + share % per_type
        return edge, slot

    row_edge, row_slot = route(colat, row_types, colat_count)
    col_edge, col_slot = route(lon, col_types, lon_count)
    row_dest = (other, row_edge, lon)
    col_dest = (other, colat, col_edge)
    at_row_edge = jnp.logical_or(colat == 0, colat == colat_count - 1)
    at_col_edge = jnp.logical_or(lon == 0, lon == lon_count - 1)
    parity_row = (colat // (colat_count - 1)).astype(jnp.int32)
    parity_col = (lon // (lon_count - 1)).astype(jnp.int32)

    def row_sender(slot):
        kind = 2 * (slot // row_types) + parity_row
        return (other, kind * row_types + slot % row_types, lon)

    def col_sender(slot):
        kind = 2 * (slot // col_types) + parity_col
        return (other, colat, kind * col_types + slot % col_types)

    barrier = pltpu.get_barrier_semaphore()
    pl.semaphore_signal(barrier, 1, device_id=row_dest, device_id_type=MESH)
    pl.semaphore_signal(barrier, 1, device_id=col_dest, device_id_type=MESH)

    @pl.when(at_row_edge)
    def _():
        for slot in range(2 * row_types):
            pl.semaphore_signal(barrier, 1, device_id=row_sender(slot), device_id_type=MESH)

    @pl.when(at_col_edge)
    def _():
        for slot in range(2 * col_types):
            pl.semaphore_signal(barrier, 1, device_id=col_sender(slot), device_id_type=MESH)

    ext_rows, span, radial_len = out_ref.shape[1], out_ref.shape[2], out_ref.shape[3]
    height = ext_rows - 2
    breadth = fields_ref.shape[2] - 2 * col_pad
    lead = (span - breadth) // 2
    col_ids = lax.broadcasted_iota(jnp.int32, (span, radial_len), 0) - lead + lon * breadth
    col_ok = jnp.logical_and(col_ids >= 0, col_ids < lon_count * breadth)

    def body(row, carry):
        global_row = row - 1 + colat * height
        ok = jnp.logical_and(col_ok, jnp.logical_and(global_row >= 0, global_row < colat_count * height))

        def load(field, down, across):
            return fields_ref[field, row + row_pad - 1 + down, pl.ds(col_pad - lead + across, span), :]

        center = [load(field, 0, 0) for field in range(4)]
        thermal = coefs_ref[0, row, pl.ds(col_pad - lead, span), :]
        viscous = coefs_ref[1, row, pl.ds(col_pad - lead, span), :]
        for field in range(4):
            along_lat = [load(field, offset - 2, 0) for offset in range(5)]
            along_lon = [load(field, 0, offset - 2) for offset in range(5)]
            along_rad = [shifted(center[field], offset - 2) for offset in range(5)]
            laplace = spread(along_rad) + spread(along_lat) + spread(along_lon)
            transport = (
                center[1] * slope(along_rad)
                + center[2] * slope(along_lat)
                + center[3] * slope(along_lon)
            )
            change = (thermal if field == 0 else viscous) * laplace - transport
            stepped_value = center[field] + (TIME_STEP / 12.0) * change
            if field == 1:
                stepped_value = stepped_value + (TIME_STEP * BUOYANCY) * center[0]
            out_ref[field, row] = jnp.where(ok, stepped_value, 0.0)
        return carry

    lax.fori_loop(0, ext_rows, body, 0)
    whole = pltpu.make_async_copy(
        out_ref.at[:, pl.ds(1, height), pl.ds(lead, breadth), :], final_hbm, block_sem.at[0]
    )
    whole.start()

    slots = rows_ref.shape[0]
    column = lax.broadcasted_iota(jnp.int32, (span, radial_len), 0)
    for slot in range(slots):
        first = rows_ref[slot]
        across = cols_ref[slot] + (lead - 1)
        frac_row = frac_ref[0, slot]
        frac_lon = frac_ref[1, slot]
        weight = jnp.where(
            column == across, 1.0 - frac_lon, jnp.where(column == across + 1, frac_lon, 0.0)
        )
        mixed = []
        for field in range(4):
            upper = jnp.sum(weight * out_ref[field, first], axis=0, keepdims=True)
            lower = jnp.sum(weight * out_ref[field, first + 1], axis=0, keepdims=True)
            mixed.append((1.0 - frac_row) * upper + frac_row * lower)
        cosine = trig_ref[0, slot]
        sine_part = trig_ref[1, slot]
        turned = [
            mixed[0],
            mixed[1],
            cosine * mixed[2] - sine_part * mixed[3],
            sine_part * mixed[2] + cosine * mixed[3],
        ]
        for field in range(4):
            if slot < row_share:
                row_send[field, pl.ds(slot, 1), :] = turned[field]
            else:
                col_send[field, pl.ds(slot - row_share, 1), :] = turned[field]

    expected = (
        2
        + at_row_edge.astype(jnp.int32) * (2 * row_types)
        + at_col_edge.astype(jnp.int32) * (2 * col_types)
    )
    pl.semaphore_wait(barrier, expected)

    row_copy = pltpu.make_async_remote_copy(
        row_send, row_out.at[row_slot], send_sem.at[0], row_sem.at[row_slot],
        device_id=row_dest, device_id_type=MESH,
    )
    col_copy = pltpu.make_async_remote_copy(
        col_send, col_out.at[col_slot], send_sem.at[1], col_sem.at[col_slot],
        device_id=col_dest, device_id_type=MESH,
    )
    row_copy.start()
    col_copy.start()
    row_copy.wait_send()
    col_copy.wait_send()

    @pl.when(at_row_edge)
    def _():
        for slot in range(2 * row_types):
            pltpu.make_async_remote_copy(
                row_send, row_out.at[slot], send_sem.at[0], row_sem.at[slot],
                device_id=row_sender(slot), device_id_type=MESH,
            ).wait_recv()

    @pl.when(at_col_edge)
    def _():
        for slot in range(2 * col_types):
            pltpu.make_async_remote_copy(
                col_send, col_out.at[slot], send_sem.at[1], col_sem.at[slot],
                device_id=col_sender(slot), device_id_type=MESH,
            ).wait_recv()

    col_share = col_out.shape[2]
    whole.wait()

    def put_columns(first, second):
        for slot in range(2 * col_types):
            column = first if slot < col_types else second
            base = (slot % col_types) * col_share
            for field in range(4):
                for offset in range(col_share):
                    out_ref[field, 1 + base + offset, pl.ds(lead + column, 1), :] = (
                        col_out[slot, field, pl.ds(offset, 1), :]
                    )

    def put_rows(first, second):
        for slot in range(2 * row_types):
            line = first if slot < row_types else second
            base = (slot % row_types) * row_share
            for field in range(4):
                out_ref[field, 1 + line, pl.ds(lead + base, row_share), :] = row_out[slot, field]

    @pl.when(lon == 0)
    def _():
        put_columns(0, 1)

    @pl.when(lon == lon_count - 1)
    def _():
        put_columns(breadth - 1, breadth - 2)

    @pl.when(colat == 0)
    def _():
        put_rows(0, 1)

    @pl.when(colat == colat_count - 1)
    def _():
        put_rows(height - 1, height - 2)

    def patch(rows, cols):
        part = pltpu.make_async_copy(
            out_ref.at[:, pl.ds(1 + rows[0], rows[1]), pl.ds(lead + cols[0], cols[1]), :],
            final_hbm.at[:, pl.ds(rows[0], rows[1]), pl.ds(cols[0], cols[1]), :],
            block_sem.at[1],
        )
        part.start()
        part.wait()

    @pl.when(lon == 0)
    def _():
        patch((0, height), (0, 2))

    @pl.when(lon == lon_count - 1)
    def _():
        patch((0, height), (breadth - 2, 2))

    @pl.when(colat == 0)
    def _():
        patch((0, 2), (0, breadth))

    @pl.when(colat == colat_count - 1)
    def _():
        patch((height - 2, 2), (0, breadth))


def stepped(fields_pad, coefs_pad, row_pad, col_pad, lead, rows, cols, frac, trig, row_share):
    height = coefs_pad.shape[1] - 2
    breadth = fields_pad.shape[2] - 2 * col_pad
    span = breadth + 2 * lead
    radial_len = fields_pad.shape[3]
    slots = rows.shape[0]
    row_types = lax.axis_size("colat") // 4
    col_types = lax.axis_size("lon") // 4
    dtype = fields_pad.dtype
    vmem = pl.BlockSpec(memory_space=pltpu.VMEM)
    smem = pl.BlockSpec(memory_space=pltpu.SMEM)
    return pl.pallas_call(
        functools.partial(step_kernel, row_pad, col_pad),
        out_shape=(
            jax.ShapeDtypeStruct((4, height + 2, span, radial_len), dtype),
            jax.ShapeDtypeStruct((4, height, breadth, radial_len), dtype),
            jax.ShapeDtypeStruct((2 * row_types, 4, row_share, radial_len), dtype),
            jax.ShapeDtypeStruct((2 * col_types, 4, slots - row_share, radial_len), dtype),
        ),
        in_specs=[vmem, vmem, smem, smem, smem, smem],
        out_specs=(vmem, pl.BlockSpec(memory_space=pl.ANY), vmem, vmem),
        scratch_shapes=[
            pltpu.VMEM((4, row_share, radial_len), dtype),
            pltpu.VMEM((4, slots - row_share, radial_len), dtype),
            pltpu.SemaphoreType.DMA((2,)),
            pltpu.SemaphoreType.DMA((2,)),
            pltpu.SemaphoreType.DMA((2 * row_types,)),
            pltpu.SemaphoreType.DMA((2 * col_types,)),
        ],
        compiler_params=pltpu.CompilerParams(collective_id=0, has_side_effects=True),
    )(fields_pad, coefs_pad, rows, cols, frac, trig)


def advance(padded, thermal, viscous):
    height = padded.shape[1] - 4
    breadth = padded.shape[2] - 4
    center = padded[:, 2 : 2 + height, 2 : 2 + breadth]
    radial_len = center.shape[3]
    radial_pad = jnp.pad(center, ((0, 0), (0, 0), (0, 0), (2, 2)))
    along_lat = [padded[:, offset : offset + height, 2 : 2 + breadth] for offset in range(5)]
    along_lon = [padded[:, 2 : 2 + height, offset : offset + breadth] for offset in range(5)]
    along_rad = [radial_pad[..., offset : offset + radial_len] for offset in range(5)]
    laplace = curvature(along_rad) + curvature(along_lat) + curvature(along_lon)
    transport = (
        center[1:2] * gradient(along_rad)
        + center[2:3] * gradient(along_lat)
        + center[3:4] * gradient(along_lon)
    )
    diffusion = jnp.stack([thermal, viscous, viscous, viscous])
    change = diffusion * laplace - transport
    change = change.at[1].add(BUOYANCY * center[0])
    return center + TIME_STEP * change


def local(fields_now, diffusivity, viscosity, donor_row, donor_column, donor_offset, rim_angle):
    fields = fields_now[:, 0]
    thermal = diffusivity[0]
    viscous = viscosity[0]
    height = fields.shape[1]
    breadth = fields.shape[2]
    radial_len = fields.shape[3]
    colat_pos = lax.axis_index("colat")
    lon_pos = lax.axis_index("lon")
    colat_count = lax.axis_size("colat")
    lon_count = lax.axis_size("lon")
    row_share = 4 * breadth // colat_count
    fields_pad, coefs_pad = halo_exchange(fields, thermal, viscous, 3)
    lead = 4
    angles = rim_angle.reshape(-1)
    trig = jnp.stack([jnp.cos(angles), jnp.sin(angles)])
    frac = donor_offset.reshape(2, -1)
    extended, fresh, row_buf, col_buf = stepped(
        fields_pad, coefs_pad, 3, 8, lead, donor_row.reshape(-1), donor_column.reshape(-1),
        frac, trig, row_share,
    )
    return fresh[:, None]


def solution(mesh):
    placed = (
        P(None, "panel", "colat", "lon", None),
        P("panel", "colat", "lon", None),
        P("panel", "colat", "lon", None),
        P("panel", "colat", "lon", None),
        P("panel", "colat", "lon", None),
        P("panel", "colat", "lon", None, None),
        P("panel", "colat", "lon", None),
    )
    return jax.shard_map(
        local,
        mesh=mesh,
        in_specs=placed,
        out_specs=P(None, "panel", "colat", "lon", None),
        check_vma=False,
    )
```

```python
import functools

import jax
import jax.numpy as jnp
from jax import lax
from jax.sharding import PartitionSpec as P
from jax.experimental import pallas as pl
from jax.experimental.pallas import tpu as pltpu

MESH = pl.DeviceIdType.MESH

TIME_STEP = 0.05
BUOYANCY = 1.0


def with_halo(x, sides, width):
    for axis, dim in sides:
        count, length = (lax.axis_size(axis), x.shape[dim])
        up = [(i, (i + 1) % count) for i in range(count - 1)]
        down = [(j, i) for i, j in up]
        last = lax.slice_in_dim(x, length - width, length, axis=dim)
        leading = lax.slice_in_dim(x, 0, width, axis=dim)
        before = lax.ppermute(last, axis, up)
        after = lax.ppermute(leading, axis, down)
        x = jnp.concatenate([before, x, after], axis=dim)
    return x


def swapped(block, axis, stride):
    count = lax.axis_size(axis)
    route = []
    for low in range(count):
        high = low | 1 << stride
        if high != low and high < count:
            route += [(low, high), (high, low)]
    return lax.ppermute(block, axis, route)


DIRECTIONS = ((-1, -1), (-1, 0), (-1, 1), (0, -1), (0, 1), (1, -1), (1, 0), (1, 1))


def window(step, width, length, offset):
    if step < 0:
        return offset, width
    if step > 0:
        return offset + length - width, width
    return offset, length


def landing(step, width, length, offset):
    if step < 0:
        return offset - width, width
    if step > 0:
        return offset + length, width
    return offset, length


def part_rank(step, part):
    sides = abs(step[0]) + abs(step[1])
    if part == 0 and step[1] == 0:
        return 0
    if part == 0 and sides == 1:
        return 1
    return 2 + part + sides


def halo_kernel(width, margins, fields_in, thermal_in, viscous_in, fields_out, coefs_out, send_sem, recv_sem):
    count = len(DIRECTIONS)
    panel = lax.axis_index("panel")
    colat = lax.axis_index("colat")
    lon = lax.axis_index("lon")
    colat_count = lax.axis_size("colat")
    lon_count = lax.axis_size("lon")
    height, breadth = fields_in.shape[1], fields_in.shape[2]

    for out, (row_pad, col_pad) in ((fields_out, margins[0]), (coefs_out, margins[1])):
        lead = out.shape[:1]
        total_rows, total_cols = out.shape[1], out.shape[2]
        out[:, pl.ds(0, row_pad)] = jnp.zeros(lead + (row_pad, total_cols, out.shape[3]), out.dtype)
        out[:, pl.ds(row_pad + height, row_pad)] = jnp.zeros(
            lead + (row_pad, total_cols, out.shape[3]), out.dtype
        )
        side = jnp.zeros(lead + (height, col_pad, out.shape[3]), out.dtype)
        out[:, pl.ds(row_pad, height), pl.ds(0, col_pad)] = side
        out[:, pl.ds(row_pad, height), pl.ds(col_pad + breadth, total_cols - col_pad - breadth)] = side
    fields_out[:, pl.ds(margins[0][0], height), pl.ds(margins[0][1], breadth)] = fields_in[...]
    coefs_out[0, pl.ds(margins[1][0], height), pl.ds(margins[1][1], breadth)] = thermal_in[...]
    coefs_out[1, pl.ds(margins[1][0], height), pl.ds(margins[1][1], breadth)] = viscous_in[...]

    def present(step):
        row = colat + step[0]
        col = lon + step[1]
        inside = jnp.logical_and(row >= 0, row < colat_count)
        return jnp.logical_and(inside, jnp.logical_and(col >= 0, col < lon_count))

    def source(part, step):
        depth = width if part == 0 else 1
        rows = window(step[0], depth, height, 0)
        cols = window(step[1], depth, breadth, 0)
        ref = (fields_in, thermal_in, viscous_in)[part]
        if part == 0:
            return ref.at[:, pl.ds(rows[0], rows[1]), pl.ds(cols[0], cols[1]), :]
        return ref.at[pl.ds(rows[0], rows[1]), pl.ds(cols[0], cols[1]), :]

    def target(part, step):
        depth = width if part == 0 else 1
        row_pad, col_pad = margins[0] if part == 0 else margins[1]
        rows = landing(step[0], depth, height, row_pad)
        cols = landing(step[1], depth, breadth, col_pad)
        if part == 0:
            return fields_out.at[:, pl.ds(rows[0], rows[1]), pl.ds(cols[0], cols[1]), :]
        return coefs_out.at[part - 1, pl.ds(rows[0], rows[1]), pl.ds(cols[0], cols[1]), :]

    def outgoing(index, part):
        step = DIRECTIONS[index]
        back = tuple(-s for s in step)
        return pltpu.make_async_remote_copy(
            source(part, step), target(part, back),
            send_sem.at[index, part], recv_sem.at[count - 1 - index, part],
            device_id=(panel, colat + step[0], lon + step[1]), device_id_type=MESH,
        )

    def incoming(index, part):
        step = DIRECTIONS[index]
        spot = target(part, step)
        return pltpu.make_async_remote_copy(
            spot, spot, send_sem.at[index, part], recv_sem.at[index, part],
            device_id=(panel, colat + step[0], lon + step[1]), device_id_type=MESH,
        )

    barrier = pltpu.get_barrier_semaphore()
    expected = jnp.int32(0)
    for index, step in enumerate(DIRECTIONS):
        exists = present(step)
        expected = expected + exists.astype(jnp.int32)

        @pl.when(exists)
        def _():
            pl.semaphore_signal(
                barrier, 1, device_id=(panel, colat + step[0], lon + step[1]),
                device_id_type=MESH,
            )

    pl.semaphore_wait(barrier, expected)
    by_size = sorted(
        ((index, part) for index in range(count) for part in range(3)),
        key=lambda item: (part_rank(DIRECTIONS[item[0]], item[1]), item[0], item[1]),
    )
    for index, part in by_size:

        @pl.when(present(DIRECTIONS[index]))
        def _():
            outgoing(index, part).start()

    for index, step in enumerate(DIRECTIONS):

        @pl.when(present(step))
        def _():
            for part in range(3):
                outgoing(index, part).wait_send()
            for part in range(3):
                incoming(index, part).wait_recv()


def halo_exchange(fields, thermal, viscous, width):
    lane_pad = 8
    height, breadth, radial_len = fields.shape[1], fields.shape[2], fields.shape[3]
    margins = ((width, lane_pad), (1, lane_pad))
    vmem = pl.BlockSpec(memory_space=pltpu.VMEM)
    count = len(DIRECTIONS)
    return pl.pallas_call(
        functools.partial(halo_kernel, width, margins),
        out_shape=(
            jax.ShapeDtypeStruct(
                (4, height + 2 * width, breadth + 2 * lane_pad, radial_len), fields.dtype
            ),
            jax.ShapeDtypeStruct((2, height + 2, breadth + 2 * lane_pad, radial_len), fields.dtype),
        ),
        in_specs=[vmem, vmem, vmem],
        out_specs=(vmem, vmem),
        scratch_shapes=[
            pltpu.SemaphoreType.DMA((count, 3)),
            pltpu.SemaphoreType.DMA((count, 3)),
        ],
        compiler_params=pltpu.CompilerParams(collective_id=1, has_side_effects=True),
    )(fields, thermal, viscous)


def gradient(stencil):
    return (8.0 * (stencil[3] - stencil[1]) - (stencil[4] - stencil[0])) / 12.0


def curvature(stencil):
    return (16.0 * (stencil[3] + stencil[1]) - (stencil[4] + stencil[0]) - 30.0 * stencil[2]) / 12.0


def slope(stencil):
    return 8.0 * (stencil[3] - stencil[1]) - (stencil[4] - stencil[0])


def spread(stencil):
    return 16.0 * (stencil[3] + stencil[1]) - (stencil[4] + stencil[0]) - 30.0 * stencil[2]


def shifted(block, step):
    size = block.shape[-1]
    lane = lax.broadcasted_iota(jnp.int32, block.shape, block.ndim - 1)
    moved = pltpu.roll(block, (size - step) % size, block.ndim - 1)
    keep = jnp.logical_and(lane + step >= 0, lane + step < size)
    return jnp.where(keep, moved, 0.0)


def step_kernel(
    row_pad, col_pad, fields_ref, coefs_ref, rows_ref, cols_ref, frac_ref, trig_ref,
    out_ref, final_ref, row_out, col_out, row_send, col_send, send_sem, row_sem, col_sem,
):
    panel = lax.axis_index("panel")
    colat = lax.axis_index("colat")
    lon = lax.axis_index("lon")
    colat_count = lax.axis_size("colat")
    lon_count = lax.axis_size("lon")
    row_types = row_out.shape[0] // 2
    col_types = col_out.shape[0] // 2
    row_share = row_send.shape[1]
    other = 1 - panel

    def route(share, per_type, count):
        kind = share // per_type
        edge = (kind % 2) * (count - 1)
        slot = (kind // 2) * per_type + share % per_type
        return edge, slot

    row_edge, row_slot = route(colat, row_types, colat_count)
    col_edge, col_slot = route(lon, col_types, lon_count)
    row_dest = (other, row_edge, lon)
    col_dest = (other, colat, col_edge)
    at_row_edge = jnp.logical_or(colat == 0, colat == colat_count - 1)
    at_col_edge = jnp.logical_or(lon == 0, lon == lon_count - 1)
    parity_row = (colat // (colat_count - 1)).astype(jnp.int32)
    parity_col = (lon // (lon_count - 1)).astype(jnp.int32)

    def row_sender(slot):
        kind = 2 * (slot // row_types) + parity_row
        return (other, kind * row_types + slot % row_types, lon)

    def col_sender(slot):
        kind = 2 * (slot // col_types) + parity_col
        return (other, colat, kind * col_types + slot % col_types)

    barrier = pltpu.get_barrier_semaphore()
    pl.semaphore_signal(barrier, 1, device_id=row_dest, device_id_type=MESH)
    pl.semaphore_signal(barrier, 1, device_id=col_dest, device_id_type=MESH)

    @pl.when(at_row_edge)
    def _():
        for slot in range(2 * row_types):
            pl.semaphore_signal(barrier, 1, device_id=row_sender(slot), device_id_type=MESH)

    @pl.when(at_col_edge)
    def _():
        for slot in range(2 * col_types):
            pl.semaphore_signal(barrier, 1, device_id=col_sender(slot), device_id_type=MESH)

    ext_rows, span, radial_len = out_ref.shape[1], out_ref.shape[2], out_ref.shape[3]
    height = ext_rows - 2
    breadth = fields_ref.shape[2] - 2 * col_pad
    lead = (span - breadth) // 2
    col_ids = lax.broadcasted_iota(jnp.int32, (span, radial_len), 0) - lead + lon * breadth
    col_ok = jnp.logical_and(col_ids >= 0, col_ids < lon_count * breadth)

    def body(row, carry):
        global_row = row - 1 + colat * height
        ok = jnp.logical_and(col_ok, jnp.logical_and(global_row >= 0, global_row < colat_count * height))

        def load(field, down, across):
            return fields_ref[field, row + row_pad - 1 + down, pl.ds(col_pad - lead + across, span), :]

        center = [load(field, 0, 0) for field in range(4)]
        thermal = coefs_ref[0, row, pl.ds(col_pad - lead, span), :]
        viscous = coefs_ref[1, row, pl.ds(col_pad - lead, span), :]
        for field in range(4):
            along_lat = [load(field, offset - 2, 0) for offset in range(5)]
            along_lon = [load(field, 0, offset - 2) for offset in range(5)]
            along_rad = [shifted(center[field], offset - 2) for offset in range(5)]
            laplace = spread(along_rad) + spread(along_lat) + spread(along_lon)
            transport = (
                center[1] * slope(along_rad)
                + center[2] * slope(along_lat)
                + center[3] * slope(along_lon)
            )
            change = (thermal if field == 0 else viscous) * laplace - transport
            stepped_value = center[field] + (TIME_STEP / 12.0) * change
            if field == 1:
                stepped_value = stepped_value + (TIME_STEP * BUOYANCY) * center[0]
            out_ref[field, row] = jnp.where(ok, stepped_value, 0.0)
        return carry

    lax.fori_loop(0, ext_rows, body, 0)
    for field in range(4):
        final_ref[field] = out_ref[field, pl.ds(1, height), pl.ds(lead, breadth), :]

    slots = rows_ref.shape[0]
    column = lax.broadcasted_iota(jnp.int32, (span, radial_len), 0)
    for slot in range(slots):
        first = rows_ref[slot]
        across = cols_ref[slot] + (lead - 1)
        frac_row = frac_ref[0, slot]
        frac_lon = frac_ref[1, slot]
        weight = jnp.where(
            column == across, 1.0 - frac_lon, jnp.where(column == across + 1, frac_lon, 0.0)
        )
        mixed = []
        for field in range(4):
            upper = jnp.sum(weight * out_ref[field, first], axis=0, keepdims=True)
            lower = jnp.sum(weight * out_ref[field, first + 1], axis=0, keepdims=True)
            mixed.append((1.0 - frac_row) * upper + frac_row * lower)
        cosine = trig_ref[0, slot]
        sine_part = trig_ref[1, slot]
        turned = [
            mixed[0],
            mixed[1],
            cosine * mixed[2] - sine_part * mixed[3],
            sine_part * mixed[2] + cosine * mixed[3],
        ]
        for field in range(4):
            if slot < row_share:
                row_send[field, pl.ds(slot, 1), :] = turned[field]
            else:
                col_send[field, pl.ds(slot - row_share, 1), :] = turned[field]

    expected = (
        2
        + at_row_edge.astype(jnp.int32) * (2 * row_types)
        + at_col_edge.astype(jnp.int32) * (2 * col_types)
    )
    pl.semaphore_wait(barrier, expected)

    row_copy = pltpu.make_async_remote_copy(
        row_send, row_out.at[row_slot], send_sem.at[0], row_sem.at[row_slot],
        device_id=row_dest, device_id_type=MESH,
    )
    col_copy = pltpu.make_async_remote_copy(
        col_send, col_out.at[col_slot], send_sem.at[1], col_sem.at[col_slot],
        device_id=col_dest, device_id_type=MESH,
    )
    row_copy.start()
    col_copy.start()
    row_copy.wait_send()
    col_copy.wait_send()

    @pl.when(at_row_edge)
    def _():
        for slot in range(2 * row_types):
            pltpu.make_async_remote_copy(
                row_send, row_out.at[slot], send_sem.at[0], row_sem.at[slot],
                device_id=row_sender(slot), device_id_type=MESH,
            ).wait_recv()

    @pl.when(at_col_edge)
    def _():
        for slot in range(2 * col_types):
            pltpu.make_async_remote_copy(
                col_send, col_out.at[slot], send_sem.at[1], col_sem.at[slot],
                device_id=col_sender(slot), device_id_type=MESH,
            ).wait_recv()

    col_share = col_out.shape[2]

    def put_columns(first, second):
        for slot in range(2 * col_types):
            column = first if slot < col_types else second
            base = (slot % col_types) * col_share
            for field in range(4):
                for offset in range(col_share):
                    final_ref[field, base + offset, pl.ds(column, 1), :] = (
                        col_out[slot, field, pl.ds(offset, 1), :]
                    )

    def put_rows(first, second):
        for slot in range(2 * row_types):
            line = first if slot < row_types else second
            base = (slot % row_types) * row_share
            for field in range(4):
                final_ref[field, line, pl.ds(base, row_share), :] = row_out[slot, field]

    @pl.when(lon == 0)
    def _():
        put_columns(0, 1)

    @pl.when(lon == lon_count - 1)
    def _():
        put_columns(breadth - 1, breadth - 2)

    @pl.when(colat == 0)
    def _():
        put_rows(0, 1)

    @pl.when(colat == colat_count - 1)
    def _():
        put_rows(height - 1, height - 2)


def stepped(fields_pad, coefs_pad, row_pad, col_pad, lead, rows, cols, frac, trig, row_share):
    height = coefs_pad.shape[1] - 2
    breadth = fields_pad.shape[2] - 2 * col_pad
    span = breadth + 2 * lead
    radial_len = fields_pad.shape[3]
    slots = rows.shape[0]
    row_types = lax.axis_size("colat") // 4
    col_types = lax.axis_size("lon") // 4
    dtype = fields_pad.dtype
    vmem = pl.BlockSpec(memory_space=pltpu.VMEM)
    smem = pl.BlockSpec(memory_space=pltpu.SMEM)
    return pl.pallas_call(
        functools.partial(step_kernel, row_pad, col_pad),
        out_shape=(
            jax.ShapeDtypeStruct((4, height + 2, span, radial_len), dtype),
            jax.ShapeDtypeStruct((4, height, breadth, radial_len), dtype),
            jax.ShapeDtypeStruct((2 * row_types, 4, row_share, radial_len), dtype),
            jax.ShapeDtypeStruct((2 * col_types, 4, slots - row_share, radial_len), dtype),
        ),
        in_specs=[vmem, vmem, smem, smem, smem, smem],
        out_specs=(vmem, vmem, vmem, vmem),
        scratch_shapes=[
            pltpu.VMEM((4, row_share, radial_len), dtype),
            pltpu.VMEM((4, slots - row_share, radial_len), dtype),
            pltpu.SemaphoreType.DMA((2,)),
            pltpu.SemaphoreType.DMA((2 * row_types,)),
            pltpu.SemaphoreType.DMA((2 * col_types,)),
        ],
        compiler_params=pltpu.CompilerParams(collective_id=0, has_side_effects=True),
    )(fields_pad, coefs_pad, rows, cols, frac, trig)


def advance(padded, thermal, viscous):
    height = padded.shape[1] - 4
    breadth = padded.shape[2] - 4
    center = padded[:, 2 : 2 + height, 2 : 2 + breadth]
    radial_len = center.shape[3]
    radial_pad = jnp.pad(center, ((0, 0), (0, 0), (0, 0), (2, 2)))
    along_lat = [padded[:, offset : offset + height, 2 : 2 + breadth] for offset in range(5)]
    along_lon = [padded[:, 2 : 2 + height, offset : offset + breadth] for offset in range(5)]
    along_rad = [radial_pad[..., offset : offset + radial_len] for offset in range(5)]
    laplace = curvature(along_rad) + curvature(along_lat) + curvature(along_lon)
    transport = (
        center[1:2] * gradient(along_rad)
        + center[2:3] * gradient(along_lat)
        + center[3:4] * gradient(along_lon)
    )
    diffusion = jnp.stack([thermal, viscous, viscous, viscous])
    change = diffusion * laplace - transport
    change = change.at[1].add(BUOYANCY * center[0])
    return center + TIME_STEP * change


def local(fields_now, diffusivity, viscosity, donor_row, donor_column, donor_offset, rim_angle):
    fields = fields_now[:, 0]
    thermal = diffusivity[0]
    viscous = viscosity[0]
    height = fields.shape[1]
    breadth = fields.shape[2]
    radial_len = fields.shape[3]
    colat_pos = lax.axis_index("colat")
    lon_pos = lax.axis_index("lon")
    colat_count = lax.axis_size("colat")
    lon_count = lax.axis_size("lon")
    row_share = 4 * breadth // colat_count
    fields_pad, coefs_pad = halo_exchange(fields, thermal, viscous, 3)
    lead = 4
    angles = rim_angle.reshape(-1)
    trig = jnp.stack([jnp.cos(angles), jnp.sin(angles)])
    frac = donor_offset.reshape(2, -1)
    extended, fresh, row_buf, col_buf = stepped(
        fields_pad, coefs_pad, 3, 8, lead, donor_row.reshape(-1), donor_column.reshape(-1),
        frac, trig, row_share,
    )
    return fresh[:, None]


def solution(mesh):
    placed = (
        P(None, "panel", "colat", "lon", None),
        P("panel", "colat", "lon", None),
        P("panel", "colat", "lon", None),
        P("panel", "colat", "lon", None),
        P("panel", "colat", "lon", None),
        P("panel", "colat", "lon", None, None),
        P("panel", "colat", "lon", None),
    )
    return jax.shard_map(
        local,
        mesh=mesh,
        in_specs=placed,
        out_specs=P(None, "panel", "colat", "lon", None),
        check_vma=False,
    )
```

```python
import functools

import jax
import jax.numpy as jnp
from jax import lax
from jax.sharding import PartitionSpec as P
from jax.experimental import pallas as pl
from jax.experimental.pallas import tpu as pltpu

MESH = pl.DeviceIdType.MESH

TIME_STEP = 0.05
BUOYANCY = 1.0


def with_halo(x, sides, width):
    for axis, dim in sides:
        count, length = (lax.axis_size(axis), x.shape[dim])
        up = [(i, (i + 1) % count) for i in range(count - 1)]
        down = [(j, i) for i, j in up]
        last = lax.slice_in_dim(x, length - width, length, axis=dim)
        leading = lax.slice_in_dim(x, 0, width, axis=dim)
        before = lax.ppermute(last, axis, up)
        after = lax.ppermute(leading, axis, down)
        x = jnp.concatenate([before, x, after], axis=dim)
    return x


def swapped(block, axis, stride):
    count = lax.axis_size(axis)
    route = []
    for low in range(count):
        high = low | 1 << stride
        if high != low and high < count:
            route += [(low, high), (high, low)]
    return lax.ppermute(block, axis, route)


DIRECTIONS = ((-1, -1), (-1, 0), (-1, 1), (0, -1), (0, 1), (1, -1), (1, 0), (1, 1))


def window(step, width, length, offset):
    if step < 0:
        return offset, width
    if step > 0:
        return offset + length - width, width
    return offset, length


def landing(step, width, length, offset):
    if step < 0:
        return offset - width, width
    if step > 0:
        return offset + length, width
    return offset, length


def halo_kernel(width, margins, fields_in, thermal_in, viscous_in, fields_out, coefs_out, send_sem, recv_sem):
    count = len(DIRECTIONS)
    panel = lax.axis_index("panel")
    colat = lax.axis_index("colat")
    lon = lax.axis_index("lon")
    colat_count = lax.axis_size("colat")
    lon_count = lax.axis_size("lon")
    height, breadth = fields_in.shape[1], fields_in.shape[2]

    for out, (row_pad, col_pad) in ((fields_out, margins[0]), (coefs_out, margins[1])):
        lead = out.shape[:1]
        total_rows, total_cols = out.shape[1], out.shape[2]
        out[:, pl.ds(0, row_pad)] = jnp.zeros(lead + (row_pad, total_cols, out.shape[3]), out.dtype)
        out[:, pl.ds(row_pad + height, row_pad)] = jnp.zeros(
            lead + (row_pad, total_cols, out.shape[3]), out.dtype
        )
        side = jnp.zeros(lead + (height, col_pad, out.shape[3]), out.dtype)
        out[:, pl.ds(row_pad, height), pl.ds(0, col_pad)] = side
        out[:, pl.ds(row_pad, height), pl.ds(col_pad + breadth, total_cols - col_pad - breadth)] = side
    fields_out[:, pl.ds(margins[0][0], height), pl.ds(margins[0][1], breadth)] = fields_in[...]
    coefs_out[0, pl.ds(margins[1][0], height), pl.ds(margins[1][1], breadth)] = thermal_in[...]
    coefs_out[1, pl.ds(margins[1][0], height), pl.ds(margins[1][1], breadth)] = viscous_in[...]

    def present(step):
        row = colat + step[0]
        col = lon + step[1]
        inside = jnp.logical_and(row >= 0, row < colat_count)
        return jnp.logical_and(inside, jnp.logical_and(col >= 0, col < lon_count))

    def source(part, step):
        depth = width if part == 0 else 1
        rows = window(step[0], depth, height, 0)
        cols = window(step[1], depth, breadth, 0)
        ref = (fields_in, thermal_in, viscous_in)[part]
        if part == 0:
            return ref.at[:, pl.ds(rows[0], rows[1]), pl.ds(cols[0], cols[1]), :]
        return ref.at[pl.ds(rows[0], rows[1]), pl.ds(cols[0], cols[1]), :]

    def target(part, step):
        depth = width if part == 0 else 1
        row_pad, col_pad = margins[0] if part == 0 else margins[1]
        rows = landing(step[0], depth, height, row_pad)
        cols = landing(step[1], depth, breadth, col_pad)
        if part == 0:
            return fields_out.at[:, pl.ds(rows[0], rows[1]), pl.ds(cols[0], cols[1]), :]
        return coefs_out.at[part - 1, pl.ds(rows[0], rows[1]), pl.ds(cols[0], cols[1]), :]

    def outgoing(index, part):
        step = DIRECTIONS[index]
        back = tuple(-s for s in step)
        return pltpu.make_async_remote_copy(
            source(part, step), target(part, back),
            send_sem.at[index, part], recv_sem.at[count - 1 - index, part],
            device_id=(panel, colat + step[0], lon + step[1]), device_id_type=MESH,
        )

    def incoming(index, part):
        step = DIRECTIONS[index]
        spot = target(part, step)
        return pltpu.make_async_remote_copy(
            spot, spot, send_sem.at[index, part], recv_sem.at[index, part],
            device_id=(panel, colat + step[0], lon + step[1]), device_id_type=MESH,
        )

    barrier = pltpu.get_barrier_semaphore()
    expected = jnp.int32(0)
    for index, step in enumerate(DIRECTIONS):
        exists = present(step)
        expected = expected + exists.astype(jnp.int32)

        @pl.when(exists)
        def _():
            pl.semaphore_signal(
                barrier, 1, device_id=(panel, colat + step[0], lon + step[1]),
                device_id_type=MESH,
            )

    pl.semaphore_wait(barrier, expected)
    for index, step in enumerate(DIRECTIONS):

        @pl.when(present(step))
        def _():
            for part in range(3):
                outgoing(index, part).start()

    for index, step in enumerate(DIRECTIONS):

        @pl.when(present(step))
        def _():
            for part in range(3):
                outgoing(index, part).wait_send()
            for part in range(3):
                incoming(index, part).wait_recv()


def halo_exchange(fields, thermal, viscous, width):
    lane_pad = 8
    height, breadth, radial_len = fields.shape[1], fields.shape[2], fields.shape[3]
    margins = ((width, lane_pad), (1, lane_pad))
    vmem = pl.BlockSpec(memory_space=pltpu.VMEM)
    count = len(DIRECTIONS)
    return pl.pallas_call(
        functools.partial(halo_kernel, width, margins),
        out_shape=(
            jax.ShapeDtypeStruct(
                (4, height + 2 * width, breadth + 2 * lane_pad, radial_len), fields.dtype
            ),
            jax.ShapeDtypeStruct((2, height + 2, breadth + 2 * lane_pad, radial_len), fields.dtype),
        ),
        in_specs=[vmem, vmem, vmem],
        out_specs=(vmem, vmem),
        scratch_shapes=[
            pltpu.SemaphoreType.DMA((count, 3)),
            pltpu.SemaphoreType.DMA((count, 3)),
        ],
        compiler_params=pltpu.CompilerParams(collective_id=1, has_side_effects=True),
    )(fields, thermal, viscous)


def gradient(stencil):
    return (8.0 * (stencil[3] - stencil[1]) - (stencil[4] - stencil[0])) / 12.0


def curvature(stencil):
    return (16.0 * (stencil[3] + stencil[1]) - (stencil[4] + stencil[0]) - 30.0 * stencil[2]) / 12.0


def slope(stencil):
    return 8.0 * (stencil[3] - stencil[1]) - (stencil[4] - stencil[0])


def spread(stencil):
    return 16.0 * (stencil[3] + stencil[1]) - (stencil[4] + stencil[0]) - 30.0 * stencil[2]


def shifted(block, step):
    size = block.shape[-1]
    lane = lax.broadcasted_iota(jnp.int32, block.shape, block.ndim - 1)
    moved = pltpu.roll(block, (size - step) % size, block.ndim - 1)
    keep = jnp.logical_and(lane + step >= 0, lane + step < size)
    return jnp.where(keep, moved, 0.0)


def step_kernel(
    row_pad, col_pad, fields_ref, coefs_ref, rows_ref, cols_ref, frac_ref, trig_ref,
    out_ref, final_ref, row_out, col_out, row_send, col_send, send_sem, row_sem, col_sem,
):
    panel = lax.axis_index("panel")
    colat = lax.axis_index("colat")
    lon = lax.axis_index("lon")
    colat_count = lax.axis_size("colat")
    lon_count = lax.axis_size("lon")
    row_types = row_out.shape[0] // 2
    col_types = col_out.shape[0] // 2
    row_share = row_send.shape[1]
    other = 1 - panel

    def route(share, per_type, count):
        kind = share // per_type
        edge = (kind % 2) * (count - 1)
        slot = (kind // 2) * per_type + share % per_type
        return edge, slot

    row_edge, row_slot = route(colat, row_types, colat_count)
    col_edge, col_slot = route(lon, col_types, lon_count)
    row_dest = (other, row_edge, lon)
    col_dest = (other, colat, col_edge)
    at_row_edge = jnp.logical_or(colat == 0, colat == colat_count - 1)
    at_col_edge = jnp.logical_or(lon == 0, lon == lon_count - 1)
    parity_row = (colat // (colat_count - 1)).astype(jnp.int32)
    parity_col = (lon // (lon_count - 1)).astype(jnp.int32)

    def row_sender(slot):
        kind = 2 * (slot // row_types) + parity_row
        return (other, kind * row_types + slot % row_types, lon)

    def col_sender(slot):
        kind = 2 * (slot // col_types) + parity_col
        return (other, colat, kind * col_types + slot % col_types)

    barrier = pltpu.get_barrier_semaphore()
    pl.semaphore_signal(barrier, 1, device_id=row_dest, device_id_type=MESH)
    pl.semaphore_signal(barrier, 1, device_id=col_dest, device_id_type=MESH)

    @pl.when(at_row_edge)
    def _():
        for slot in range(2 * row_types):
            pl.semaphore_signal(barrier, 1, device_id=row_sender(slot), device_id_type=MESH)

    @pl.when(at_col_edge)
    def _():
        for slot in range(2 * col_types):
            pl.semaphore_signal(barrier, 1, device_id=col_sender(slot), device_id_type=MESH)

    ext_rows, span, radial_len = out_ref.shape[1], out_ref.shape[2], out_ref.shape[3]
    height = ext_rows - 2
    breadth = fields_ref.shape[2] - 2 * col_pad
    lead = (span - breadth) // 2
    col_ids = lax.broadcasted_iota(jnp.int32, (span, radial_len), 0) - lead + lon * breadth
    col_ok = jnp.logical_and(col_ids >= 0, col_ids < lon_count * breadth)

    def body(row, carry):
        global_row = row - 1 + colat * height
        ok = jnp.logical_and(col_ok, jnp.logical_and(global_row >= 0, global_row < colat_count * height))

        def load(field, down, across):
            return fields_ref[field, row + row_pad - 1 + down, pl.ds(col_pad - lead + across, span), :]

        center = [load(field, 0, 0) for field in range(4)]
        thermal = coefs_ref[0, row, pl.ds(col_pad - lead, span), :]
        viscous = coefs_ref[1, row, pl.ds(col_pad - lead, span), :]
        for field in range(4):
            along_lat = [load(field, offset - 2, 0) for offset in range(5)]
            along_lon = [load(field, 0, offset - 2) for offset in range(5)]
            along_rad = [shifted(center[field], offset - 2) for offset in range(5)]
            laplace = spread(along_rad) + spread(along_lat) + spread(along_lon)
            transport = (
                center[1] * slope(along_rad)
                + center[2] * slope(along_lat)
                + center[3] * slope(along_lon)
            )
            change = (thermal if field == 0 else viscous) * laplace - transport
            stepped_value = center[field] + (TIME_STEP / 12.0) * change
            if field == 1:
                stepped_value = stepped_value + (TIME_STEP * BUOYANCY) * center[0]
            out_ref[field, row] = jnp.where(ok, stepped_value, 0.0)
        return carry

    lax.fori_loop(0, ext_rows, body, 0)

    slots = rows_ref.shape[0]
    column = lax.broadcasted_iota(jnp.int32, (span, radial_len), 0)
    for slot in range(slots):
        first = rows_ref[slot]
        across = cols_ref[slot] + (lead - 1)
        frac_row = frac_ref[0, slot]
        frac_lon = frac_ref[1, slot]
        weight = jnp.where(
            column == across, 1.0 - frac_lon, jnp.where(column == across + 1, frac_lon, 0.0)
        )
        mixed = []
        for field in range(4):
            upper = jnp.sum(weight * out_ref[field, first], axis=0, keepdims=True)
            lower = jnp.sum(weight * out_ref[field, first + 1], axis=0, keepdims=True)
            mixed.append((1.0 - frac_row) * upper + frac_row * lower)
        cosine = trig_ref[0, slot]
        sine_part = trig_ref[1, slot]
        turned = [
            mixed[0],
            mixed[1],
            cosine * mixed[2] - sine_part * mixed[3],
            sine_part * mixed[2] + cosine * mixed[3],
        ]
        for field in range(4):
            if slot < row_share:
                row_send[field, pl.ds(slot, 1), :] = turned[field]
            else:
                col_send[field, pl.ds(slot - row_share, 1), :] = turned[field]

    expected = (
        2
        + at_row_edge.astype(jnp.int32) * (2 * row_types)
        + at_col_edge.astype(jnp.int32) * (2 * col_types)
    )
    pl.semaphore_wait(barrier, expected)

    row_copy = pltpu.make_async_remote_copy(
        row_send, row_out.at[row_slot], send_sem.at[0], row_sem.at[row_slot],
        device_id=row_dest, device_id_type=MESH,
    )
    col_copy = pltpu.make_async_remote_copy(
        col_send, col_out.at[col_slot], send_sem.at[1], col_sem.at[col_slot],
        device_id=col_dest, device_id_type=MESH,
    )
    row_copy.start()
    col_copy.start()
    for field in range(4):
        final_ref[field] = out_ref[field, pl.ds(1, height), pl.ds(lead, breadth), :]
    row_copy.wait_send()
    col_copy.wait_send()

    @pl.when(at_row_edge)
    def _():
        for slot in range(2 * row_types):
            pltpu.make_async_remote_copy(
                row_send, row_out.at[slot], send_sem.at[0], row_sem.at[slot],
                device_id=row_sender(slot), device_id_type=MESH,
            ).wait_recv()

    @pl.when(at_col_edge)
    def _():
        for slot in range(2 * col_types):
            pltpu.make_async_remote_copy(
                col_send, col_out.at[slot], send_sem.at[1], col_sem.at[slot],
                device_id=col_sender(slot), device_id_type=MESH,
            ).wait_recv()

    col_share = col_out.shape[2]

    def put_columns(first, second):
        for slot in range(2 * col_types):
            column = first if slot < col_types else second
            base = (slot % col_types) * col_share
            for field in range(4):
                for offset in range(col_share):
                    final_ref[field, base + offset, pl.ds(column, 1), :] = (
                        col_out[slot, field, pl.ds(offset, 1), :]
                    )

    def put_rows(first, second):
        for slot in range(2 * row_types):
            line = first if slot < row_types else second
            base = (slot % row_types) * row_share
            for field in range(4):
                final_ref[field, line, pl.ds(base, row_share), :] = row_out[slot, field]

    @pl.when(lon == 0)
    def _():
        put_columns(0, 1)

    @pl.when(lon == lon_count - 1)
    def _():
        put_columns(breadth - 1, breadth - 2)

    @pl.when(colat == 0)
    def _():
        put_rows(0, 1)

    @pl.when(colat == colat_count - 1)
    def _():
        put_rows(height - 1, height - 2)


def stepped(fields_pad, coefs_pad, row_pad, col_pad, lead, rows, cols, frac, trig, row_share):
    height = coefs_pad.shape[1] - 2
    breadth = fields_pad.shape[2] - 2 * col_pad
    span = breadth + 2 * lead
    radial_len = fields_pad.shape[3]
    slots = rows.shape[0]
    row_types = lax.axis_size("colat") // 4
    col_types = lax.axis_size("lon") // 4
    dtype = fields_pad.dtype
    vmem = pl.BlockSpec(memory_space=pltpu.VMEM)
    smem = pl.BlockSpec(memory_space=pltpu.SMEM)
    return pl.pallas_call(
        functools.partial(step_kernel, row_pad, col_pad),
        out_shape=(
            jax.ShapeDtypeStruct((4, height + 2, span, radial_len), dtype),
            jax.ShapeDtypeStruct((4, height, breadth, radial_len), dtype),
            jax.ShapeDtypeStruct((2 * row_types, 4, row_share, radial_len), dtype),
            jax.ShapeDtypeStruct((2 * col_types, 4, slots - row_share, radial_len), dtype),
        ),
        in_specs=[vmem, vmem, smem, smem, smem, smem],
        out_specs=(vmem, vmem, vmem, vmem),
        scratch_shapes=[
            pltpu.VMEM((4, row_share, radial_len), dtype),
            pltpu.VMEM((4, slots - row_share, radial_len), dtype),
            pltpu.SemaphoreType.DMA((2,)),
            pltpu.SemaphoreType.DMA((2 * row_types,)),
            pltpu.SemaphoreType.DMA((2 * col_types,)),
        ],
        compiler_params=pltpu.CompilerParams(collective_id=0, has_side_effects=True),
    )(fields_pad, coefs_pad, rows, cols, frac, trig)


def advance(padded, thermal, viscous):
    height = padded.shape[1] - 4
    breadth = padded.shape[2] - 4
    center = padded[:, 2 : 2 + height, 2 : 2 + breadth]
    radial_len = center.shape[3]
    radial_pad = jnp.pad(center, ((0, 0), (0, 0), (0, 0), (2, 2)))
    along_lat = [padded[:, offset : offset + height, 2 : 2 + breadth] for offset in range(5)]
    along_lon = [padded[:, 2 : 2 + height, offset : offset + breadth] for offset in range(5)]
    along_rad = [radial_pad[..., offset : offset + radial_len] for offset in range(5)]
    laplace = curvature(along_rad) + curvature(along_lat) + curvature(along_lon)
    transport = (
        center[1:2] * gradient(along_rad)
        + center[2:3] * gradient(along_lat)
        + center[3:4] * gradient(along_lon)
    )
    diffusion = jnp.stack([thermal, viscous, viscous, viscous])
    change = diffusion * laplace - transport
    change = change.at[1].add(BUOYANCY * center[0])
    return center + TIME_STEP * change


def local(fields_now, diffusivity, viscosity, donor_row, donor_column, donor_offset, rim_angle):
    fields = fields_now[:, 0]
    thermal = diffusivity[0]
    viscous = viscosity[0]
    height = fields.shape[1]
    breadth = fields.shape[2]
    radial_len = fields.shape[3]
    colat_pos = lax.axis_index("colat")
    lon_pos = lax.axis_index("lon")
    colat_count = lax.axis_size("colat")
    lon_count = lax.axis_size("lon")
    row_share = 4 * breadth // colat_count
    fields_pad, coefs_pad = halo_exchange(fields, thermal, viscous, 3)
    lead = 4
    angles = rim_angle.reshape(-1)
    trig = jnp.stack([jnp.cos(angles), jnp.sin(angles)])
    frac = donor_offset.reshape(2, -1)
    extended, fresh, row_buf, col_buf = stepped(
        fields_pad, coefs_pad, 3, 8, lead, donor_row.reshape(-1), donor_column.reshape(-1),
        frac, trig, row_share,
    )
    return fresh[:, None]


def solution(mesh):
    placed = (
        P(None, "panel", "colat", "lon", None),
        P("panel", "colat", "lon", None),
        P("panel", "colat", "lon", None),
        P("panel", "colat", "lon", None),
        P("panel", "colat", "lon", None),
        P("panel", "colat", "lon", None, None),
        P("panel", "colat", "lon", None),
    )
    return jax.shard_map(
        local,
        mesh=mesh,
        in_specs=placed,
        out_specs=P(None, "panel", "colat", "lon", None),
        check_vma=False,
    )
```
